128 devices in a mesh: sec: 4 (over x), dev: 32 (over y, z, core).
Axes of the slice: x: 4, y: 4, z: 4, core: 2. Of those that a mesh axis runs over, the one named last changes fastest.
Arguments:
- velocity: float32 [3, 64, 64, 4096], P(None, 'sec', None, 'dev'), may hold values from -6 to 6
- source: float32 [3, 64, 64, 4096], P(None, 'sec', None, 'dev'), may hold values from -6 to 6
- viscosity: float32 [64, 64, 4096], P('sec', None, 'dev'), may hold values from 0.25 to 4
- owners: int32 [32, 64, 1], P('dev', 'sec'), may hold values from 0 to 31; in each aligned block of 16 rows (0 to 15, 16 to 31, ..., all dimensions but the last counted through in order) at most 2 rows name the same one
- targets: int32 [32, 64], P('dev', 'sec'), may hold values from 0 to 15
- shell_load: float32 [6, 262144], P(None, ('sec', 'dev')), may hold values from -6 to 6
- shell_state: float32 [6, 262144], P(None, ('sec', 'dev')), may hold values from -3 to 3
- shell_inverse: float32 [6, 6, 262144], P(None, None, ('sec', 'dev')), may hold values from -0.06 to 0.5
Outputs:
- velocity_out: float32 [3, 64, 64, 4096], P(None, 'sec', None, 'dev')
- shell_out: float32 [6, 262144], P(None, ('sec', 'dev'))
The draws below stay inside these ranges and needn't reach their ends.
Inputs may be any that keep to these rules, and one draw needn't show every extreme that they name: `owners`: among the face blocks of one device (the aligned blocks of 16 rows), no owner is named more than 2 times, a bound that some block reaches.
All inputs are finite; a program needn't handle non-finite values.
Results may differ from the reference program's by a relative error of at most 0.00013.
Values sent between devices are 32-bit elements; how exact they have to be, the bound alone decides.
A program may use at most 128 MiB of HBM per device.

```python
import math
import jax
import jax.numpy as jnp
import numpy as np
from jax import lax

CX = 16
NB = 16
SWEEPS = 8
SHELL_SWEEPS = 8
SUBITERS = 2
NX = 64
NY = 64
NZ = 4096
CAP = 2
NODES = 262144
N_SEC = 4
N_DEV = 32


def draw_shell_inverse(key, part):
    diag_key = jax.random.fold_in(key, 11)
    off_key = jax.random.fold_in(key, 12)
    diag = jax.random.uniform(diag_key, (6, NODES), jnp.float32, 0.3, 0.5)
    off = jax.random.uniform(off_key, (6, 6, NODES), jnp.float32, -0.05, 0.05)
    eye = jnp.eye(6, dtype=jnp.float32)[:, :, None]
    return eye * diag[:, None, :] + (1.0 - eye) * off


def with_ends(result, own_key, least, top_value):
    longest = result.shape.index(max(result.shape))
    spots = []
    for shift in (0, 1):
        where = [jax.random.randint(jax.random.fold_in(own_key, axis), (), 0, length) for axis, length in enumerate(result.shape)]
        where[longest] = (where[longest] + shift) % result.shape[longest]
        spots.append(tuple(where))
    return result.at[spots[0]].set(least).at[spots[1]].set(top_value)


def block_levels(own_key, shape, pieces, smallest, top_value):
    level, own = 1.0, jax.random.fold_in(own_key, 6)
    for dim, parts in pieces:
        heights = jnp.exp(jax.random.uniform(jax.random.fold_in(own, dim), (parts,), jnp.float32, smallest / len(pieces), top_value / len(pieces)))
        level = level * jnp.repeat(heights, shape[dim] // parts).reshape([-1 if axis == dim else 1 for axis in range(len(shape))])
    return level


def shared_out(rng, own, number, rows, count, top, limit, lean):
    ranking = jax.random.permutation(rng, count)
    heavy_load, ordinary = load_shares(count, rows * top, limit, lean, True), load_shares(count, rows * top, limit, lean, False)
    places = jnp.arange(count)

    def named(sizes, rotation):
        used = int((sizes > 0).sum())
        fixed = max(1, used // 4)
        moved = fixed + (places - fixed + rotation * (used - fixed)) % max(1, count - fixed)
        return jnp.zeros((count,), jnp.int32).at[ranking[jnp.where(places < fixed, places, moved)]].set(jnp.asarray(sizes, jnp.int32))

    sizes = jnp.where(number % 4 == 0, named(heavy_load, number // 4), named(ordinary, number - number // 4 - 1))
    mixed = jax.random.permutation(jax.random.fold_in(own, 3), count)
    donor, receiver = mixed[0:count // 2 * 2:2], mixed[1:count // 2 * 2:2]
    margin = jnp.minimum(sizes[donor] - 1, limit - sizes[receiver]) // 2
    margin = jnp.where((donor == ranking[0]) | (receiver == ranking[0]) | (sizes[receiver] == 0), 0, jnp.maximum(margin, 0))
    moved = jax.random.randint(jax.random.fold_in(own, 4), (count // 2,), 0, 1 << 20) % (margin + 1)
    sizes = sizes.at[donor].add(-moved).at[receiver].add(moved)
    members = jnp.searchsorted(jnp.cumsum(sizes), jnp.arange(rows * top), side="right").astype(jnp.int32)
    listing = members.reshape(top, rows).T
    listing = listing[jax.random.permutation(jax.random.fold_in(own, 1), rows)]
    rotation = jax.random.randint(jax.random.fold_in(own, 2), (rows, 1), 0, top)
    return jnp.take_along_axis(listing, (jnp.arange(top)[None, :] + rotation) % top, axis=1)


def load_shares(number_of, total, bound, skew, full):
    portions = [(1 << 20) // math.isqrt(grade ** skew) + 1 for grade in range(1, number_of + 1)]
    largest = bound if full else min(bound, max(-(-total // number_of), total * portions[0] // sum(portions)))
    least = 1 if total - largest >= number_of - 1 else 0
    counts, rest = [largest] + [least] * (number_of - 1), total - largest - least * (number_of - 1)
    while rest > 0:
        free = [i for i in range(1, number_of) if counts[i] < largest] or [i for i in range(1, number_of) if counts[i] < bound]
        pool, left = sum([portions[i] for i in free]), rest
        for i in free:
            extra = min(bound - counts[i], max(1, left * portions[i] // pool), rest)
            counts[i] = counts[i] + extra
            rest = rest - extra
    return np.array(counts)


def bell_draw(stream_key, extent, width, most, shards=(), kind=jnp.bfloat16):
    values = jax.random.normal(stream_key, extent, jnp.float32) * width
    if len(shards) > 0:
        values = block_levels(stream_key, extent, shards, -0.22, 0.18) * values
    return jnp.clip(values, min=-most, max=most).astype(kind)


def setup_inputs(seed: int = 0) -> dict:
    keys = jax.random.split(jax.random.key(seed), 9)
    velocity = bell_draw(keys[0], (3, NX, NY, NZ), 1.0, 6.0, ((1, 4), (3, 32)), jnp.float32)
    source = bell_draw(keys[1], (3, NX, NY, NZ), 1.0, 6.0, ((1, 4), (3, 32)), jnp.float32)
    viscosity = jnp.clip(jnp.exp(math.log(4.0) - 2.7725887 * jax.random.uniform(keys[2], (NX, NY, NZ), jnp.float32) ** block_levels(keys[2], (NX, NY, NZ), ((0, 4), (2, 32)), -0.2, 0.2)), 0.25, 4.0)
    owners_keys = jax.random.split(jax.random.fold_in(keys[3], 1), N_DEV * NX // CX)
    owners_turns = jax.random.permutation(jax.random.fold_in(keys[3], 3), N_DEV * NX // CX)
    owners = jax.vmap(lambda own, number: shared_out(jax.random.fold_in(keys[3], 2), own, number, CX, N_DEV, 1, CAP, 2))(owners_keys, owners_turns).reshape((N_DEV, NX, 1))
    targets = with_ends(jax.random.randint(keys[4], (N_DEV, NX), 0, NB), jax.random.fold_in(keys[4], 1), 0, NB - 1).astype(jnp.int32)
    shell_load = bell_draw(keys[5], (6, NODES), 1.0, 6.0, ((1, 128),), jnp.float32)
    shell_state = bell_draw(keys[6], (6, NODES), 0.5, 3.0, ((1, 128),), jnp.float32)
    shell_inverse = draw_shell_inverse(jax.random.fold_in(keys[8], 71), 0)
    return dict(velocity=velocity, source=source, viscosity=viscosity, owners=owners, targets=targets, shell_load=shell_load, shell_state=shell_state, shell_inverse=shell_inverse)


def face_terms(nu):
    padded = jnp.pad(nu, ((1, 1), (0, 0), (1, 1)))
    edge = jnp.pad(nu, ((0, 0), (1, 1), (0, 0)), mode="edge")
    fxm = 0.5 * (nu + padded[:-2, :, 1:-1])
    fxp = 0.5 * (nu + padded[2:, :, 1:-1])
    fzm = 0.5 * (nu + padded[1:-1, :, :-2])
    fzp = 0.5 * (nu + padded[1:-1, :, 2:])
    fym = 0.5 * (nu + edge[:, :-2, :])
    fyp = 0.5 * (nu + edge[:, 2:, :])
    denom = 1.0 + fxm + fxp + fzm + fzp + fym + fyp
    return fxm, fxp, fzm, fzp, fym, fyp, denom


def relax(u, terms, rhs, wall):
    fxm, fxp, fzm, fzp, fym, fyp, denom = terms
    upad = jnp.pad(u, ((0, 0), (1, 1), (0, 0), (1, 1)))
    zero_layer = jnp.zeros((3, u.shape[1], 1, u.shape[3]), jnp.float32)
    uy = jnp.concatenate([wall[:, :, None, :], u, zero_layer], axis=2)
    num = rhs + fxm * upad[:, :-2, :, 1:-1] + fxp * upad[:, 2:, :, 1:-1]
    num = num + fzm * upad[:, 1:-1, :, :-2] + fzp * upad[:, 1:-1, :, 2:]
    num = num + fym * uy[:, :, :-2, :] + fyp * uy[:, :, 2:, :]
    return num / denom


def reference(velocity, source, viscosity, owners, targets, shell_load, shell_state, shell_inverse):
    nblocks = NODES // 128
    owner_map = owners[:, :, 0].T
    target_map = targets.T
    section = (jnp.arange(NX, dtype=jnp.int32) // CX)[:, None]
    index = (section * (N_DEV * NB) + owner_map * NB + target_map).reshape(NX * N_DEV)
    terms = face_terms(viscosity)
    u = velocity
    shell = shell_state
    length = N_DEV * NB * 128
    for outer in range(SUBITERS):
        blocks = shell[:3].reshape(3, nblocks, 128)
        wall = blocks[:, index, :].reshape(3, NX, N_DEV * 128)

        def sweep(step, state):
            return relax(state, terms, source, wall)

        u = lax.fori_loop(0, SWEEPS, sweep, u)
        traction = 2.0 * viscosity[None, :, 0, :] * (u[:, :, 0, :] - wall)
        tblocks = traction.reshape(3, NX * N_DEV, 128).transpose(1, 0, 2)
        summed = jax.ops.segment_sum(tblocks, index, num_segments=nblocks)
        added = summed.transpose(1, 0, 2).reshape(3, NODES)
        force = jnp.concatenate([shell_load[:3] + added, shell_load[3:]], axis=0)

        def shell_sweep(step, state):
            chains = jnp.pad(state.reshape(6, N_SEC, length), ((0, 0), (0, 0), (1, 1)))
            beside = (chains[:, :, :-2] + chains[:, :, 2:]).reshape(6, NODES)
            drive = force + 0.4 * beside
            return jnp.sum(shell_inverse * drive[None, :, :], axis=1)

        shell = lax.fori_loop(0, SHELL_SWEEPS, shell_sweep, shell)
    return u, shell
```

```python
import jax
import jax.numpy as jnp
from jax import lax
from jax.experimental import pallas as pl
from jax.experimental.pallas import tpu as pltpu
from jax.sharding import PartitionSpec as P

SWEEPS = 8
SHELL_SWEEPS = 8
SUBITERS = 2
CX = 16
NY = 64
LANES = 128
NB = 16
ROWS = 3 * CX
MESH = pl.DeviceIdType.MESH
F32 = jnp.float32
HIGHEST = lax.Precision.HIGHEST


def kernel(
    nsec, ndev,
    vel_ref, src_ref, nu_ref, key_ref, tgt_ref, load_ref, state_ref, inv_ref,
    uout_ref, sout_ref,
    U, NU, CF, RHS, ZS, ZR, MV, NZS, NZR,
    S, ST, G, GT, AS, AR, WROW, WALL,
    SH, FORCE, INV, IS, IR, HS, HR,
    xs_sem, xr_sem, zs_sem, zr_sem, nxs_sem, nxr_sem, nzs_sem, nzr_sem,
    as_sem, ar_sem, is_sem, ir_sem, hs_sem, hr_sem,
):
    sec = lax.axis_index("sec")
    dev = lax.axis_index("dev")
    has = {("x", 0): sec > 0, ("x", 1): sec < nsec - 1, ("z", 0): dev > 0, ("z", 1): dev < ndev - 1}
    lane = lax.broadcasted_iota(jnp.int32, (8, LANES), 1)
    sub = lax.broadcasted_iota(jnp.int32, (8, LANES), 0)

    def target(axis, side):
        step = 1 if side else -1
        return {"sec": sec + step} if axis == "x" else {"dev": dev + step}

    def u_copy(slot, c, side):
        own, there = (CX, 0) if side else (1, CX + 1)
        return pltpu.make_async_remote_copy(
            src_ref=U.at[slot, c, own], dst_ref=U.at[slot, c, there],
            send_sem=xs_sem.at[slot, c, side], recv_sem=xr_sem.at[slot, c, 1 - side],
            device_id=target("x", side), device_id_type=MESH)

    def z_copy(slot, c, side):
        return pltpu.make_async_remote_copy(
            src_ref=ZS.at[slot, c], dst_ref=ZR.at[slot, c, 1 - side],
            send_sem=zs_sem.at[slot, c, side], recv_sem=zr_sem.at[slot, c, 1 - side],
            device_id=target("z", side), device_id_type=MESH)

    def nu_copy(side):
        own, there = (CX, 0) if side else (1, CX + 1)
        return pltpu.make_async_remote_copy(
            src_ref=NU.at[own], dst_ref=NU.at[there],
            send_sem=nxs_sem.at[side], recv_sem=nxr_sem.at[1 - side],
            device_id=target("x", side), device_id_type=MESH)

    def nz_copy(side):
        return pltpu.make_async_remote_copy(
            src_ref=NZS, dst_ref=NZR.at[1 - side],
            send_sem=nzs_sem.at[side], recv_sem=nzr_sem.at[1 - side],
            device_id=target("z", side), device_id_type=MESH)

    def inv_copy(side):
        return pltpu.make_async_remote_copy(
            src_ref=IS.at[side], dst_ref=IR.at[1 - side],
            send_sem=is_sem.at[side], recv_sem=ir_sem.at[1 - side],
            device_id=target("z", side), device_id_type=MESH)

    def end_copy(k, side):
        return pltpu.make_async_remote_copy(
            src_ref=HS.at[k, side], dst_ref=HR.at[k, 1 - side],
            send_sem=hs_sem.at[k, side], recv_sem=hr_sem.at[k, 1 - side],
            device_id=target("z", side), device_id_type=MESH)

    def both(axis, act):
        for side in (0, 1):
            @pl.when(has[(axis, side)])
            def _():
                act(side)

    def exchange_start(phase):
        def send(i, carry):
            peer = lax.rem(dev + i, ndev)
            pltpu.make_async_remote_copy(
                src_ref=AS.at[phase, peer], dst_ref=AR.at[phase, dev],
                send_sem=as_sem.at[phase], recv_sem=ar_sem.at[phase],
                device_id={"dev": peer}, device_id_type=MESH).start()
            return carry

        lax.fori_loop(1, ndev, send, 0)
        AR[phase, dev] = AS[phase, dev]

    def exchange_wait(phase):
        copy = pltpu.make_async_remote_copy(
            src_ref=AS.at[phase, pl.ds(0, ndev - 1)], dst_ref=AR.at[phase, pl.ds(0, ndev - 1)],
            send_sem=as_sem.at[phase], recv_sem=ar_sem.at[phase],
            device_id={"dev": lax.rem(dev + 1, ndev)}, device_id_type=MESH)
        copy.wait_send()
        copy.wait_recv()

    def dot(a, b):
        return lax.dot_general(a, b, (((1,), (0,)), ((), ())), precision=HIGHEST, preferred_element_type=F32)

    def tall(rows):
        return jnp.concatenate([rows, jnp.zeros((LANES - ROWS, LANES), F32)], axis=0)

    def pack_plane(ref, x, tiles):
        packed = tiles[0]
        for j in range(1, 8):
            packed = jnp.where((lane == 2 * j) | (lane == 2 * j - 1), pltpu.roll(tiles[j], 2 * j, 1), packed)
        m = lax.rem(x, 8)
        packed = pltpu.roll(packed, 16 * m, 1)
        here = lax.rem(lane + 1, LANES) // 16 == m
        v = x // 8
        ref[v] = jnp.where(here, packed, ref[v])

    def merged(low, high):
        return jnp.where(lane % 2 == 0, pltpu.roll(low, 1, 1), pltpu.roll(high, LANES - 1, 1))

    def z_pair(tile, mx, j):
        h = pltpu.roll(mx, (LANES - 2 * j) % LANES, 1)
        zm = jnp.where(lane == 0, h, pltpu.roll(tile, 1, 1))
        zp = jnp.where(lane == LANES - 1, h, pltpu.roll(tile, LANES - 1, 1))
        return zm, zp

    def halo_row(x):
        return pltpu.roll(MV[x // 8], lax.rem(LANES - 16 * lax.rem(x, 8), LANES), 1)

    zero_plane = jnp.zeros((NY, LANES), F32)
    for slot in (0, 1):
        for c in range(3):
            U[slot, c, 0] = zero_plane
            U[slot, c, CX + 1] = zero_plane
    NU[0] = zero_plane
    NU[CX + 1] = zero_plane
    ZR[...] = jnp.zeros(ZR.shape, F32)
    ZS[...] = jnp.zeros(ZS.shape, F32)
    NZR[...] = jnp.zeros(NZR.shape, F32)
    NZS[...] = jnp.zeros(NZS.shape, F32)
    IR[...] = jnp.zeros(IR.shape, F32)
    IS[...] = jnp.zeros(IS.shape, F32)
    HR[...] = jnp.zeros(HR.shape, F32)
    HS[...] = jnp.zeros(HS.shape, F32)

    barrier = pltpu.get_barrier_semaphore()

    def greet(i, carry):
        pl.semaphore_signal(barrier, inc=1, device_id={"dev": lax.rem(dev + i, ndev)}, device_id_type=MESH)
        return carry

    lax.fori_loop(1, ndev, greet, 0)
    both("x", lambda side: pl.semaphore_signal(barrier, inc=1, device_id=target("x", side), device_id_type=MESH))

    def take(x, carry):
        tiles = []
        for j in range(8):
            tile = nu_ref[x, pl.ds(j, 8, stride=8), :]
            NU[x + 1, pl.ds(8 * j, 8), :] = tile
            tiles.append(tile)
        pack_plane(NZS, x, tiles)
        for c in range(3):
            tiles = []
            for j in range(8):
                tile = vel_ref[c, x, pl.ds(j, 8, stride=8), :]
                U[0, c, x + 1, pl.ds(8 * j, 8), :] = tile
                tiles.append(tile)
            pack_plane(ZS.at[0, c], x, tiles)
        return carry

    lax.fori_loop(0, CX, take, 0)
    rows256 = lax.broadcasted_iota(jnp.int32, (8 * ndev, LANES), 0)
    one_hot = jnp.where(rows256 == key_ref[...], 1.0, 0.0).astype(F32)
    S[...] = one_hot
    ST[...] = one_hot.T
    rows128 = lax.broadcasted_iota(jnp.int32, (LANES, LANES), 0)
    names = jnp.where(rows128 == tgt_ref[...], 1.0, 0.0).astype(F32)
    AS[0] = dot(one_hot, names.T).reshape(ndev, 8, LANES)
    for a in range(6):
        IS[0, pl.ds(6 * a, 6), :] = inv_ref[a, :, 0, :]
        IS[1, pl.ds(6 * a, 6), :] = inv_ref[a, :, NB - 1, :]

    others = (ndev - 1) + jnp.where(has[("x", 0)], 1, 0) + jnp.where(has[("x", 1)], 1, 0)
    pl.semaphore_wait(barrier, others)

    both("x", lambda side: nu_copy(side).start())
    both("z", lambda side: nz_copy(side).start())
    exchange_start(0)
    for c in range(3):
        both("x", lambda side: u_copy(0, c, side).start())
        both("z", lambda side: z_copy(0, c, side).start())
    both("z", lambda side: inv_copy(side).start())

    SH[...] = jnp.zeros(SH.shape, F32)
    FORCE[...] = jnp.zeros(FORCE.shape, F32)
    for f in range(6):
        SH[f, pl.ds(0, NB), :] = state_ref[f]

    def ends(right, left):
        return jnp.where(sub == 0, right, jnp.where(sub == 7, left, 0.0))

    exchange_wait(0)
    got = AR[0].reshape(8 * ndev, LANES)
    G[...] = got
    GT[...] = got.T

    def send_wall(k):
        rows = jnp.concatenate([SH[f, pl.ds(0, NB), :] for f in range(3)], axis=0)
        AS[1 + k] = dot(G[...], tall(rows)).reshape(ndev, 8, LANES)
        exchange_start(1 + k)

    def take_wall(k):
        exchange_wait(1 + k)
        wall = dot(ST[...], AR[1 + k].reshape(8 * ndev, LANES))
        WROW[...] = wall[:ROWS]
        for q in range(ROWS):
            WALL[q] = jnp.broadcast_to(wall[q : q + 1], (8, LANES))

    send_wall(0)

    both("x", lambda side: nu_copy(side).wait_send())
    both("x", lambda side: nu_copy(1 - side).wait_recv())
    both("z", lambda side: nz_copy(side).wait_send())
    both("z", lambda side: nz_copy(1 - side).wait_recv())
    for v in range(2):
        MV[v] = merged(NZR[0, v], NZR[1, v])

    def coefficients(x, carry):
        mx = halo_row(x)
        tiles = [NU[x + 1, pl.ds(8 * j, 8), :] for j in range(8)]
        for j in range(8):
            rows = pl.ds(8 * j, 8)
            t = tiles[j]
            zm, zp = z_pair(t, mx, j)
            ym = tiles[j - 1] if j else jnp.where(sub == 0, t, pltpu.roll(tiles[7], 1, 0))
            yp = tiles[j + 1] if j < 7 else jnp.where(sub == 7, t, pltpu.roll(tiles[0], 7, 0))
            faces = [0.5 * (t + o) for o in (NU[x, rows, :], NU[x + 2, rows, :], zm, zp, ym, yp)]
            total = 1.0 + faces[0]
            for f in faces[1:]:
                total = total + f
            inverse = 1.0 / total
            for n, f in enumerate(faces):
                CF[n, x, rows, :] = f * inverse
            for c in range(3):
                RHS[c, x, rows, :] = src_ref[c, x, pl.ds(j, 8, stride=8), :] * inverse
        return carry

    lax.fori_loop(0, CX, coefficients, 0)

    both("z", lambda side: inv_copy(side).wait_send())
    both("z", lambda side: inv_copy(1 - side).wait_recv())
    for a in range(6):
        for b in range(6):
            n = 6 * a + b
            INV[n, pl.ds(0, NB), :] = inv_ref[a, b]
            INV[n, pl.ds(NB, 8), :] = ends(IR[1, pl.ds(n, 1), :], IR[0, pl.ds(n, 1), :])

    def plane(c, x, old, new):
        mx = halo_row(x)
        tiles = [U[old, c, x + 1, pl.ds(8 * j, 8), :] for j in range(8)]
        done = []
        for j in range(8):
            rows = pl.ds(8 * j, 8)
            t = tiles[j]
            zm, zp = z_pair(t, mx, j)
            ym = tiles[j - 1] if j else jnp.where(sub == 0, WALL[c * CX + x], pltpu.roll(tiles[7], 1, 0))
            yp = tiles[j + 1] if j < 7 else jnp.where(sub == 7, 0.0, pltpu.roll(tiles[0], 7, 0))
            num = RHS[c, x, rows, :] + CF[0, x, rows, :] * U[old, c, x, rows, :]
            num = num + CF[1, x, rows, :] * U[old, c, x + 2, rows, :]
            num = num + CF[2, x, rows, :] * zm + CF[3, x, rows, :] * zp
            num = num + CF[4, x, rows, :] * ym + CF[5, x, rows, :] * yp
            U[new, c, x + 1, rows, :] = num
            done.append(num)
        pack_plane(ZS.at[new, c], x, done)

    last = SUBITERS * SWEEPS

    def level(k, carry):
        new = lax.rem(k, 2)
        old = 1 - new

        def component(c, carry):
            both("z", lambda side: z_copy(old, c, 1 - side).wait_recv())
            for v in range(2):
                MV[v] = merged(ZR[old, c, 0, v], ZR[old, c, 1, v])
            both("x", lambda side: u_copy(old, c, 1 - side).wait_recv())

            @pl.when(k >= 2)
            def _():
                both("x", lambda side: u_copy(new, c, side).wait_send())
                both("z", lambda side: z_copy(new, c, side).wait_send())

            def edge(i, carry):
                plane(c, i * (CX - 1), old, new)
                return carry

            lax.fori_loop(0, 2, edge, 0)

            @pl.when(k < last)
            def _():
                both("x", lambda side: u_copy(new, c, side).start())

            def inner(x, carry):
                plane(c, x, old, new)
                return carry

            lax.fori_loop(1, CX - 1, inner, 0)

            @pl.when(k < last)
            def _():
                both("z", lambda side: z_copy(new, c, side).start())
            return carry

        lax.fori_loop(0, 3, component, 0)
        return carry

    def shell_sweep(step, carry):
        drive = []
        lane24 = lax.broadcasted_iota(jnp.int32, (24, LANES), 1)
        for f in range(6):
            s = SH[f]
            up = pltpu.roll(s, 1, 1)
            before = jnp.where(lane24 == 0, pltpu.roll(up, 1, 0), up)
            down = pltpu.roll(s, LANES - 1, 1)
            after = jnp.where(lane24 == LANES - 1, pltpu.roll(down, 23, 0), down)
            drive.append(FORCE[f] + 0.4 * (before + after))
        for a in range(6):
            total = INV[6 * a] * drive[0]
            for b in range(1, 6):
                total = total + INV[6 * a + b] * drive[b]
            SH[a] = total
        return carry

    def subiteration(k, carry):
        take_wall(k)
        lax.fori_loop(k * SWEEPS + 1, (k + 1) * SWEEPS + 1, level, 0)
        double = 2.0 * NU[pl.ds(1, CX), 0, :]
        pulls = []
        for c in range(3):
            wall = WROW[pl.ds(CX * c, CX), :]
            pulls.append(double * (U[0, c, pl.ds(1, CX), 0, :] - wall))
        AS[3 + k] = dot(S[...], tall(jnp.concatenate(pulls, axis=0))).reshape(ndev, 8, LANES)
        exchange_start(3 + k)
        exchange_wait(3 + k)
        added = dot(GT[...], AR[3 + k].reshape(8 * ndev, LANES))
        for f in range(6):
            force = load_ref[f]
            if f < 3:
                force = force + added[NB * f : NB * (f + 1)]
            FORCE[f, pl.ds(0, NB), :] = force
            HS[k, 0, pl.ds(f, 1), :] = force[0:1]
            HS[k, 1, pl.ds(f, 1), :] = force[NB - 1 : NB]
            HS[k, 0, pl.ds(8 + f, 1), :] = SH[f, pl.ds(0, 1), :]
            HS[k, 1, pl.ds(8 + f, 1), :] = SH[f, pl.ds(NB - 1, 1), :]
        both("z", lambda side: end_copy(k, side).start())
        both("z", lambda side: end_copy(k, side).wait_send())
        both("z", lambda side: end_copy(k, 1 - side).wait_recv())
        for f in range(6):
            FORCE[f, pl.ds(NB, 8), :] = ends(HR[k, 1, pl.ds(f, 1), :], HR[k, 0, pl.ds(f, 1), :])
            SH[f, pl.ds(NB, 8), :] = ends(HR[k, 1, pl.ds(8 + f, 1), :], HR[k, 0, pl.ds(8 + f, 1), :])
        lax.fori_loop(0, SHELL_SWEEPS, shell_sweep, 0)

        @pl.when(k + 1 < SUBITERS)
        def _():
            send_wall(k + 1)
        return carry

    lax.fori_loop(0, SUBITERS, subiteration, 0)

    for f in range(6):
        sout_ref[f] = SH[f, pl.ds(0, NB), :]

    def give(x, carry):
        for c in range(3):
            for j in range(8):
                uout_ref[c, x, pl.ds(j, 8, stride=8), :] = U[0, c, x + 1, pl.ds(8 * j, 8), :]
        return carry

    lax.fori_loop(0, CX, give, 0)
    for c in range(3):
        both("x", lambda side: u_copy(1, c, side).wait_send())
        both("z", lambda side: z_copy(1, c, side).wait_send())


def body(velocity, source, viscosity, owners, targets, shell_load, shell_state, shell_inverse):
    nsec = lax.axis_size("sec")
    ndev = lax.axis_size("dev")
    owner = owners.reshape(CX)
    place = jnp.arange(CX, dtype=jnp.int32)
    earlier = (owner[:, None] == owner[None, :]) & (place[:, None] < place[None, :])
    rank = jnp.sum(jnp.where(earlier, 1, 0), axis=0).astype(jnp.int32)
    key = owner * 8 + rank
    keys = jnp.concatenate([key, key + 2, key + 4, jnp.full((LANES - ROWS,), -1, jnp.int32)])[None, :]
    name = targets.reshape(CX)
    names = jnp.concatenate([name, name + NB, name + 2 * NB, jnp.full((LANES - ROWS,), -1, jnp.int32)])[None, :]

    vmem = pl.BlockSpec(memory_space=pltpu.VMEM)
    dma = pltpu.SemaphoreType.DMA
    out = pl.pallas_call(
        lambda *refs: kernel(nsec, ndev, *refs),
        out_shape=(
            jax.ShapeDtypeStruct((3, CX, NY, LANES), F32),
            jax.ShapeDtypeStruct((6, NB, LANES), F32),
        ),
        in_specs=[vmem] * 8,
        out_specs=(vmem, vmem),
        scratch_shapes=[
            pltpu.VMEM((2, 3, CX + 2, NY, LANES), F32),
            pltpu.VMEM((CX + 2, NY, LANES), F32),
            pltpu.VMEM((6, CX, NY, LANES), F32),
            pltpu.VMEM((3, CX, NY, LANES), F32),
            pltpu.VMEM((2, 3, 2, 8, LANES), F32),
            pltpu.VMEM((2, 3, 2, 2, 8, LANES), F32),
            pltpu.VMEM((2, 8, LANES), F32),
            pltpu.VMEM((2, 8, LANES), F32),
            pltpu.VMEM((2, 2, 8, LANES), F32),
            pltpu.VMEM((8 * ndev, LANES), F32),
            pltpu.VMEM((LANES, 8 * ndev), F32),
            pltpu.VMEM((8 * ndev, LANES), F32),
            pltpu.VMEM((LANES, 8 * ndev), F32),
            pltpu.VMEM((5, ndev, 8, LANES), F32),
            pltpu.VMEM((5, ndev, 8, LANES), F32),
            pltpu.VMEM((ROWS, LANES), F32),
            pltpu.VMEM((ROWS, 8, LANES), F32),
            pltpu.VMEM((6, 24, LANES), F32),
            pltpu.VMEM((6, 24, LANES), F32),
            pltpu.VMEM((36, 24, LANES), F32),
            pltpu.VMEM((2, 40, LANES), F32),
            pltpu.VMEM((2, 40, LANES), F32),
            pltpu.VMEM((2, 2, 16, LANES), F32),
            pltpu.VMEM((2, 2, 16, LANES), F32),
            dma((2, 3, 2)), dma((2, 3, 2)), dma((2, 3, 2)), dma((2, 3, 2)),
            dma((2,)), dma((2,)), dma((2,)), dma((2,)),
            dma((5,)), dma((5,)),
            dma((2,)), dma((2,)), dma((2, 2)), dma((2, 2)),
        ],
        compiler_params=pltpu.CompilerParams(
            collective_id=0, has_side_effects=True, vmem_limit_bytes=40 * 1024 * 1024),
    )(
        velocity, source, viscosity, keys, names,
        shell_load.reshape(6, NB, LANES), shell_state.reshape(6, NB, LANES),
        shell_inverse.reshape(6, 6, NB, LANES),
    )
    return out[0], out[1].reshape(6, NB * LANES)


def solution(mesh):
    in_specs = (
        P(None, "sec", None, "dev"),
        P(None, "sec", None, "dev"),
        P("sec", None, "dev"),
        P("dev", "sec", None),
        P("dev", "sec"),
        P(None, ("sec", "dev")),
        P(None, ("sec", "dev")),
        P(None, None, ("sec", "dev")),
    )
    out_specs = (P(None, "sec", None, "dev"), P(None, ("sec", "dev")))
    return jax.shard_map(body, mesh=mesh, in_specs=in_specs, out_specs=out_specs, check_vma=False)
```

```python
import jax
import jax.numpy as jnp
from jax import lax
from jax.experimental import pallas as pl
from jax.experimental.pallas import tpu as pltpu
from jax.sharding import PartitionSpec as P

SWEEPS = 8
SHELL_SWEEPS = 8
SUBITERS = 2
CX = 16
NY = 64
LANES = 128
NB = 16
ROWS = 3 * CX
MESH = pl.DeviceIdType.MESH
F32 = jnp.float32
HIGHEST = lax.Precision.HIGHEST


def kernel(
    nsec, ndev,
    vel_ref, src_ref, nu_ref, key_ref, tgt_ref, load_ref, state_ref, inv_ref,
    uout_ref, sout_ref,
    UA, UB, NU, CF, RHS, ZS, ZR, NZS, NZR,
    S, ST, G, GT, AS, AR, WROW, WALL,
    SH, FORCE, INV, IS, IR, HS, HR,
    xs_sem, xr_sem, zs_sem, zr_sem, nxs_sem, nxr_sem, nzs_sem, nzr_sem,
    as_sem, ar_sem, is_sem, ir_sem, hs_sem, hr_sem,
):
    sec = lax.axis_index("sec")
    dev = lax.axis_index("dev")
    has = {("x", 0): sec > 0, ("x", 1): sec < nsec - 1, ("z", 0): dev > 0, ("z", 1): dev < ndev - 1}
    lane = lax.broadcasted_iota(jnp.int32, (8, LANES), 1)
    sub = lax.broadcasted_iota(jnp.int32, (8, LANES), 0)

    def target(axis, side):
        step = 1 if side else -1
        return {"sec": sec + step} if axis == "x" else {"dev": dev + step}

    def u_copy(slot, c, side):
        own, there = (CX, 0) if side else (1, CX + 1)
        u = (UA, UB)[slot]
        return pltpu.make_async_remote_copy(
            src_ref=u.at[c, own], dst_ref=u.at[c, there],
            send_sem=xs_sem.at[slot, c, side], recv_sem=xr_sem.at[slot, c, 1 - side],
            device_id=target("x", side), device_id_type=MESH)

    def z_copy(slot, c, side):
        return pltpu.make_async_remote_copy(
            src_ref=ZS.at[slot, c], dst_ref=ZR.at[slot, c, 1 - side],
            send_sem=zs_sem.at[slot, c, side], recv_sem=zr_sem.at[slot, c, 1 - side],
            device_id=target("z", side), device_id_type=MESH)

    def nu_copy(side):
        own, there = (CX, 0) if side else (1, CX + 1)
        return pltpu.make_async_remote_copy(
            src_ref=NU.at[own], dst_ref=NU.at[there],
            send_sem=nxs_sem.at[side], recv_sem=nxr_sem.at[1 - side],
            device_id=target("x", side), device_id_type=MESH)

    def nz_copy(side):
        return pltpu.make_async_remote_copy(
            src_ref=NZS, dst_ref=NZR.at[1 - side],
            send_sem=nzs_sem.at[side], recv_sem=nzr_sem.at[1 - side],
            device_id=target("z", side), device_id_type=MESH)

    def inv_copy(side):
        return pltpu.make_async_remote_copy(
            src_ref=IS.at[side], dst_ref=IR.at[1 - side],
            send_sem=is_sem.at[side], recv_sem=ir_sem.at[1 - side],
            device_id=target("z", side), device_id_type=MESH)

    def end_copy(k, side):
        return pltpu.make_async_remote_copy(
            src_ref=HS.at[k, side], dst_ref=HR.at[k, 1 - side],
            send_sem=hs_sem.at[k, side], recv_sem=hr_sem.at[k, 1 - side],
            device_id=target("z", side), device_id_type=MESH)

    def both(axis, act):
        for side in (0, 1):
            @pl.when(has[(axis, side)])
            def _():
                act(side)

    def exchange_start(phase):
        def send(i, carry):
            peer = lax.rem(dev + i, ndev)
            pltpu.make_async_remote_copy(
                src_ref=AS.at[phase, peer], dst_ref=AR.at[phase, dev],
                send_sem=as_sem.at[phase], recv_sem=ar_sem.at[phase],
                device_id={"dev": peer}, device_id_type=MESH).start()
            return carry

        lax.fori_loop(1, ndev, send, 0)
        AR[phase, dev] = AS[phase, dev]

    def exchange_wait(phase):
        copy = pltpu.make_async_remote_copy(
            src_ref=AS.at[phase, pl.ds(0, ndev - 1)], dst_ref=AR.at[phase, pl.ds(0, ndev - 1)],
            send_sem=as_sem.at[phase], recv_sem=ar_sem.at[phase],
            device_id={"dev": lax.rem(dev + 1, ndev)}, device_id_type=MESH)
        copy.wait_send()
        copy.wait_recv()

    def dot(a, b):
        return lax.dot_general(a, b, (((1,), (0,)), ((), ())), precision=HIGHEST, preferred_element_type=F32)

    def tall(rows):
        return jnp.concatenate([rows, jnp.zeros((LANES - ROWS, LANES), F32)], axis=0)

    def packed(x, tiles, held):
        for j in range(8):
            q = 8 * (x % 8) + j
            here = (lane == 2 * q) | (lane == (2 * q - 1) % LANES)
            moved = pltpu.roll(tiles[j], 2 * q, 1) if q else tiles[j]
            held = moved if held is None else jnp.where(here, moved, held)
        return held

    def merged(low, high):
        return jnp.where(lane % 2 == 0, pltpu.roll(low, 1, 1), pltpu.roll(high, LANES - 1, 1))

    def z_pair(tile, halo, x, j):
        q = 8 * (x % 8) + j
        h = pltpu.roll(halo, LANES - 2 * q, 1) if q else halo
        zm = jnp.where(lane == 0, h, pltpu.roll(tile, 1, 1))
        zp = jnp.where(lane == LANES - 1, h, pltpu.roll(tile, LANES - 1, 1))
        return zm, zp

    zero_plane = jnp.zeros((NY, LANES), F32)
    for u in (UA, UB):
        for c in range(3):
            u[c, 0] = zero_plane
            u[c, CX + 1] = zero_plane
    NU[0] = zero_plane
    NU[CX + 1] = zero_plane
    ZR[...] = jnp.zeros(ZR.shape, F32)
    ZS[...] = jnp.zeros(ZS.shape, F32)
    NZR[...] = jnp.zeros(NZR.shape, F32)
    NZS[...] = jnp.zeros(NZS.shape, F32)
    IR[...] = jnp.zeros(IR.shape, F32)
    IS[...] = jnp.zeros(IS.shape, F32)
    HR[...] = jnp.zeros(HR.shape, F32)
    HS[...] = jnp.zeros(HS.shape, F32)

    barrier = pltpu.get_barrier_semaphore()

    def greet(i, carry):
        pl.semaphore_signal(barrier, inc=1, device_id={"dev": lax.rem(dev + i, ndev)}, device_id_type=MESH)
        return carry

    lax.fori_loop(1, ndev, greet, 0)
    both("x", lambda side: pl.semaphore_signal(barrier, inc=1, device_id=target("x", side), device_id_type=MESH))

    def take(v, carry):
        held = None
        for i in range(8):
            x = 8 * v + i
            tiles = [nu_ref[x, pl.ds(j, 8, stride=8), :] for j in range(8)]
            for j in range(8):
                NU[x + 1, pl.ds(8 * j, 8), :] = tiles[j]
            held = packed(i, tiles, held)
        NZS[v] = held
        return carry

    lax.fori_loop(0, 2, take, 0)

    def take_velocity(n, carry):
        c, v = n // 2, lax.rem(n, 2)
        held = None
        for i in range(8):
            x = 8 * v + i
            tiles = [vel_ref[c, x, pl.ds(j, 8, stride=8), :] for j in range(8)]
            for j in range(8):
                UA[c, x + 1, pl.ds(8 * j, 8), :] = tiles[j]
            held = packed(i, tiles, held)
        ZS[0, c, v] = held
        return carry

    lax.fori_loop(0, 6, take_velocity, 0)
    rows256 = lax.broadcasted_iota(jnp.int32, (8 * ndev, LANES), 0)
    one_hot = jnp.where(rows256 == key_ref[...], 1.0, 0.0).astype(F32)
    S[...] = one_hot
    ST[...] = one_hot.T
    rows128 = lax.broadcasted_iota(jnp.int32, (LANES, LANES), 0)
    names = jnp.where(rows128 == tgt_ref[...], 1.0, 0.0).astype(F32)
    AS[0] = dot(one_hot, names.T).reshape(ndev, 8, LANES)
    for a in range(6):
        IS[0, pl.ds(6 * a, 6), :] = inv_ref[a, :, 0, :]
        IS[1, pl.ds(6 * a, 6), :] = inv_ref[a, :, NB - 1, :]

    others = (ndev - 1) + jnp.where(has[("x", 0)], 1, 0) + jnp.where(has[("x", 1)], 1, 0)
    pl.semaphore_wait(barrier, others)

    both("x", lambda side: nu_copy(side).start())
    both("z", lambda side: nz_copy(side).start())
    exchange_start(0)
    for c in range(3):
        both("x", lambda side: u_copy(0, c, side).start())
        both("z", lambda side: z_copy(0, c, side).start())
    both("z", lambda side: inv_copy(side).start())

    SH[...] = jnp.zeros(SH.shape, F32)
    FORCE[...] = jnp.zeros(FORCE.shape, F32)
    for f in range(6):
        SH[f, pl.ds(0, NB), :] = state_ref[f]

    def ends(right, left):
        return jnp.where(sub == 0, right, jnp.where(sub == 7, left, 0.0))

    exchange_wait(0)
    got = AR[0].reshape(8 * ndev, LANES)
    G[...] = got
    GT[...] = got.T

    def send_wall(k):
        rows = jnp.concatenate([SH[f, pl.ds(0, NB), :] for f in range(3)], axis=0)
        AS[1 + k] = dot(G[...], tall(rows)).reshape(ndev, 8, LANES)
        exchange_start(1 + k)

    def take_wall(k):
        exchange_wait(1 + k)
        wall = dot(ST[...], AR[1 + k].reshape(8 * ndev, LANES))
        WROW[...] = wall[:ROWS]
        for q in range(ROWS):
            WALL[q] = jnp.broadcast_to(wall[q : q + 1], (8, LANES))

    send_wall(0)

    both("x", lambda side: nu_copy(side).wait_send())
    both("x", lambda side: nu_copy(1 - side).wait_recv())
    both("z", lambda side: nz_copy(side).wait_send())
    both("z", lambda side: nz_copy(1 - side).wait_recv())
    def coefficients(v, carry):
        halo = merged(NZR[0, v], NZR[1, v])
        for i in range(8):
            x = 8 * v + i
            tiles = [NU[x + 1, pl.ds(8 * j, 8), :] for j in range(8)]
            for j in range(8):
                rows = pl.ds(8 * j, 8)
                t = tiles[j]
                zm, zp = z_pair(t, halo, i, j)
                ym = tiles[j - 1] if j else jnp.where(sub == 0, t, pltpu.roll(tiles[7], 1, 0))
                yp = tiles[j + 1] if j < 7 else jnp.where(sub == 7, t, pltpu.roll(tiles[0], 7, 0))
                faces = [0.5 * (t + o) for o in (NU[x, rows, :], NU[x + 2, rows, :], zm, zp, ym, yp)]
                total = 1.0 + faces[0]
                for f in faces[1:]:
                    total = total + f
                inverse = 1.0 / total
                for n, f in enumerate(faces):
                    CF[n, x, rows, :] = f * inverse
                for c in range(3):
                    RHS[c, x, rows, :] = src_ref[c, x, pl.ds(j, 8, stride=8), :] * inverse
        return carry

    lax.fori_loop(0, 2, coefficients, 0)

    both("z", lambda side: inv_copy(side).wait_send())
    both("z", lambda side: inv_copy(1 - side).wait_recv())
    for a in range(6):
        for b in range(6):
            n = 6 * a + b
            INV[n, pl.ds(0, NB), :] = inv_ref[a, b]
            INV[n, pl.ds(NB, 8), :] = ends(IR[1, pl.ds(n, 1), :], IR[0, pl.ds(n, 1), :])

    def plane(c, x, old, new, halo, held):
        tiles = [old[c, x + 1, pl.ds(8 * j, 8), :] for j in range(8)]
        done = []
        for j in range(8):
            rows = pl.ds(8 * j, 8)
            t = tiles[j]
            zm, zp = z_pair(t, halo, x, j)
            ym = tiles[j - 1] if j else jnp.where(sub == 0, WALL[c * CX + x], pltpu.roll(tiles[7], 1, 0))
            yp = tiles[j + 1] if j < 7 else jnp.where(sub == 7, 0.0, pltpu.roll(tiles[0], 7, 0))
            num = RHS[c, x, rows, :] + CF[0, x, rows, :] * old[c, x, rows, :]
            num = num + CF[1, x, rows, :] * old[c, x + 2, rows, :]
            num = num + CF[4, x, rows, :] * ym + CF[5, x, rows, :] * yp
            num = num + (CF[2, x, rows, :] * zm + CF[3, x, rows, :] * zp)
            new[c, x + 1, rows, :] = num
            done.append(num)
        return packed(x, done, held)

    last = SUBITERS * SWEEPS

    def level(k, slot):
        old, new = ((UB, UA), (UA, UB))[slot]

        def component(c, carry):
            both("z", lambda side: z_copy(1 - slot, c, 1 - side).wait_recv())
            halos = [merged(ZR[1 - slot, c, 0, v], ZR[1 - slot, c, 1, v]) for v in range(2)]
            both("x", lambda side: u_copy(1 - slot, c, 1 - side).wait_recv())

            @pl.when(k >= 2)
            def _():
                both("x", lambda side: u_copy(slot, c, side).wait_send())
                both("z", lambda side: z_copy(slot, c, side).wait_send())

            first = plane(c, 0, old, new, halos[0], None)
            second = plane(c, CX - 1, old, new, halos[1], None)

            @pl.when(k < last)
            def _():
                both("x", lambda side: u_copy(slot, c, side).start())

            for x in range(1, CX // 2):
                first = plane(c, x, old, new, halos[0], first)
            ZS[slot, c, 0] = first
            for x in range(CX // 2, CX - 1):
                second = plane(c, x, old, new, halos[1], second)
            ZS[slot, c, 1] = second

            @pl.when(k < last)
            def _():
                both("z", lambda side: z_copy(slot, c, side).start())
            return carry

        lax.fori_loop(0, 3, component, 0)

    def levels(n, carry):
        level(2 * n + 1, 1)
        level(2 * n + 2, 0)
        return carry

    def shell_sweep(step, carry):
        drive = []
        lane24 = lax.broadcasted_iota(jnp.int32, (24, LANES), 1)
        for f in range(6):
            s = SH[f]
            up = pltpu.roll(s, 1, 1)
            before = jnp.where(lane24 == 0, pltpu.roll(up, 1, 0), up)
            down = pltpu.roll(s, LANES - 1, 1)
            after = jnp.where(lane24 == LANES - 1, pltpu.roll(down, 23, 0), down)
            drive.append(FORCE[f] + 0.4 * (before + after))
        for a in range(6):
            total = INV[6 * a] * drive[0]
            for b in range(1, 6):
                total = total + INV[6 * a + b] * drive[b]
            SH[a] = total
        return carry

    def subiteration(k, carry):
        take_wall(k)
        lax.fori_loop(k * (SWEEPS // 2), (k + 1) * (SWEEPS // 2), levels, 0)
        double = 2.0 * NU[pl.ds(1, CX), 0, :]
        pulls = []
        for c in range(3):
            wall = WROW[pl.ds(CX * c, CX), :]
            pulls.append(double * (UA[c, pl.ds(1, CX), 0, :] - wall))
        AS[3 + k] = dot(S[...], tall(jnp.concatenate(pulls, axis=0))).reshape(ndev, 8, LANES)
        exchange_start(3 + k)
        exchange_wait(3 + k)
        added = dot(GT[...], AR[3 + k].reshape(8 * ndev, LANES))
        for f in range(6):
            force = load_ref[f]
            if f < 3:
                force = force + added[NB * f : NB * (f + 1)]
            FORCE[f, pl.ds(0, NB), :] = force
            HS[k, 0, pl.ds(f, 1), :] = force[0:1]
            HS[k, 1, pl.ds(f, 1), :] = force[NB - 1 : NB]
            HS[k, 0, pl.ds(8 + f, 1), :] = SH[f, pl.ds(0, 1), :]
            HS[k, 1, pl.ds(8 + f, 1), :] = SH[f, pl.ds(NB - 1, 1), :]
        both("z", lambda side: end_copy(k, side).start())
        both("z", lambda side: end_copy(k, side).wait_send())
        both("z", lambda side: end_copy(k, 1 - side).wait_recv())
        for f in range(6):
            FORCE[f, pl.ds(NB, 8), :] = ends(HR[k, 1, pl.ds(f, 1), :], HR[k, 0, pl.ds(f, 1), :])
            SH[f, pl.ds(NB, 8), :] = ends(HR[k, 1, pl.ds(8 + f, 1), :], HR[k, 0, pl.ds(8 + f, 1), :])
        lax.fori_loop(0, SHELL_SWEEPS, shell_sweep, 0)

        @pl.when(k + 1 < SUBITERS)
        def _():
            send_wall(k + 1)
        return carry

    lax.fori_loop(0, SUBITERS, subiteration, 0)

    for f in range(6):
        sout_ref[f] = SH[f, pl.ds(0, NB), :]

    def give(x, carry):
        for c in range(3):
            for j in range(8):
                uout_ref[c, x, pl.ds(j, 8, stride=8), :] = UA[c, x + 1, pl.ds(8 * j, 8), :]
        return carry

    lax.fori_loop(0, CX, give, 0)
    for c in range(3):
        both("x", lambda side: u_copy(1, c, side).wait_send())
        both("z", lambda side: z_copy(1, c, side).wait_send())


def body(velocity, source, viscosity, owners, targets, shell_load, shell_state, shell_inverse):
    nsec = lax.axis_size("sec")
    ndev = lax.axis_size("dev")
    owner = owners.reshape(CX)
    place = jnp.arange(CX, dtype=jnp.int32)
    earlier = (owner[:, None] == owner[None, :]) & (place[:, None] < place[None, :])
    rank = jnp.sum(jnp.where(earlier, 1, 0), axis=0).astype(jnp.int32)
    key = owner * 8 + rank
    keys = jnp.concatenate([key, key + 2, key + 4, jnp.full((LANES - ROWS,), -1, jnp.int32)])[None, :]
    name = targets.reshape(CX)
    names = jnp.concatenate([name, name + NB, name + 2 * NB, jnp.full((LANES - ROWS,), -1, jnp.int32)])[None, :]

    vmem = pl.BlockSpec(memory_space=pltpu.VMEM)
    dma = pltpu.SemaphoreType.DMA
    out = pl.pallas_call(
        lambda *refs: kernel(nsec, ndev, *refs),
        out_shape=(
            jax.ShapeDtypeStruct((3, CX, NY, LANES), F32),
            jax.ShapeDtypeStruct((6, NB, LANES), F32),
        ),
        in_specs=[vmem] * 8,
        out_specs=(vmem, vmem),
        scratch_shapes=[
            pltpu.VMEM((3, CX + 2, NY, LANES), F32),
            pltpu.VMEM((3, CX + 2, NY, LANES), F32),
            pltpu.VMEM((CX + 2, NY, LANES), F32),
            pltpu.VMEM((6, CX, NY, LANES), F32),
            pltpu.VMEM((3, CX, NY, LANES), F32),
            pltpu.VMEM((2, 3, 2, 8, LANES), F32),
            pltpu.VMEM((2, 3, 2, 2, 8, LANES), F32),
            pltpu.VMEM((2, 8, LANES), F32),
            pltpu.VMEM((2, 2, 8, LANES), F32),
            pltpu.VMEM((8 * ndev, LANES), F32),
            pltpu.VMEM((LANES, 8 * ndev), F32),
            pltpu.VMEM((8 * ndev, LANES), F32),
            pltpu.VMEM((LANES, 8 * ndev), F32),
            pltpu.VMEM((5, ndev, 8, LANES), F32),
            pltpu.VMEM((5, ndev, 8, LANES), F32),
            pltpu.VMEM((ROWS, LANES), F32),
            pltpu.VMEM((ROWS, 8, LANES), F32),
            pltpu.VMEM((6, 24, LANES), F32),
            pltpu.VMEM((6, 24, LANES), F32),
            pltpu.VMEM((36, 24, LANES), F32),
            pltpu.VMEM((2, 40, LANES), F32),
            pltpu.VMEM((2, 40, LANES), F32),
            pltpu.VMEM((2, 2, 16, LANES), F32),
            pltpu.VMEM((2, 2, 16, LANES), F32),
            dma((2, 3, 2)), dma((2, 3, 2)), dma((2, 3, 2)), dma((2, 3, 2)),
            dma((2,)), dma((2,)), dma((2,)), dma((2,)),
            dma((5,)), dma((5,)),
            dma((2,)), dma((2,)), dma((2, 2)), dma((2, 2)),
        ],
        compiler_params=pltpu.CompilerParams(
            collective_id=0, has_side_effects=True, vmem_limit_bytes=40 * 1024 * 1024),
    )(
        velocity, source, viscosity, keys, names,
        shell_load.reshape(6, NB, LANES), shell_state.reshape(6, NB, LANES),
        shell_inverse.reshape(6, 6, NB, LANES),
    )
    return out[0], out[1].reshape(6, NB * LANES)


def solution(mesh):
    in_specs = (
        P(None, "sec", None, "dev"),
        P(None, "sec", None, "dev"),
        P("sec", None, "dev"),
        P("dev", "sec", None),
        P("dev", "sec"),
        P(None, ("sec", "dev")),
        P(None, ("sec", "dev")),
        P(None, None, ("sec", "dev")),
    )
    out_specs = (P(None, "sec", None, "dev"), P(None, ("sec", "dev")))
    return jax.shard_map(body, mesh=mesh, in_specs=in_specs, out_specs=out_specs, check_vma=False)
```

```python
import jax
import jax.numpy as jnp
from jax import lax
from jax.experimental import pallas as pl
from jax.experimental.pallas import tpu as pltpu
from jax.sharding import PartitionSpec as P

SWEEPS = 8
SHELL_SWEEPS = 8
SUBITERS = 2
CX = 16
NY = 64
LANES = 128
NB = 16
ROWS = 3 * CX
MESH = pl.DeviceIdType.MESH
F32 = jnp.float32
HIGHEST = lax.Precision.HIGHEST


def kernel(
    nsec, ndev,
    vel_ref, src_ref, nu_ref, key_ref, tgt_ref, load_ref, state_ref, inv_ref,
    uout_ref, sout_ref,
    UA, UB, NU, CF, CW, RHS, RW, ZS, ZR, NZS, NZR,
    S, ST, G, GT, AS, AR, WT, PULL, N2,
    SH, FORCE, INV, IS, IR, HS, HR,
    xs_sem, xr_sem, zs_sem, zr_sem, nxs_sem, nxr_sem, nzs_sem, nzr_sem,
    as_sem, ar_sem, is_sem, ir_sem, hs_sem, hr_sem,
):
    sec = lax.axis_index("sec")
    dev = lax.axis_index("dev")
    has = {("x", 0): sec > 0, ("x", 1): sec < nsec - 1, ("z", 0): dev > 0, ("z", 1): dev < ndev - 1}
    lane = lax.broadcasted_iota(jnp.int32, (8, LANES), 1)
    sub = lax.broadcasted_iota(jnp.int32, (8, LANES), 0)

    def target(axis, side):
        step = 1 if side else -1
        return {"sec": sec + step} if axis == "x" else {"dev": dev + step}

    def u_copy(slot, c, side):
        own, there = (CX, 0) if side else (1, CX + 1)
        u = (UA, UB)[slot]
        return pltpu.make_async_remote_copy(
            src_ref=u.at[c, own], dst_ref=u.at[c, there],
            send_sem=xs_sem.at[slot, c, side], recv_sem=xr_sem.at[slot, c, 1 - side],
            device_id=target("x", side), device_id_type=MESH)

    def z_copy(slot, c, side):
        return pltpu.make_async_remote_copy(
            src_ref=ZS.at[slot, c], dst_ref=ZR.at[slot, c, 1 - side],
            send_sem=zs_sem.at[slot, c, side], recv_sem=zr_sem.at[slot, c, 1 - side],
            device_id=target("z", side), device_id_type=MESH)

    def nu_copy(side):
        own, there = (CX, 0) if side else (1, CX + 1)
        return pltpu.make_async_remote_copy(
            src_ref=NU.at[0, own], dst_ref=NU.at[0, there],
            send_sem=nxs_sem.at[side], recv_sem=nxr_sem.at[1 - side],
            device_id=target("x", side), device_id_type=MESH)

    def nz_copy(side):
        return pltpu.make_async_remote_copy(
            src_ref=NZS, dst_ref=NZR.at[1 - side],
            send_sem=nzs_sem.at[side], recv_sem=nzr_sem.at[1 - side],
            device_id=target("z", side), device_id_type=MESH)

    def inv_copy(side):
        return pltpu.make_async_remote_copy(
            src_ref=IS.at[side], dst_ref=IR.at[1 - side],
            send_sem=is_sem.at[side], recv_sem=ir_sem.at[1 - side],
            device_id=target("z", side), device_id_type=MESH)

    def end_copy(k, side):
        return pltpu.make_async_remote_copy(
            src_ref=HS.at[k, side], dst_ref=HR.at[k, 1 - side],
            send_sem=hs_sem.at[k, side], recv_sem=hr_sem.at[k, 1 - side],
            device_id=target("z", side), device_id_type=MESH)

    def both(axis, act):
        for side in (0, 1):
            @pl.when(has[(axis, side)])
            def _():
                act(side)

    def exchange_start(phase):
        def send(i, carry):
            peer = lax.rem(dev + i, ndev)
            pltpu.make_async_remote_copy(
                src_ref=AS.at[phase, peer], dst_ref=AR.at[phase, dev],
                send_sem=as_sem.at[phase], recv_sem=ar_sem.at[phase],
                device_id={"dev": peer}, device_id_type=MESH).start()
            return carry

        lax.fori_loop(1, ndev, send, 0)
        AR[phase, dev] = AS[phase, dev]

    def exchange_wait(phase):
        copy = pltpu.make_async_remote_copy(
            src_ref=AS.at[phase, pl.ds(0, ndev - 1)], dst_ref=AR.at[phase, pl.ds(0, ndev - 1)],
            send_sem=as_sem.at[phase], recv_sem=ar_sem.at[phase],
            device_id={"dev": lax.rem(dev + 1, ndev)}, device_id_type=MESH)
        copy.wait_send()
        copy.wait_recv()

    def dot(a, b):
        return lax.dot_general(a, b, (((1,), (0,)), ((), ())), precision=HIGHEST, preferred_element_type=F32)

    def tall(rows):
        return jnp.concatenate([rows, jnp.zeros((LANES - ROWS, LANES), F32)], axis=0)

    half = lane < LANES // 2
    half16 = lax.broadcasted_iota(jnp.int32, (CX, LANES), 1) < LANES // 2

    def turn(first, second):
        top = [jnp.where(half, first[n], pltpu.roll(second[n], LANES // 2, 1)) for n in range(8)]
        low = [jnp.where(half, pltpu.roll(first[n], LANES // 2, 1), second[n]) for n in range(8)]
        return jnp.concatenate(top + low, axis=0).T

    def spread(ref, c, x, rows):
        for m in range(8):
            ref[c, x, pl.ds(m, 8, stride=8), :] = rows[8 * m : 8 * m + 8]

    def face_rows(low, high):
        return jnp.where(half16, low, high)

    def beside(low, high, before, after):
        inner = pltpu.roll(jnp.where(half16, high, low), LANES // 2, 1)
        zm = jnp.where(half16, pltpu.roll(before, LANES // 2, 1), inner)
        zp = jnp.where(half16, inner, pltpu.roll(after, LANES // 2, 1))
        return zm, zp

    def z_first(row, tile):
        return jnp.where(sub == 0, row, pltpu.roll(tile, 1, 0))

    def z_last(row, tile):
        return jnp.where(sub == 7, row, pltpu.roll(tile, 7, 0))

    zero_plane = jnp.zeros((NY, LANES), F32)
    for u in (UA, UB):
        for c in range(3):
            u[c, 0] = zero_plane
            u[c, CX + 1] = zero_plane
    NU[0, 0] = zero_plane
    NU[0, CX + 1] = zero_plane
    ZR[...] = jnp.zeros(ZR.shape, F32)
    ZS[...] = jnp.zeros(ZS.shape, F32)
    NZR[...] = jnp.zeros(NZR.shape, F32)
    NZS[...] = jnp.zeros(NZS.shape, F32)
    IR[...] = jnp.zeros(IR.shape, F32)
    IS[...] = jnp.zeros(IS.shape, F32)
    HR[...] = jnp.zeros(HR.shape, F32)
    HS[...] = jnp.zeros(HS.shape, F32)

    barrier = pltpu.get_barrier_semaphore()

    def greet(i, carry):
        pl.semaphore_signal(barrier, inc=1, device_id={"dev": lax.rem(dev + i, ndev)}, device_id_type=MESH)
        return carry

    lax.fori_loop(1, ndev, greet, 0)
    both("x", lambda side: pl.semaphore_signal(barrier, inc=1, device_id=target("x", side), device_id_type=MESH))

    def take(refs):
        def step(i, carry):
            for ref, c, out, d, shift in refs:
                first = [ref[c, 2 * i, pl.ds(8 * n, 8), :] for n in range(8)]
                second = [ref[c, 2 * i + 1, pl.ds(8 * n, 8), :] for n in range(8)]
                rows = turn(first, second)
                spread(out, d, 2 * i + shift, rows[:NY])
                spread(out, d, 2 * i + 1 + shift, rows[NY:])
            return carry

        lax.fori_loop(0, CX // 2, step, 0)

    take([(nu_ref, 0, NU, 0, 1)] + [(vel_ref, c, UA, c, 1) for c in range(3)])
    NZS[...] = face_rows(NU[0, pl.ds(1, CX), 0, :], NU[0, pl.ds(1, CX), NY - 1, :])
    for c in range(3):
        ZS[0, c] = face_rows(UA[c, pl.ds(1, CX), 0, :], UA[c, pl.ds(1, CX), NY - 1, :])
    wet = nu_ref[0, :, 0, :]
    N2[...] = 2.0 * tall(jnp.concatenate([wet, wet, wet], axis=0)).T
    rows256 = lax.broadcasted_iota(jnp.int32, (8 * ndev, LANES), 0)
    one_hot = jnp.where(rows256 == key_ref[...], 1.0, 0.0).astype(F32)
    S[...] = one_hot
    ST[...] = one_hot.T
    rows128 = lax.broadcasted_iota(jnp.int32, (LANES, LANES), 0)
    names = jnp.where(rows128 == tgt_ref[...], 1.0, 0.0).astype(F32)
    AS[0] = dot(one_hot, names.T).reshape(ndev, 8, LANES)
    for a in range(6):
        IS[0, pl.ds(6 * a, 6), :] = inv_ref[a, :, 0, :]
        IS[1, pl.ds(6 * a, 6), :] = inv_ref[a, :, NB - 1, :]

    others = (ndev - 1) + jnp.where(has[("x", 0)], 1, 0) + jnp.where(has[("x", 1)], 1, 0)
    pl.semaphore_wait(barrier, others)

    both("x", lambda side: nu_copy(side).start())
    both("z", lambda side: nz_copy(side).start())
    exchange_start(0)
    for c in range(3):
        both("x", lambda side: u_copy(0, c, side).start())
        both("z", lambda side: z_copy(0, c, side).start())
    both("z", lambda side: inv_copy(side).start())

    SH[...] = jnp.zeros(SH.shape, F32)
    FORCE[...] = jnp.zeros(FORCE.shape, F32)
    for f in range(6):
        SH[f, pl.ds(0, NB), :] = state_ref[f]

    def ends(right, left):
        return jnp.where(sub == 0, right, jnp.where(sub == 7, left, 0.0))

    exchange_wait(0)
    got = AR[0].reshape(8 * ndev, LANES)
    G[...] = got
    GT[...] = got.T

    def send_wall(k):
        rows = jnp.concatenate([SH[f, pl.ds(0, NB), :] for f in range(3)], axis=0)
        AS[1 + k] = dot(G[...], tall(rows)).reshape(ndev, 8, LANES)
        exchange_start(1 + k)

    def take_wall(k):
        exchange_wait(1 + k)
        wall = dot(ST[...], AR[1 + k].reshape(8 * ndev, LANES))
        WT[...] = wall.T
        tiles = [
            jnp.where(
                half,
                WT[pl.ds(j, 8, stride=8), :],
                pltpu.roll(WT[pl.ds(NY + j, 8, stride=8), :], LANES // 2, 1))
            for j in range(8)
        ]
        for q in range(ROWS):
            c, x = q // CX, q % CX
            for j in range(8):
                rows = pl.ds(8 * j, 8)
                wall = pltpu.roll(tiles[j], LANES - q, 1) if q else tiles[j]
                RW[c, x, rows, :] = RHS[c, x, rows, :] + CW[x, rows, :] * wall

    send_wall(0)
    take([(src_ref, c, RHS, c, 0) for c in range(3)])

    both("x", lambda side: nu_copy(side).wait_send())
    both("x", lambda side: nu_copy(1 - side).wait_recv())
    both("z", lambda side: nz_copy(side).wait_send())
    both("z", lambda side: nz_copy(1 - side).wait_recv())
    nzm, nzp = beside(NU[0, pl.ds(1, CX), 0, :], NU[0, pl.ds(1, CX), NY - 1, :], NZR[0], NZR[1])
    y_first = lane % NY == 0
    y_last = lane % NY == NY - 1
    for x in range(CX):
        tiles = [NU[0, x + 1, pl.ds(8 * j, 8), :] for j in range(8)]
        for j in range(8):
            rows = pl.ds(8 * j, 8)
            t = tiles[j]
            zm = tiles[j - 1] if j else z_first(nzm[x : x + 1], tiles[7])
            zp = tiles[j + 1] if j < 7 else z_last(nzp[x : x + 1], tiles[0])
            ym = jnp.where(y_first, t, pltpu.roll(t, 1, 1))
            yp = jnp.where(y_last, t, pltpu.roll(t, LANES - 1, 1))
            faces = [0.5 * (t + o) for o in (NU[0, x, rows, :], NU[0, x + 2, rows, :], zm, zp, ym, yp)]
            total = 1.0 + faces[0]
            for f in faces[1:]:
                total = total + f
            inverse = 1.0 / total
            for n in range(4):
                CF[n, x, rows, :] = faces[n] * inverse
            below = faces[4] * inverse
            CW[x, rows, :] = jnp.where(y_first, below, 0.0)
            CF[4, x, rows, :] = jnp.where(y_first, 0.0, below)
            CF[5, x, rows, :] = jnp.where(y_last, 0.0, faces[5] * inverse)
            for c in range(3):
                RHS[c, x, rows, :] = RHS[c, x, rows, :] * inverse

    both("z", lambda side: inv_copy(side).wait_send())
    both("z", lambda side: inv_copy(1 - side).wait_recv())
    for a in range(6):
        for b in range(6):
            n = 6 * a + b
            INV[n, pl.ds(0, NB), :] = inv_ref[a, b]
            INV[n, pl.ds(NB, 8), :] = ends(IR[1, pl.ds(n, 1), :], IR[0, pl.ds(n, 1), :])

    def plane(c, x, old, new, zms, zps):
        tiles = [old[c, x + 1, pl.ds(8 * j, 8), :] for j in range(8)]
        for j in range(8):
            rows = pl.ds(8 * j, 8)
            t = tiles[j]
            zm = tiles[j - 1] if j else z_first(zms[x : x + 1], tiles[7])
            zp = tiles[j + 1] if j < 7 else z_last(zps[x : x + 1], tiles[0])
            num = RW[c, x, rows, :] + CF[0, x, rows, :] * old[c, x, rows, :]
            num = num + CF[1, x, rows, :] * old[c, x + 2, rows, :]
            num = num + CF[2, x, rows, :] * zm + CF[3, x, rows, :] * zp
            ys = CF[4, x, rows, :] * pltpu.roll(t, 1, 1) + CF[5, x, rows, :] * pltpu.roll(t, LANES - 1, 1)
            new[c, x + 1, rows, :] = num + ys

    last = SUBITERS * SWEEPS

    def level(k, slot):
        old, new = ((UB, UA), (UA, UB))[slot]

        def component(c, carry):
            both("z", lambda side: z_copy(1 - slot, c, 1 - side).wait_recv())
            zms, zps = beside(
                old[c, pl.ds(1, CX), 0, :], old[c, pl.ds(1, CX), NY - 1, :],
                ZR[1 - slot, c, 0], ZR[1 - slot, c, 1])
            both("x", lambda side: u_copy(1 - slot, c, 1 - side).wait_recv())

            @pl.when(k >= 2)
            def _():
                both("x", lambda side: u_copy(slot, c, side).wait_send())
                both("z", lambda side: z_copy(slot, c, side).wait_send())

            plane(c, 0, old, new, zms, zps)
            plane(c, CX - 1, old, new, zms, zps)

            @pl.when(k < last)
            def _():
                both("x", lambda side: u_copy(slot, c, side).start())

            for x in range(1, CX - 1):
                plane(c, x, old, new, zms, zps)
            ZS[slot, c] = face_rows(new[c, pl.ds(1, CX), 0, :], new[c, pl.ds(1, CX), NY - 1, :])

            @pl.when(k < last)
            def _():
                both("z", lambda side: z_copy(slot, c, side).start())
            return carry

        lax.fori_loop(0, 3, component, 0)

    def levels(n, carry):
        level(2 * n + 1, 1)
        level(2 * n + 2, 0)
        return carry

    def shell_sweep(step, carry):
        drive = []
        lane24 = lax.broadcasted_iota(jnp.int32, (24, LANES), 1)
        for f in range(6):
            s = SH[f]
            up = pltpu.roll(s, 1, 1)
            before = jnp.where(lane24 == 0, pltpu.roll(up, 1, 0), up)
            down = pltpu.roll(s, LANES - 1, 1)
            after = jnp.where(lane24 == LANES - 1, pltpu.roll(down, 23, 0), down)
            drive.append(FORCE[f] + 0.4 * (before + after))
        for a in range(6):
            total = INV[6 * a] * drive[0]
            for b in range(1, 6):
                total = total + INV[6 * a + b] * drive[b]
            SH[a] = total
        return carry

    def subiteration(k, carry):
        take_wall(k)
        lax.fori_loop(k * (SWEEPS // 2), (k + 1) * (SWEEPS // 2), levels, 0)
        tiles = [jnp.zeros((8, LANES), F32) for j in range(8)]
        for q in range(ROWS):
            here = (lane == q) | (lane == q + NY)
            for j in range(8):
                tile = UA[q // CX, q % CX + 1, pl.ds(8 * j, 8), :]
                tiles[j] = jnp.where(here, pltpu.roll(tile, q, 1) if q else tile, tiles[j])
        for j in range(8):
            PULL[pl.ds(j, 8, stride=8), :] = jnp.where(half, tiles[j], 0.0)
            PULL[pl.ds(NY + j, 8, stride=8), :] = jnp.where(half, pltpu.roll(tiles[j], LANES // 2, 1), 0.0)
        pulls = N2[...] * (PULL[...] - WT[...])
        AS[3 + k] = dot(S[...], pulls.T).reshape(ndev, 8, LANES)
        exchange_start(3 + k)
        exchange_wait(3 + k)
        added = dot(GT[...], AR[3 + k].reshape(8 * ndev, LANES))
        for f in range(6):
            force = load_ref[f]
            if f < 3:
                force = force + added[NB * f : NB * (f + 1)]
            FORCE[f, pl.ds(0, NB), :] = force
            HS[k, 0, pl.ds(f, 1), :] = force[0:1]
            HS[k, 1, pl.ds(f, 1), :] = force[NB - 1 : NB]
            HS[k, 0, pl.ds(8 + f, 1), :] = SH[f, pl.ds(0, 1), :]
            HS[k, 1, pl.ds(8 + f, 1), :] = SH[f, pl.ds(NB - 1, 1), :]
        both("z", lambda side: end_copy(k, side).start())
        both("z", lambda side: end_copy(k, side).wait_send())
        both("z", lambda side: end_copy(k, 1 - side).wait_recv())
        for f in range(6):
            FORCE[f, pl.ds(NB, 8), :] = ends(HR[k, 1, pl.ds(f, 1), :], HR[k, 0, pl.ds(f, 1), :])
            SH[f, pl.ds(NB, 8), :] = ends(HR[k, 1, pl.ds(8 + f, 1), :], HR[k, 0, pl.ds(8 + f, 1), :])
        lax.fori_loop(0, SHELL_SWEEPS, shell_sweep, 0)

        @pl.when(k + 1 < SUBITERS)
        def _():
            send_wall(k + 1)
        return carry

    lax.fori_loop(0, SUBITERS, subiteration, 0)

    for f in range(6):
        sout_ref[f] = SH[f, pl.ds(0, NB), :]

    def give(i, carry):
        for c in range(3):
            rows = jnp.concatenate(
                [UA[c, 2 * i + 1 + p, pl.ds(m, 8, stride=8), :] for p in range(2) for m in range(8)], axis=0).T
            for n in range(8):
                top, low = rows[8 * n : 8 * n + 8], rows[NY + 8 * n : NY + 8 * n + 8]
                uout_ref[c, 2 * i, pl.ds(8 * n, 8), :] = jnp.where(half, top, pltpu.roll(low, LANES // 2, 1))
                uout_ref[c, 2 * i + 1, pl.ds(8 * n, 8), :] = jnp.where(half, pltpu.roll(top, LANES // 2, 1), low)
        return carry

    lax.fori_loop(0, CX // 2, give, 0)
    for c in range(3):
        both("x", lambda side: u_copy(1, c, side).wait_send())
        both("z", lambda side: z_copy(1, c, side).wait_send())


def body(velocity, source, viscosity, owners, targets, shell_load, shell_state, shell_inverse):
    nsec = lax.axis_size("sec")
    ndev = lax.axis_size("dev")
    owner = owners.reshape(CX)
    place = jnp.arange(CX, dtype=jnp.int32)
    earlier = (owner[:, None] == owner[None, :]) & (place[:, None] < place[None, :])
    rank = jnp.sum(jnp.where(earlier, 1, 0), axis=0).astype(jnp.int32)
    key = owner * 8 + rank
    keys = jnp.concatenate([key, key + 2, key + 4, jnp.full((LANES - ROWS,), -1, jnp.int32)])[None, :]
    name = targets.reshape(CX)
    names = jnp.concatenate([name, name + NB, name + 2 * NB, jnp.full((LANES - ROWS,), -1, jnp.int32)])[None, :]

    vmem = pl.BlockSpec(memory_space=pltpu.VMEM)
    dma = pltpu.SemaphoreType.DMA
    out = pl.pallas_call(
        lambda *refs: kernel(nsec, ndev, *refs),
        out_shape=(
            jax.ShapeDtypeStruct((3, CX, NY, LANES), F32),
            jax.ShapeDtypeStruct((6, NB, LANES), F32),
        ),
        in_specs=[vmem] * 8,
        out_specs=(vmem, vmem),
        scratch_shapes=[
            pltpu.VMEM((3, CX + 2, NY, LANES), F32),
            pltpu.VMEM((3, CX + 2, NY, LANES), F32),
            pltpu.VMEM((1, CX + 2, NY, LANES), F32),
            pltpu.VMEM((6, CX, NY, LANES), F32),
            pltpu.VMEM((CX, NY, LANES), F32),
            pltpu.VMEM((3, CX, NY, LANES), F32),
            pltpu.VMEM((3, CX, NY, LANES), F32),
            pltpu.VMEM((2, 3, CX, LANES), F32),
            pltpu.VMEM((2, 3, 2, CX, LANES), F32),
            pltpu.VMEM((CX, LANES), F32),
            pltpu.VMEM((2, CX, LANES), F32),
            pltpu.VMEM((8 * ndev, LANES), F32),
            pltpu.VMEM((LANES, 8 * ndev), F32),
            pltpu.VMEM((8 * ndev, LANES), F32),
            pltpu.VMEM((LANES, 8 * ndev), F32),
            pltpu.VMEM((5, ndev, 8, LANES), F32),
            pltpu.VMEM((5, ndev, 8, LANES), F32),
            pltpu.VMEM((LANES, LANES), F32),
            pltpu.VMEM((LANES, LANES), F32),
            pltpu.VMEM((LANES, LANES), F32),
            pltpu.VMEM((6, 24, LANES), F32),
            pltpu.VMEM((6, 24, LANES), F32),
            pltpu.VMEM((36, 24, LANES), F32),
            pltpu.VMEM((2, 40, LANES), F32),
            pltpu.VMEM((2, 40, LANES), F32),
            pltpu.VMEM((2, 2, 16, LANES), F32),
            pltpu.VMEM((2, 2, 16, LANES), F32),
            dma((2, 3, 2)), dma((2, 3, 2)), dma((2, 3, 2)), dma((2, 3, 2)),
            dma((2,)), dma((2,)), dma((2,)), dma((2,)),
            dma((5,)), dma((5,)),
            dma((2,)), dma((2,)), dma((2, 2)), dma((2, 2)),
        ],
        compiler_params=pltpu.CompilerParams(
            collective_id=0, has_side_effects=True, vmem_limit_bytes=40 * 1024 * 1024),
    )(
        velocity, source, viscosity[None], keys, names,
        shell_load.reshape(6, NB, LANES), shell_state.reshape(6, NB, LANES),
        shell_inverse.reshape(6, 6, NB, LANES),
    )
    return out[0], out[1].reshape(6, NB * LANES)


def solution(mesh):
    in_specs = (
        P(None, "sec", None, "dev"),
        P(None, "sec", None, "dev"),
        P("sec", None, "dev"),
        P("dev", "sec", None),
        P("dev", "sec"),
        P(None, ("sec", "dev")),
        P(None, ("sec", "dev")),
        P(None, None, ("sec", "dev")),
    )
    out_specs = (P(None, "sec", None, "dev"), P(None, ("sec", "dev")))
    return jax.shard_map(body, mesh=mesh, in_specs=in_specs, out_specs=out_specs, check_vma=False)
```

```python
import jax
import jax.numpy as jnp
from jax import lax
from jax.experimental import pallas as pl
from jax.experimental.pallas import tpu as pltpu
from jax.sharding import PartitionSpec as P

SWEEPS = 8
SHELL_SWEEPS = 8
SUBITERS = 2
CX = 16
NY = 64
LANES = 128
NB = 16
ROWS = 3 * CX
MESH = pl.DeviceIdType.MESH
F32 = jnp.float32
HIGHEST = lax.Precision.HIGHEST


def kernel(
    nsec, ndev,
    vel_ref, src_ref, nu_ref, key_ref, tgt_ref, load_ref, state_ref, inv_ref,
    uout_ref, sout_ref,
    UA, UB, NU, CF, CW, SRC, RHS, RW, XR, ZS, ZR, CS, CR,
    NXR, NZS, NZR, NCS, NCR, SXR, EC, ECR, HC, RH,
    S, ST, G, GT, AS, AR, WT, WQ, WX, WXR, WZR, PULL, N2,
    SH, FORCE, INV, IS, IR, HS, HR,
    xs_sem, xr_sem, zs_sem, zr_sem, cs_sem, cr_sem,
    nxs_sem, nxr_sem, nzs_sem, nzr_sem, ncs_sem, ncr_sem, ss_sem, sr_sem, es_sem, er_sem,
    wxs_sem, wxr_sem, wzs_sem, wzr_sem,
    as_sem, ar_sem, is_sem, ir_sem, hs_sem, hr_sem,
):
    sec = lax.axis_index("sec")
    dev = lax.axis_index("dev")
    has = {("x", 0): sec > 0, ("x", 1): sec < nsec - 1, ("z", 0): dev > 0, ("z", 1): dev < ndev - 1}
    lane = lax.broadcasted_iota(jnp.int32, (8, LANES), 1)
    sub = lax.broadcasted_iota(jnp.int32, (8, LANES), 0)

    def target(axis, side):
        step = 1 if side else -1
        return {"sec": sec + step} if axis == "x" else {"dev": dev + step}

    def remote(src, dst, send_sem, recv_sem, device):
        return pltpu.make_async_remote_copy(
            src_ref=src, dst_ref=dst, send_sem=send_sem, recv_sem=recv_sem,
            device_id=device, device_id_type=MESH)

    def u_copy(p, c, side):
        return remote(UA.at[c, pl.ds((CX - 2) * side, 2)], XR.at[p, c, 1 - side],
                      xs_sem.at[p, c, side], xr_sem.at[p, c, 1 - side], target("x", side))

    def z_copy(p, c, side):
        return remote(ZS.at[p, c], ZR.at[p, c, 1 - side],
                      zs_sem.at[p, c, side], zr_sem.at[p, c, 1 - side], target("z", side))

    def corner(a, b):
        return {"sec": sec + 2 * a - 1, "dev": dev + 2 * b - 1}

    def c_copy(p, c, a, b):
        return remote(CS.at[p, c, a], CR.at[p, c, 1 - a, 1 - b],
                      cs_sem.at[p, c, a, b], cr_sem.at[p, c, 1 - a, 1 - b], corner(a, b))

    def nu_copy(side):
        return remote(NU.at[0, pl.ds((CX - 2) * side, 2)], NXR.at[1 - side],
                      nxs_sem.at[side], nxr_sem.at[1 - side], target("x", side))

    def nz_copy(side):
        return remote(NZS, NZR.at[1 - side], nzs_sem.at[side], nzr_sem.at[1 - side], target("z", side))

    def nc_copy(a, b):
        return remote(NCS.at[a], NCR.at[1 - a, 1 - b],
                      ncs_sem.at[a, b], ncr_sem.at[1 - a, 1 - b], corner(a, b))

    def src_copy(side):
        return remote(SRC.at[:, (CX - 1) * side], SXR.at[1 - side],
                      ss_sem.at[side], sr_sem.at[1 - side], target("x", side))

    def edge_copy(side):
        return remote(EC, ECR.at[1 - side], es_sem.at[side], er_sem.at[1 - side], target("z", side))

    def wall_x_copy(k, side):
        return remote(WX.at[k], WXR.at[k, 1 - side],
                      wxs_sem.at[k, side], wxr_sem.at[k, 1 - side], target("x", side))

    def wall_z_copy(k, side):
        return remote(WQ.at[k], WZR.at[k, 1 - side],
                      wzs_sem.at[k, side], wzr_sem.at[k, 1 - side], target("z", side))

    def inv_copy(side):
        return pltpu.make_async_remote_copy(
            src_ref=IS.at[side], dst_ref=IR.at[1 - side],
            send_sem=is_sem.at[side], recv_sem=ir_sem.at[1 - side],
            device_id=target("z", side), device_id_type=MESH)

    def end_copy(k, side):
        return pltpu.make_async_remote_copy(
            src_ref=HS.at[k, side], dst_ref=HR.at[k, 1 - side],
            send_sem=hs_sem.at[k, side], recv_sem=hr_sem.at[k, 1 - side],
            device_id=target("z", side), device_id_type=MESH)

    def both(axis, act):
        for side in (0, 1):
            @pl.when(has[(axis, side)])
            def _():
                act(side)

    def corners(act):
        for a in (0, 1):
            for b in (0, 1):
                @pl.when(has[("x", a)] & has[("z", b)])
                def _():
                    act(a, b)

    def exchange_start(phase):
        def send(i, carry):
            peer = lax.rem(dev + i, ndev)
            pltpu.make_async_remote_copy(
                src_ref=AS.at[phase, peer], dst_ref=AR.at[phase, dev],
                send_sem=as_sem.at[phase], recv_sem=ar_sem.at[phase],
                device_id={"dev": peer}, device_id_type=MESH).start()
            return carry

        lax.fori_loop(1, ndev, send, 0)
        AR[phase, dev] = AS[phase, dev]

    def exchange_wait(phase):
        copy = pltpu.make_async_remote_copy(
            src_ref=AS.at[phase, pl.ds(0, ndev - 1)], dst_ref=AR.at[phase, pl.ds(0, ndev - 1)],
            send_sem=as_sem.at[phase], recv_sem=ar_sem.at[phase],
            device_id={"dev": lax.rem(dev + 1, ndev)}, device_id_type=MESH)
        copy.wait_send()
        copy.wait_recv()

    def dot(a, b):
        return lax.dot_general(a, b, (((1,), (0,)), ((), ())), precision=HIGHEST, preferred_element_type=F32)

    def tall(rows):
        return jnp.concatenate([rows, jnp.zeros((LANES - ROWS, LANES), F32)], axis=0)

    half = lane < LANES // 2
    half16 = lax.broadcasted_iota(jnp.int32, (CX, LANES), 1) < LANES // 2

    def turn(first, second):
        top = [jnp.where(half, first[n], pltpu.roll(second[n], LANES // 2, 1)) for n in range(8)]
        low = [jnp.where(half, pltpu.roll(first[n], LANES // 2, 1), second[n]) for n in range(8)]
        return jnp.concatenate(top + low, axis=0).T

    def spread(ref, c, x, rows):
        for m in range(8):
            ref[c, x, pl.ds(m, 8, stride=8), :] = rows[8 * m : 8 * m + 8]

    def face_rows(ref, c, low, high):
        return jnp.where(half16, ref[c, pl.ds(0, CX), low, :], ref[c, pl.ds(0, CX), high, :])

    def outer(before, after):
        part = lax.broadcasted_iota(jnp.int32, before.shape, 1) < LANES // 2
        return jnp.where(part, pltpu.roll(before, LANES // 2, 1), pltpu.roll(after, LANES // 2, 1))

    def z_first(row, tile):
        t = pltpu.roll(tile, 1, 0)
        return jnp.where(sub == 0, jnp.where(half, row, pltpu.roll(t, LANES // 2, 1)), t)

    def z_last(row, tile):
        t = pltpu.roll(tile, 7, 0)
        return jnp.where(sub == 7, jnp.where(half, pltpu.roll(t, LANES // 2, 1), row), t)

    for ref in (XR, ZR, CR, NXR, NZR, NCR, SXR, ECR, WXR, WZR, CS, NCS):
        ref[...] = jnp.zeros(ref.shape, F32)
    IR[...] = jnp.zeros(IR.shape, F32)
    IS[...] = jnp.zeros(IS.shape, F32)
    HR[...] = jnp.zeros(HR.shape, F32)
    HS[...] = jnp.zeros(HS.shape, F32)

    barrier = pltpu.get_barrier_semaphore()

    def greet(i, carry):
        pl.semaphore_signal(barrier, inc=1, device_id={"dev": lax.rem(dev + i, ndev)}, device_id_type=MESH)
        return carry

    lax.fori_loop(1, ndev, greet, 0)
    both("x", lambda side: pl.semaphore_signal(barrier, inc=1, device_id=target("x", side), device_id_type=MESH))
    corners(lambda a, b: pl.semaphore_signal(barrier, inc=1, device_id=corner(a, b), device_id_type=MESH))

    def take(refs):
        def step(i, carry):
            for ref, c, out, d, shift in refs:
                first = [ref[c, 2 * i, pl.ds(8 * n, 8), :] for n in range(8)]
                second = [ref[c, 2 * i + 1, pl.ds(8 * n, 8), :] for n in range(8)]
                rows = turn(first, second)
                spread(out, d, 2 * i + shift, rows[:NY])
                spread(out, d, 2 * i + 1 + shift, rows[NY:])
            return carry

        lax.fori_loop(0, CX // 2, step, 0)

    take([(nu_ref, 0, NU, 0, 0)] + [(vel_ref, c, UA, c, 0) for c in range(3)])

    def send_corner(ref, rows):
        ref[0, pl.ds(0, 1), :] = rows[0:1]
        ref[1, pl.ds(0, 1), :] = rows[CX - 1 : CX]

    NZS[...] = face_rows(NU, 0, 0, NY - 1)
    send_corner(NCS, NZS[...])
    for c in range(3):
        ZS[0, c, pl.ds(0, CX), :] = face_rows(UA, c, 0, NY - 1)
        ZS[0, c, pl.ds(CX, CX), :] = face_rows(UA, c, 8, NY - 9)
        send_corner(CS.at[0, c], ZS[0, c, pl.ds(0, CX), :])
    wet = nu_ref[0, :, 0, :]
    N2[...] = 2.0 * tall(jnp.concatenate([wet, wet, wet], axis=0)).T
    rows256 = lax.broadcasted_iota(jnp.int32, (8 * ndev, LANES), 0)
    one_hot = jnp.where(rows256 == key_ref[...], 1.0, 0.0).astype(F32)
    S[...] = one_hot
    ST[...] = one_hot.T
    rows128 = lax.broadcasted_iota(jnp.int32, (LANES, LANES), 0)
    names = jnp.where(rows128 == tgt_ref[...], 1.0, 0.0).astype(F32)
    AS[0] = dot(one_hot, names.T).reshape(ndev, 8, LANES)
    for a in range(6):
        IS[0, pl.ds(6 * a, 6), :] = inv_ref[a, :, 0, :]
        IS[1, pl.ds(6 * a, 6), :] = inv_ref[a, :, NB - 1, :]

    sides_x = jnp.where(has[("x", 0)], 1, 0) + jnp.where(has[("x", 1)], 1, 0)
    sides_z = jnp.where(has[("z", 0)], 1, 0) + jnp.where(has[("z", 1)], 1, 0)
    pl.semaphore_wait(barrier, (ndev - 1) + sides_x + sides_x * sides_z)

    both("x", lambda side: nu_copy(side).start())
    both("z", lambda side: nz_copy(side).start())
    corners(lambda a, b: nc_copy(a, b).start())
    exchange_start(0)
    for c in range(3):
        both("x", lambda side: u_copy(0, c, side).start())
        both("z", lambda side: z_copy(0, c, side).start())
        corners(lambda a, b: c_copy(0, c, a, b).start())
    both("z", lambda side: inv_copy(side).start())
    take([(src_ref, c, SRC, c, 0) for c in range(3)])
    both("x", lambda side: src_copy(side).start())

    SH[...] = jnp.zeros(SH.shape, F32)
    FORCE[...] = jnp.zeros(FORCE.shape, F32)
    for f in range(6):
        SH[f, pl.ds(0, NB), :] = state_ref[f]

    def ends(right, left):
        return jnp.where(sub == 0, right, jnp.where(sub == 7, left, 0.0))

    exchange_wait(0)
    got = AR[0].reshape(8 * ndev, LANES)
    G[...] = got
    GT[...] = got.T

    def send_wall(k):
        rows = jnp.concatenate([SH[f, pl.ds(0, NB), :] for f in range(3)], axis=0)
        AS[1 + k] = dot(G[...], tall(rows)).reshape(ndev, 8, LANES)
        exchange_start(1 + k)

    def take_wall(k):
        exchange_wait(1 + k)
        wall = dot(ST[...], AR[1 + k].reshape(8 * ndev, LANES))
        WQ[k] = wall[:ROWS]
        both("z", lambda side: wall_z_copy(k, side).start())
        WT[...] = wall.T
        for j in range(8):
            WX[k, pl.ds(8 * j, 8), :] = jnp.where(
                half,
                WT[pl.ds(j, 8, stride=8), :],
                pltpu.roll(WT[pl.ds(NY + j, 8, stride=8), :], LANES // 2, 1))
        both("x", lambda side: wall_x_copy(k, side).start())
        tiles = [WX[k, pl.ds(8 * j, 8), :] for j in range(8)]
        for c in range(3):
            for x in range(CX):
                add_wall(c, x, c * CX + x, tiles)

    def add_wall(c, x, q, tiles):
        for j in range(8):
            rows = pl.ds(8 * j, 8)
            wall = pltpu.roll(tiles[j], LANES - q, 1) if q else tiles[j]
            RW[c, x + 1, rows, :] = RHS[c, x + 1, rows, :] + CW[x + 1, rows, :] * wall

    def take_wall_halo(k):
        both("z", lambda side: wall_z_copy(k, side).wait_send())
        both("z", lambda side: wall_z_copy(k, 1 - side).wait_recv())
        both("x", lambda side: wall_x_copy(k, side).wait_send())
        both("x", lambda side: wall_x_copy(k, 1 - side).wait_recv())
        for c in range(3):
            rows = pl.ds(CX * c, CX)
            wall = jnp.where(half16, pltpu.roll(WZR[k, 0, rows, :], 1, 1), pltpu.roll(WZR[k, 1, rows, :], LANES // 2, 1))
            RH[c] = HC[7 + c] + HC[6] * wall
        for side, x, own in ((0, -1, CX - 1), (1, CX, 0)):
            tiles = [WXR[k, side, pl.ds(8 * j, 8), :] for j in range(8)]
            for c in range(3):
                add_wall(c, x, c * CX + own, tiles)

    send_wall(0)

    both("x", lambda side: nu_copy(side).wait_send())
    both("x", lambda side: nu_copy(1 - side).wait_recv())
    both("z", lambda side: nz_copy(side).wait_send())
    both("z", lambda side: nz_copy(1 - side).wait_recv())
    corners(lambda a, b: nc_copy(a, b).wait_send())
    corners(lambda a, b: nc_copy(1 - a, 1 - b).wait_recv())
    both("x", lambda side: src_copy(side).wait_send())
    both("x", lambda side: src_copy(1 - side).wait_recv())
    y_first = lane % NY == 0
    y_last = lane % NY == NY - 1
    nu_rows = outer(NZR[0], NZR[1])

    def halo_planes(ref, c, near):
        def get(x, j):
            rows = pl.ds(8 * j, 8)
            if x < 0:
                return near(0, x + 2, rows)
            if x >= CX:
                return near(1, x - CX, rows)
            return ref[c, x, rows, :]
        return get

    get_nu = halo_planes(NU, 0, lambda side, n, rows: NXR[side, n, rows, :])

    def coefficients(x, row, valid):
        tiles = [get_nu(x, j) for j in range(8)]
        for j in range(8):
            rows = pl.ds(8 * j, 8)
            t = tiles[j]
            zm = tiles[j - 1] if j else z_first(row, tiles[7])
            zp = tiles[j + 1] if j < 7 else z_last(row, tiles[0])
            ym = jnp.where(y_first, t, pltpu.roll(t, 1, 1))
            yp = jnp.where(y_last, t, pltpu.roll(t, LANES - 1, 1))
            faces = [0.5 * (t + o) for o in (get_nu(x - 1, j), get_nu(x + 1, j), zm, zp, ym, yp)]
            total = 1.0 + faces[0]
            for f in faces[1:]:
                total = total + f
            inverse = valid / total
            for n in range(4):
                CF[n, x + 1, rows, :] = faces[n] * inverse
            below = faces[4] * inverse
            CW[x + 1, rows, :] = jnp.where(y_first, below, 0.0)
            CF[4, x + 1, rows, :] = jnp.where(y_first, 0.0, below)
            CF[5, x + 1, rows, :] = jnp.where(y_last, 0.0, faces[5] * inverse)
            for c in range(3):
                if x < 0:
                    base = SXR[0, c, rows, :]
                elif x >= CX:
                    base = SXR[1, c, rows, :]
                else:
                    base = SRC[c, x, rows, :]
                RHS[c, x + 1, rows, :] = base * inverse

    for x in range(CX):
        coefficients(x, nu_rows[x : x + 1], 1.0)

    def edge_rows(ref, n, m):
        return jnp.where(half16, ref[n, pl.ds(1, CX), 0, :], ref[m, pl.ds(1, CX), NY - 1, :])

    for i, (n, m) in enumerate(((0, 0), (1, 1), (3, 2), (2, 3), (4, 4), (5, 5))):
        EC[i] = edge_rows(CF, n, m)
    EC[6] = jnp.where(half16, CW[pl.ds(1, CX), 0, :], CW[pl.ds(1, CX), NY - 1, :])
    for c in range(3):
        EC[7 + c] = edge_rows(RHS, c, c)
    both("z", lambda side: edge_copy(side).start())

    one_row = lax.broadcasted_iota(jnp.int32, (1, LANES), 1) < LANES // 2
    for side, x in ((0, -1), (1, CX)):
        row = outer(NCR[side, 0, pl.ds(0, 8), :], NCR[side, 1, pl.ds(0, 8), :])[0:1]
        coefficients(x, row, jnp.where(has[("x", side)], 1.0, 0.0))

    def take_edges():
        both("z", lambda side: edge_copy(side).wait_send())
        both("z", lambda side: edge_copy(1 - side).wait_recv())
        for i in range(10):
            HC[i] = outer(ECR[0, i], ECR[1, i])

    both("z", lambda side: inv_copy(side).wait_send())
    both("z", lambda side: inv_copy(1 - side).wait_recv())
    for a in range(6):
        for b in range(6):
            n = 6 * a + b
            INV[n, pl.ds(0, NB), :] = inv_ref[a, b]
            INV[n, pl.ds(NB, 8), :] = ends(IR[1, pl.ds(n, 1), :], IR[0, pl.ds(n, 1), :])

    def plane(c, x, get, put, row):
        tiles = [get(x, j) for j in range(8)]
        for j in range(8):
            rows = pl.ds(8 * j, 8)
            t = tiles[j]
            zm = tiles[j - 1] if j else z_first(row, tiles[7])
            zp = tiles[j + 1] if j < 7 else z_last(row, tiles[0])
            num = RW[c, x + 1, rows, :] + CF[0, x + 1, rows, :] * get(x - 1, j)
            num = num + CF[1, x + 1, rows, :] * get(x + 1, j)
            num = num + CF[2, x + 1, rows, :] * zm + CF[3, x + 1, rows, :] * zp
            ys = CF[4, x + 1, rows, :] * pltpu.roll(t, 1, 1)
            ys = ys + CF[5, x + 1, rows, :] * pltpu.roll(t, LANES - 1, 1)
            put(x, rows, num + ys)

    sub16 = lax.broadcasted_iota(jnp.int32, (CX, LANES), 0)
    last = SUBITERS * SWEEPS // 2

    def arrive(p, c):
        both("z", lambda side: z_copy(p, c, 1 - side).wait_recv())
        both("x", lambda side: u_copy(p, c, 1 - side).wait_recv())
        corners(lambda a, b: c_copy(p, c, 1 - a, 1 - b).wait_recv())

    def beside(p, c):
        near = outer(ZR[p, c, 0, pl.ds(0, CX), :], ZR[p, c, 1, pl.ds(0, CX), :])
        far = outer(ZR[p, c, 0, pl.ds(CX, CX), :], ZR[p, c, 1, pl.ds(CX, CX), :])
        low = outer(CR[p, c, 0, 0], CR[p, c, 0, 1])[0:1]
        high = outer(CR[p, c, 1, 0], CR[p, c, 1, 1])[0:1]
        return near, far, low, high

    def even(p, c):
        return halo_planes(UA, c, lambda side, n, rows: XR[p, c, side, n, rows, :])

    def odd(c):
        return lambda x, j: UB[c, x + 1, pl.ds(8 * j, 8), :]

    def put_odd(c):
        def put(x, rows, value):
            UB[c, x + 1, rows, :] = value
        return put

    def put_even(c):
        def put(x, rows, value):
            UA[c, x, rows, :] = value
        return put

    def middle(p, c, xs, rows):
        near, far, low, high = rows
        for x in xs:
            row = low if x < 0 else high if x >= CX else near[x : x + 1]
            plane(c, x, even(p, c), put_odd(c), row)

    def middle_rows(p, c, rows):
        near, far, low, high = rows
        before = jnp.where(sub16 == 0, low, pltpu.roll(near, 1, 0))
        after = jnp.where(sub16 == CX - 1, high, pltpu.roll(near, CX - 1, 0))
        total = RH[c] + HC[0] * before + HC[1] * after + HC[2] * far
        total = total + HC[3] * ZS[p, c, pl.ds(0, CX), :]
        return total + HC[4] * pltpu.roll(near, 1, 1) + HC[5] * pltpu.roll(near, LANES - 1, 1)

    def finish(n, p, c, rows, xs):
        near = middle_rows(p, c, rows)

        def final(group):
            for x in group:
                plane(c, x, odd(c), put_even(c), near[x : x + 1])

        both("x", lambda side: u_copy(p, c, side).wait_send())
        corners(lambda a, b: c_copy(p, c, a, b).wait_send())
        both("z", lambda side: z_copy(p, c, side).wait_send())
        final((0, 1, CX - 1, CX - 2))
        edge = [
            jnp.where(one_row, UA[c, x, pl.ds(0, 1), :], UA[c, x, pl.ds(NY - 1, 1), :]) for x in (0, CX - 1)]
        CS[1 - p, c, 0, pl.ds(0, 1), :] = edge[0]
        CS[1 - p, c, 1, pl.ds(0, 1), :] = edge[1]

        @pl.when(n + 1 < last)
        def _():
            both("x", lambda side: u_copy(1 - p, c, side).start())
            corners(lambda a, b: c_copy(1 - p, c, a, b).start())

        middle(p, c, xs, rows)
        final(range(2, CX - 2))
        ZS[1 - p, c, pl.ds(0, CX), :] = face_rows(UA, c, 0, NY - 1)
        ZS[1 - p, c, pl.ds(CX, CX), :] = face_rows(UA, c, 8, NY - 9)

        @pl.when(n + 1 < last)
        def _():
            both("z", lambda side: z_copy(1 - p, c, side).start())

    def first_pair(k):
        n = k * (SWEEPS // 2)
        p = lax.rem(n, 2)

        def start(c, carry):
            arrive(p, c)
            middle(p, c, range(CX), beside(p, c))
            return carry

        lax.fori_loop(0, 3, start, 0)
        take_wall_halo(k)

        def rest(c, carry):
            rows = beside(p, c)
            middle(p, c, (-1, CX), rows)
            finish(n, p, c, rows, ())
            return carry

        lax.fori_loop(0, 3, rest, 0)

    def pair(n, carry):
        p = lax.rem(n, 2)

        def component(c, carry):
            arrive(p, c)
            rows = beside(p, c)
            middle(p, c, (-1, 0, 1, 2, CX, CX - 1, CX - 2, CX - 3), rows)
            finish(n, p, c, rows, range(3, CX - 3))
            return carry

        lax.fori_loop(0, 3, component, 0)
        return carry

    def shell_sweep(step, carry):
        drive = []
        lane24 = lax.broadcasted_iota(jnp.int32, (24, LANES), 1)
        for f in range(6):
            s = SH[f]
            up = pltpu.roll(s, 1, 1)
            before = jnp.where(lane24 == 0, pltpu.roll(up, 1, 0), up)
            down = pltpu.roll(s, LANES - 1, 1)
            after = jnp.where(lane24 == LANES - 1, pltpu.roll(down, 23, 0), down)
            drive.append(FORCE[f] + 0.4 * (before + after))
        for a in range(6):
            total = INV[6 * a] * drive[0]
            for b in range(1, 6):
                total = total + INV[6 * a + b] * drive[b]
            SH[a] = total
        return carry

    def subiteration(k, carry):
        take_wall(k)
        first_pair(k)
        lax.fori_loop(k * (SWEEPS // 2) + 1, (k + 1) * (SWEEPS // 2), pair, 0)
        tiles = [jnp.zeros((8, LANES), F32) for j in range(8)]
        for q in range(ROWS):
            here = (lane == q) | (lane == q + NY)
            for j in range(8):
                tile = UA[q // CX, q % CX, pl.ds(8 * j, 8), :]
                tiles[j] = jnp.where(here, pltpu.roll(tile, q, 1) if q else tile, tiles[j])
        for j in range(8):
            PULL[pl.ds(j, 8, stride=8), :] = jnp.where(half, tiles[j], 0.0)
            PULL[pl.ds(NY + j, 8, stride=8), :] = jnp.where(half, pltpu.roll(tiles[j], LANES // 2, 1), 0.0)
        pulls = N2[...] * (PULL[...] - WT[...])
        AS[3 + k] = dot(S[...], pulls.T).reshape(ndev, 8, LANES)
        exchange_start(3 + k)
        exchange_wait(3 + k)
        added = dot(GT[...], AR[3 + k].reshape(8 * ndev, LANES))
        for f in range(6):
            force = load_ref[f]
            if f < 3:
                force = force + added[NB * f : NB * (f + 1)]
            FORCE[f, pl.ds(0, NB), :] = force
            HS[k, 0, pl.ds(f, 1), :] = force[0:1]
            HS[k, 1, pl.ds(f, 1), :] = force[NB - 1 : NB]
            HS[k, 0, pl.ds(8 + f, 1), :] = SH[f, pl.ds(0, 1), :]
            HS[k, 1, pl.ds(8 + f, 1), :] = SH[f, pl.ds(NB - 1, 1), :]
        both("z", lambda side: end_copy(k, side).start())
        both("z", lambda side: end_copy(k, side).wait_send())
        both("z", lambda side: end_copy(k, 1 - side).wait_recv())
        for f in range(6):
            FORCE[f, pl.ds(NB, 8), :] = ends(HR[k, 1, pl.ds(f, 1), :], HR[k, 0, pl.ds(f, 1), :])
            SH[f, pl.ds(NB, 8), :] = ends(HR[k, 1, pl.ds(8 + f, 1), :], HR[k, 0, pl.ds(8 + f, 1), :])
        lax.fori_loop(0, SHELL_SWEEPS, shell_sweep, 0)

        @pl.when(k + 1 < SUBITERS)
        def _():
            send_wall(k + 1)
        return carry

    take_edges()
    lax.fori_loop(0, SUBITERS, subiteration, 0)

    for f in range(6):
        sout_ref[f] = SH[f, pl.ds(0, NB), :]

    def give(i, carry):
        for c in range(3):
            rows = jnp.concatenate(
                [UA[c, 2 * i + p, pl.ds(m, 8, stride=8), :] for p in range(2) for m in range(8)], axis=0).T
            for n in range(8):
                top, low = rows[8 * n : 8 * n + 8], rows[NY + 8 * n : NY + 8 * n + 8]
                uout_ref[c, 2 * i, pl.ds(8 * n, 8), :] = jnp.where(half, top, pltpu.roll(low, LANES // 2, 1))
                uout_ref[c, 2 * i + 1, pl.ds(8 * n, 8), :] = jnp.where(half, pltpu.roll(top, LANES // 2, 1), low)
        return carry

    lax.fori_loop(0, CX // 2, give, 0)

def body(velocity, source, viscosity, owners, targets, shell_load, shell_state, shell_inverse):
    nsec = lax.axis_size("sec")
    ndev = lax.axis_size("dev")
    owner = owners.reshape(CX)
    place = jnp.arange(CX, dtype=jnp.int32)
    earlier = (owner[:, None] == owner[None, :]) & (place[:, None] < place[None, :])
    rank = jnp.sum(jnp.where(earlier, 1, 0), axis=0).astype(jnp.int32)
    key = owner * 8 + rank
    keys = jnp.concatenate([key, key + 2, key + 4, jnp.full((LANES - ROWS,), -1, jnp.int32)])[None, :]
    name = targets.reshape(CX)
    names = jnp.concatenate([name, name + NB, name + 2 * NB, jnp.full((LANES - ROWS,), -1, jnp.int32)])[None, :]

    vmem = pl.BlockSpec(memory_space=pltpu.VMEM)
    dma = pltpu.SemaphoreType.DMA
    out = pl.pallas_call(
        lambda *refs: kernel(nsec, ndev, *refs),
        out_shape=(
            jax.ShapeDtypeStruct((3, CX, NY, LANES), F32),
            jax.ShapeDtypeStruct((6, NB, LANES), F32),
        ),
        in_specs=[vmem] * 8,
        out_specs=(vmem, vmem),
        scratch_shapes=[
            pltpu.VMEM((3, CX, NY, LANES), F32),
            pltpu.VMEM((3, CX + 2, NY, LANES), F32),
            pltpu.VMEM((1, CX, NY, LANES), F32),
            pltpu.VMEM((6, CX + 2, NY, LANES), F32),
            pltpu.VMEM((CX + 2, NY, LANES), F32),
            pltpu.VMEM((3, CX, NY, LANES), F32),
            pltpu.VMEM((3, CX + 2, NY, LANES), F32),
            pltpu.VMEM((3, CX + 2, NY, LANES), F32),
            pltpu.VMEM((2, 3, 2, 2, NY, LANES), F32),
            pltpu.VMEM((2, 3, 2 * CX, LANES), F32),
            pltpu.VMEM((2, 3, 2, 2 * CX, LANES), F32),
            pltpu.VMEM((2, 3, 2, 8, LANES), F32),
            pltpu.VMEM((2, 3, 2, 2, 8, LANES), F32),
            pltpu.VMEM((2, 2, NY, LANES), F32),
            pltpu.VMEM((CX, LANES), F32),
            pltpu.VMEM((2, CX, LANES), F32),
            pltpu.VMEM((2, 8, LANES), F32),
            pltpu.VMEM((2, 2, 8, LANES), F32),
            pltpu.VMEM((2, 3, NY, LANES), F32),
            pltpu.VMEM((10, CX, LANES), F32),
            pltpu.VMEM((2, 10, CX, LANES), F32),
            pltpu.VMEM((10, CX, LANES), F32),
            pltpu.VMEM((3, CX, LANES), F32),
            pltpu.VMEM((8 * ndev, LANES), F32),
            pltpu.VMEM((LANES, 8 * ndev), F32),
            pltpu.VMEM((8 * ndev, LANES), F32),
            pltpu.VMEM((LANES, 8 * ndev), F32),
            pltpu.VMEM((5, ndev, 8, LANES), F32),
            pltpu.VMEM((5, ndev, 8, LANES), F32),
            pltpu.VMEM((LANES, LANES), F32),
            pltpu.VMEM((2, ROWS, LANES), F32),
            pltpu.VMEM((2, NY, LANES), F32),
            pltpu.VMEM((2, 2, NY, LANES), F32),
            pltpu.VMEM((2, 2, ROWS, LANES), F32),
            pltpu.VMEM((LANES, LANES), F32),
            pltpu.VMEM((LANES, LANES), F32),
            pltpu.VMEM((6, 24, LANES), F32),
            pltpu.VMEM((6, 24, LANES), F32),
            pltpu.VMEM((36, 24, LANES), F32),
            pltpu.VMEM((2, 40, LANES), F32),
            pltpu.VMEM((2, 40, LANES), F32),
            pltpu.VMEM((2, 2, 16, LANES), F32),
            pltpu.VMEM((2, 2, 16, LANES), F32),
            dma((2, 3, 2)), dma((2, 3, 2)), dma((2, 3, 2)), dma((2, 3, 2)),
            dma((2, 3, 2, 2)), dma((2, 3, 2, 2)),
            dma((2,)), dma((2,)), dma((2,)), dma((2,)), dma((2, 2)), dma((2, 2)),
            dma((2,)), dma((2,)), dma((2,)), dma((2,)),
            dma((2, 2)), dma((2, 2)), dma((2, 2)), dma((2, 2)),
            dma((5,)), dma((5,)),
            dma((2,)), dma((2,)), dma((2, 2)), dma((2, 2)),
        ],
        compiler_params=pltpu.CompilerParams(
            collective_id=0, has_side_effects=True, vmem_limit_bytes=40 * 1024 * 1024),
    )(
        velocity, source, viscosity[None], keys, names,
        shell_load.reshape(6, NB, LANES), shell_state.reshape(6, NB, LANES),
        shell_inverse.reshape(6, 6, NB, LANES),
    )
    return out[0], out[1].reshape(6, NB * LANES)


def solution(mesh):
    in_specs = (
        P(None, "sec", None, "dev"),
        P(None, "sec", None, "dev"),
        P("sec", None, "dev"),
        P("dev", "sec", None),
        P("dev", "sec"),
        P(None, ("sec", "dev")),
        P(None, ("sec", "dev")),
        P(None, None, ("sec", "dev")),
    )
    out_specs = (P(None, "sec", None, "dev"), P(None, ("sec", "dev")))
    return jax.shard_map(body, mesh=mesh, in_specs=in_specs, out_specs=out_specs, check_vma=False)
```

```python
import jax
import jax.numpy as jnp
from jax import lax
from jax.experimental import pallas as pl
from jax.experimental.pallas import tpu as pltpu
from jax.sharding import PartitionSpec as P

SWEEPS = 8
SHELL_SWEEPS = 8
SUBITERS = 2
CX = 16
NY = 64
LANES = 128
NB = 16
ROWS = 3 * CX
MESH = pl.DeviceIdType.MESH
F32 = jnp.float32


def kernel(
    nsec, ndev,
    vel_hbm, src_hbm, nu_hbm, owner_ref, name_ref, load_hbm, state_hbm, inv_hbm,
    uout_ref, sout_ref,
    vel_ref, src_ref, nu_ref, load_ref, state_ref, inv_ref,
    UA, UB, NU, CF, CW, SRC, RHS, RW, XR, ZS, ZR, CS, CR,
    NXR, NZS, NZR, NCS, NCR, SXR, EC, ECR, HC, RH,
    S, ST, G, GT, AS, AR, WT, WQ, WX, WXR, WZR, PULL, N2,
    SH, LOAD, FORCE, INV, IS, IR, HS, HR,
    xs_sem, xr_sem, zs_sem, zr_sem, cs_sem, cr_sem,
    nxs_sem, nxr_sem, nzs_sem, nzr_sem, ncs_sem, ncr_sem, ss_sem, sr_sem, es_sem, er_sem,
    wxs_sem, wxr_sem, wzs_sem, wzr_sem,
    as_sem, ar_sem, is_sem, ir_sem, hs_sem, hr_sem, in_sem,
):
    sec = lax.axis_index("sec")
    dev = lax.axis_index("dev")
    has = {("x", 0): sec > 0, ("x", 1): sec < nsec - 1, ("z", 0): dev > 0, ("z", 1): dev < ndev - 1}
    lane = lax.broadcasted_iota(jnp.int32, (8, LANES), 1)
    sub = lax.broadcasted_iota(jnp.int32, (8, LANES), 0)

    def target(axis, side):
        step = 1 if side else -1
        return {"sec": sec + step} if axis == "x" else {"dev": dev + step}

    def remote(src, dst, send_sem, recv_sem, device):
        return pltpu.make_async_remote_copy(
            src_ref=src, dst_ref=dst, send_sem=send_sem, recv_sem=recv_sem,
            device_id=device, device_id_type=MESH)

    def u_copy(p, c, side):
        return remote(UA.at[c, pl.ds((CX - 2) * side, 2)], XR.at[p, c, 1 - side],
                      xs_sem.at[p, c, side], xr_sem.at[p, c, 1 - side], target("x", side))

    def z_copy(p, c, side):
        return remote(ZS.at[p, c], ZR.at[p, c, 1 - side],
                      zs_sem.at[p, c, side], zr_sem.at[p, c, 1 - side], target("z", side))

    def corner(a, b):
        return {"sec": sec + 2 * a - 1, "dev": dev + 2 * b - 1}

    def c_copy(p, c, a, b):
        return remote(CS.at[p, c, a], CR.at[p, c, 1 - a, 1 - b],
                      cs_sem.at[p, c, a, b], cr_sem.at[p, c, 1 - a, 1 - b], corner(a, b))

    def nu_copy(side):
        return remote(NU.at[0, pl.ds((CX - 2) * side, 2)], NXR.at[1 - side],
                      nxs_sem.at[side], nxr_sem.at[1 - side], target("x", side))

    def nz_copy(side):
        return remote(NZS, NZR.at[1 - side], nzs_sem.at[side], nzr_sem.at[1 - side], target("z", side))

    def nc_copy(a, b):
        return remote(NCS.at[a], NCR.at[1 - a, 1 - b],
                      ncs_sem.at[a, b], ncr_sem.at[1 - a, 1 - b], corner(a, b))

    def src_copy(side):
        return remote(SRC.at[:, (CX - 1) * side], SXR.at[1 - side],
                      ss_sem.at[side], sr_sem.at[1 - side], target("x", side))

    def edge_copy(side):
        return remote(EC, ECR.at[1 - side], es_sem.at[side], er_sem.at[1 - side], target("z", side))

    def wall_x_copy(k, side):
        return remote(WX.at[k], WXR.at[k, 1 - side],
                      wxs_sem.at[k, side], wxr_sem.at[k, 1 - side], target("x", side))

    def wall_z_copy(k, side):
        return remote(WQ.at[k], WZR.at[k, 1 - side],
                      wzs_sem.at[k, side], wzr_sem.at[k, 1 - side], target("z", side))

    def inv_copy(side):
        return pltpu.make_async_remote_copy(
            src_ref=IS.at[side], dst_ref=IR.at[1 - side],
            send_sem=is_sem.at[side], recv_sem=ir_sem.at[1 - side],
            device_id=target("z", side), device_id_type=MESH)

    def end_copy(k, side):
        return pltpu.make_async_remote_copy(
            src_ref=HS.at[k, side], dst_ref=HR.at[k, 1 - side],
            send_sem=hs_sem.at[k, side], recv_sem=hr_sem.at[k, 1 - side],
            device_id=target("z", side), device_id_type=MESH)

    def both(axis, act):
        for side in (0, 1):
            @pl.when(has[(axis, side)])
            def _():
                act(side)

    def corners(act):
        for a in (0, 1):
            for b in (0, 1):
                @pl.when(has[("x", a)] & has[("z", b)])
                def _():
                    act(a, b)

    def exchange_start(phase):
        def send(i, carry):
            peer = lax.rem(dev + i, ndev)
            pltpu.make_async_remote_copy(
                src_ref=AS.at[phase, peer], dst_ref=AR.at[phase, dev],
                send_sem=as_sem.at[phase], recv_sem=ar_sem.at[phase],
                device_id={"dev": peer}, device_id_type=MESH).start()
            return carry

        lax.fori_loop(1, ndev, send, 0)
        AR[phase, dev] = AS[phase, dev]

    def exchange_wait(phase):
        copy = pltpu.make_async_remote_copy(
            src_ref=AS.at[phase, pl.ds(0, ndev - 1)], dst_ref=AR.at[phase, pl.ds(0, ndev - 1)],
            send_sem=as_sem.at[phase], recv_sem=ar_sem.at[phase],
            device_id={"dev": lax.rem(dev + 1, ndev)}, device_id_type=MESH)
        copy.wait_send()
        copy.wait_recv()

    def pick(one_hot, b):
        high = b.astype(jnp.bfloat16)
        rest = b - high.astype(F32)
        middle = rest.astype(jnp.bfloat16)
        low = (rest - middle.astype(F32)).astype(jnp.bfloat16)
        parts = jnp.concatenate([high, middle, low], axis=1)
        out = lax.dot_general(one_hot, parts, (((1,), (0,)), ((), ())), preferred_element_type=F32)
        return (out[:, :LANES] + out[:, LANES : 2 * LANES]) + out[:, 2 * LANES :]

    def tall(rows):
        return jnp.concatenate([rows, jnp.zeros((LANES - ROWS, LANES), F32)], axis=0)

    half = lane < LANES // 2
    half16 = lax.broadcasted_iota(jnp.int32, (CX, LANES), 1) < LANES // 2

    def turn(first, second):
        top = [jnp.where(half, first[n], pltpu.roll(second[n], LANES // 2, 1)) for n in range(8)]
        low = [jnp.where(half, pltpu.roll(first[n], LANES // 2, 1), second[n]) for n in range(8)]
        return jnp.concatenate(top + low, axis=0).T

    def spread(ref, c, x, rows):
        for m in range(8):
            ref[c, x, pl.ds(m, 8, stride=8), :] = rows[8 * m : 8 * m + 8]

    def face_rows(ref, c, low, high):
        return jnp.where(half16, ref[c, pl.ds(0, CX), low, :], ref[c, pl.ds(0, CX), high, :])

    def outer(before, after):
        part = lax.broadcasted_iota(jnp.int32, before.shape, 1) < LANES // 2
        return jnp.where(part, pltpu.roll(before, LANES // 2, 1), pltpu.roll(after, LANES // 2, 1))

    def z_first(row, tile):
        t = pltpu.roll(tile, 1, 0)
        return jnp.where(sub == 0, jnp.where(half, row, pltpu.roll(t, LANES // 2, 1)), t)

    def z_last(row, tile):
        t = pltpu.roll(tile, 7, 0)
        return jnp.where(sub == 7, jnp.where(half, pltpu.roll(t, LANES // 2, 1), row), t)

    loads = [
        pltpu.make_async_copy(src, dst, in_sem.at[n])
        for n, (src, dst) in enumerate((
            (state_hbm, state_ref), (nu_hbm, nu_ref), (vel_hbm, vel_ref),
            (src_hbm, src_ref), (inv_hbm, inv_ref), (load_hbm, load_ref)))]
    for copy in loads:
        copy.start()

    for ref in (XR, ZR, CR, NXR, NZR, NCR, SXR, ECR, WXR, WZR, CS, NCS):
        ref[...] = jnp.zeros(ref.shape, F32)
    IR[...] = jnp.zeros(IR.shape, F32)
    IS[...] = jnp.zeros(IS.shape, F32)
    HR[...] = jnp.zeros(HR.shape, F32)
    HS[...] = jnp.zeros(HS.shape, F32)

    barrier = pltpu.get_barrier_semaphore()

    def greet(i, carry):
        pl.semaphore_signal(barrier, inc=1, device_id={"dev": lax.rem(dev + i, ndev)}, device_id_type=MESH)
        return carry

    lax.fori_loop(1, ndev, greet, 0)
    both("x", lambda side: pl.semaphore_signal(barrier, inc=1, device_id=target("x", side), device_id_type=MESH))
    corners(lambda a, b: pl.semaphore_signal(barrier, inc=1, device_id=corner(a, b), device_id_type=MESH))

    place16 = lax.broadcasted_iota(jnp.int32, (CX, CX), 0)
    other16 = lax.broadcasted_iota(jnp.int32, (CX, CX), 1)

    def column(row):
        return jnp.sum(jnp.where(place16 == other16, jnp.broadcast_to(row, (CX, CX)), 0.0), axis=1, keepdims=True)

    owner_row = owner_ref[...].astype(F32)
    owner = column(owner_row)
    name = column(name_ref[...].astype(F32))
    same = (owner == owner_row) & (other16 < place16)
    rank = jnp.sum(jnp.where(same, 1.0, 0.0), axis=1, keepdims=True)
    slots = lax.broadcasted_iota(jnp.int32, (CX, 8 * ndev), 1).astype(F32)
    blocks = lax.broadcasted_iota(jnp.int32, (CX, LANES), 1).astype(F32)
    key = 8.0 * owner + rank
    one_hot = jnp.concatenate(
        [jnp.where(slots == key + 2.0 * c, 1.0, 0.0) for c in range(3)]
        + [jnp.zeros((LANES - ROWS, 8 * ndev), F32)], axis=0)
    names = tall(jnp.concatenate(
        [jnp.where(blocks == name + float(NB * c), 1.0, 0.0) for c in range(3)], axis=0))
    ST[...] = one_hot.astype(jnp.bfloat16)
    S[...] = one_hot.T.astype(jnp.bfloat16)
    AS[0] = lax.dot_general(
        S[...], names.astype(jnp.bfloat16), (((1,), (0,)), ((), ())), preferred_element_type=F32
    ).reshape(ndev, 8, LANES)

    sides_x = jnp.where(has[("x", 0)], 1, 0) + jnp.where(has[("x", 1)], 1, 0)
    sides_z = jnp.where(has[("z", 0)], 1, 0) + jnp.where(has[("z", 1)], 1, 0)
    pl.semaphore_wait(barrier, (ndev - 1) + sides_x + sides_x * sides_z)
    exchange_start(0)

    def take(refs):
        def step(i, carry):
            for ref, c, out, d in refs:
                first = [ref[c, 2 * i, pl.ds(8 * n, 8), :] for n in range(8)]
                second = [ref[c, 2 * i + 1, pl.ds(8 * n, 8), :] for n in range(8)]
                rows = turn(first, second)
                spread(out, d, 2 * i, rows[:NY])
                spread(out, d, 2 * i + 1, rows[NY:])
            return carry

        lax.fori_loop(0, CX // 2, step, 0)

    def send_corner(ref, rows):
        ref[0, pl.ds(0, 1), :] = rows[0:1]
        ref[1, pl.ds(0, 1), :] = rows[CX - 1 : CX]

    loads[1].wait()
    take([(nu_ref, 0, NU, 0)])
    NZS[...] = face_rows(NU, 0, 0, NY - 1)
    send_corner(NCS, NZS[...])
    corners(lambda a, b: nc_copy(a, b).start())
    both("z", lambda side: nz_copy(side).start())
    both("x", lambda side: nu_copy(side).start())
    wet = nu_ref[0, :, 0, :]
    N2[...] = 2.0 * tall(jnp.concatenate([wet, wet, wet], axis=0)).T

    loads[2].wait()
    take([(vel_ref, c, UA, c) for c in range(3)])
    for c in range(3):
        ZS[0, c, pl.ds(0, CX), :] = face_rows(UA, c, 0, NY - 1)
        ZS[0, c, pl.ds(CX, CX), :] = face_rows(UA, c, 8, NY - 9)
        send_corner(CS.at[0, c], ZS[0, c, pl.ds(0, CX), :])
        corners(lambda a, b: c_copy(0, c, a, b).start())
        both("z", lambda side: z_copy(0, c, side).start())
        both("x", lambda side: u_copy(0, c, side).start())

    loads[0].wait()
    SH[...] = jnp.zeros(SH.shape, F32)
    FORCE[...] = jnp.zeros(FORCE.shape, F32)
    for n in range(NB):
        SH[:, n, :] = state_ref[:, pl.ds(LANES * n, LANES)]

    def ends(right, left):
        return jnp.where(sub == 0, right, jnp.where(sub == 7, left, 0.0))

    exchange_wait(0)
    got = AR[0].reshape(8 * ndev, LANES)
    G[...] = got.astype(jnp.bfloat16)
    GT[...] = got.T.astype(jnp.bfloat16)

    def send_wall(k):
        rows = jnp.concatenate([SH[f, pl.ds(0, NB), :] for f in range(3)], axis=0)
        AS[1 + k] = pick(G[...], tall(rows)).reshape(ndev, 8, LANES)
        exchange_start(1 + k)

    def take_wall(k):
        exchange_wait(1 + k)
        wall = pick(ST[...], AR[1 + k].reshape(8 * ndev, LANES))
        WQ[k] = wall[:ROWS]
        both("z", lambda side: wall_z_copy(k, side).start())
        WT[...] = wall.T
        for j in range(8):
            WX[k, pl.ds(8 * j, 8), :] = jnp.where(
                half,
                WT[pl.ds(j, 8, stride=8), :],
                pltpu.roll(WT[pl.ds(NY + j, 8, stride=8), :], LANES // 2, 1))
        both("x", lambda side: wall_x_copy(k, side).start())
        tiles = [WX[k, pl.ds(8 * j, 8), :] for j in range(8)]
        for c in range(3):
            for x in range(CX):
                for j, value in enumerate(add_wall(c, x, c * CX + x, tiles)):
                    rows = pl.ds(8 * j, 8)
                    UB[c, x + 1, rows, :] = UB[c, x + 1, rows, :] + value

    def add_wall(c, x, q, tiles):
        values = []
        for j in range(8):
            rows = pl.ds(8 * j, 8)
            wall = pltpu.roll(tiles[j], LANES - q, 1) if q else tiles[j]
            values.append(CW[x + 1, rows, :] * wall)
            RW[c, x + 1, rows, :] = RHS[c, x + 1, rows, :] + values[-1]
        return values

    def take_wall_halo(k):
        both("z", lambda side: wall_z_copy(k, side).wait_send())
        both("z", lambda side: wall_z_copy(k, 1 - side).wait_recv())
        both("x", lambda side: wall_x_copy(k, side).wait_send())
        both("x", lambda side: wall_x_copy(k, 1 - side).wait_recv())
        for c in range(3):
            rows = pl.ds(CX * c, CX)
            wall = jnp.where(half16, pltpu.roll(WZR[k, 0, rows, :], 1, 1), pltpu.roll(WZR[k, 1, rows, :], LANES // 2, 1))
            RH[c] = HC[7 + c] + HC[6] * wall
        for side, x, own in ((0, -1, CX - 1), (1, CX, 0)):
            tiles = [WXR[k, side, pl.ds(8 * j, 8), :] for j in range(8)]
            for c in range(3):
                add_wall(c, x, c * CX + own, tiles)

    send_wall(0)

    loads[3].wait()
    take([(src_ref, c, SRC, c) for c in range(3)])
    both("x", lambda side: src_copy(side).start())
    loads[4].wait()
    for a in range(6):
        IS[0, pl.ds(6 * a, 6), :] = inv_ref[a, :, pl.ds(0, LANES)]
        IS[1, pl.ds(6 * a, 6), :] = inv_ref[a, :, pl.ds(LANES * (NB - 1), LANES)]
    both("z", lambda side: inv_copy(side).start())
    loads[5].wait()

    both("x", lambda side: nu_copy(side).wait_send())
    both("x", lambda side: nu_copy(1 - side).wait_recv())
    both("z", lambda side: nz_copy(side).wait_send())
    both("z", lambda side: nz_copy(1 - side).wait_recv())
    corners(lambda a, b: nc_copy(a, b).wait_send())
    corners(lambda a, b: nc_copy(1 - a, 1 - b).wait_recv())
    y_first = lane % NY == 0
    y_last = lane % NY == NY - 1
    nu_rows = outer(NZR[0], NZR[1])

    def halo_planes(ref, c, near):
        def get(x, j):
            rows = pl.ds(8 * j, 8)
            if x < 0:
                return near(0, x + 2, rows)
            if x >= CX:
                return near(1, x - CX, rows)
            return ref[c, x, rows, :]
        return get

    get_nu = halo_planes(NU, 0, lambda side, n, rows: NXR[side, n, rows, :])

    def coefficients(x, row, valid):
        tiles = [get_nu(x, j) for j in range(8)]
        for j in range(8):
            rows = pl.ds(8 * j, 8)
            t = tiles[j]
            zm = tiles[j - 1] if j else z_first(row, tiles[7])
            zp = tiles[j + 1] if j < 7 else z_last(row, tiles[0])
            ym = jnp.where(y_first, t, pltpu.roll(t, 1, 1))
            yp = jnp.where(y_last, t, pltpu.roll(t, LANES - 1, 1))
            faces = [0.5 * (t + o) for o in (get_nu(x - 1, j), get_nu(x + 1, j), zm, zp, ym, yp)]
            total = 1.0 + faces[0]
            for f in faces[1:]:
                total = total + f
            inverse = valid / total
            for n in range(4):
                CF[n, x + 1, rows, :] = faces[n] * inverse
            below = faces[4] * inverse
            CW[x + 1, rows, :] = jnp.where(y_first, below, 0.0)
            CF[4, x + 1, rows, :] = jnp.where(y_first, 0.0, below)
            CF[5, x + 1, rows, :] = jnp.where(y_last, 0.0, faces[5] * inverse)
            for c in range(3):
                if x < 0:
                    base = SXR[0, c, rows, :]
                elif x >= CX:
                    base = SXR[1, c, rows, :]
                else:
                    base = SRC[c, x, rows, :]
                RHS[c, x + 1, rows, :] = base * inverse

    for x in range(CX):
        coefficients(x, nu_rows[x : x + 1], 1.0)

    def edge_rows(ref, n, m):
        return jnp.where(half16, ref[n, pl.ds(1, CX), 0, :], ref[m, pl.ds(1, CX), NY - 1, :])

    for i, (n, m) in enumerate(((0, 0), (1, 1), (3, 2), (2, 3), (4, 4), (5, 5))):
        EC[i] = edge_rows(CF, n, m)
    EC[6] = jnp.where(half16, CW[pl.ds(1, CX), 0, :], CW[pl.ds(1, CX), NY - 1, :])
    for c in range(3):
        EC[7 + c] = edge_rows(RHS, c, c)
    both("z", lambda side: edge_copy(side).start())

    both("x", lambda side: src_copy(side).wait_send())
    both("x", lambda side: src_copy(1 - side).wait_recv())
    one_row = lax.broadcasted_iota(jnp.int32, (1, LANES), 1) < LANES // 2
    for side, x in ((0, -1), (1, CX)):
        row = outer(NCR[side, 0, pl.ds(0, 8), :], NCR[side, 1, pl.ds(0, 8), :])[0:1]
        coefficients(x, row, jnp.where(has[("x", side)], 1.0, 0.0))

    def take_edges():
        both("z", lambda side: edge_copy(side).wait_send())
        both("z", lambda side: edge_copy(1 - side).wait_recv())
        for i in range(10):
            HC[i] = outer(ECR[0, i], ECR[1, i])

    both("z", lambda side: inv_copy(side).wait_send())
    both("z", lambda side: inv_copy(1 - side).wait_recv())
    for a in range(6):
        for n in range(NB):
            INV[pl.ds(6 * a, 6), n, :] = inv_ref[a, :, pl.ds(LANES * n, LANES)]
    for n in range(36):
        INV[n, pl.ds(NB, 8), :] = ends(IR[1, pl.ds(n, 1), :], IR[0, pl.ds(n, 1), :])

    def plane(c, x, get, put, row, base=RW):
        tiles = [get(x, j) for j in range(8)]
        for j in range(8):
            rows = pl.ds(8 * j, 8)
            t = tiles[j]
            zm = tiles[j - 1] if j else z_first(row, tiles[7])
            zp = tiles[j + 1] if j < 7 else z_last(row, tiles[0])
            num = base[c, x + 1, rows, :] + CF[0, x + 1, rows, :] * get(x - 1, j)
            num = num + CF[1, x + 1, rows, :] * get(x + 1, j)
            num = num + CF[2, x + 1, rows, :] * zm + CF[3, x + 1, rows, :] * zp
            ys = CF[4, x + 1, rows, :] * pltpu.roll(t, 1, 1)
            ys = ys + CF[5, x + 1, rows, :] * pltpu.roll(t, LANES - 1, 1)
            put(x, rows, num + ys)

    sub16 = lax.broadcasted_iota(jnp.int32, (CX, LANES), 0)
    last = SUBITERS * SWEEPS // 2

    def arrive(p, c):
        both("z", lambda side: z_copy(p, c, 1 - side).wait_recv())
        both("x", lambda side: u_copy(p, c, 1 - side).wait_recv())
        corners(lambda a, b: c_copy(p, c, 1 - a, 1 - b).wait_recv())

    def beside(p, c):
        near = outer(ZR[p, c, 0, pl.ds(0, CX), :], ZR[p, c, 1, pl.ds(0, CX), :])
        far = outer(ZR[p, c, 0, pl.ds(CX, CX), :], ZR[p, c, 1, pl.ds(CX, CX), :])
        low = outer(CR[p, c, 0, 0], CR[p, c, 0, 1])[0:1]
        high = outer(CR[p, c, 1, 0], CR[p, c, 1, 1])[0:1]
        return near, far, low, high

    def even(p, c):
        return halo_planes(UA, c, lambda side, n, rows: XR[p, c, side, n, rows, :])

    def odd(c):
        return lambda x, j: UB[c, x + 1, pl.ds(8 * j, 8), :]

    def put_odd(c):
        def put(x, rows, value):
            UB[c, x + 1, rows, :] = value
        return put

    def put_even(c):
        def put(x, rows, value):
            UA[c, x, rows, :] = value
        return put

    def middle(p, c, xs, rows, base=RW):
        near, far, low, high = rows
        for x in xs:
            row = low if x < 0 else high if x >= CX else near[x : x + 1]
            plane(c, x, even(p, c), put_odd(c), row, base)

    def middle_rows(p, c, rows):
        near, far, low, high = rows
        before = jnp.where(sub16 == 0, low, pltpu.roll(near, 1, 0))
        after = jnp.where(sub16 == CX - 1, high, pltpu.roll(near, CX - 1, 0))
        total = RH[c] + HC[0] * before + HC[1] * after + HC[2] * far
        total = total + HC[3] * ZS[p, c, pl.ds(0, CX), :]
        return total + HC[4] * pltpu.roll(near, 1, 1) + HC[5] * pltpu.roll(near, LANES - 1, 1)

    def finish(n, p, c, rows, xs):
        near = middle_rows(p, c, rows)

        def final(group):
            for x in group:
                plane(c, x, odd(c), put_even(c), near[x : x + 1])

        both("x", lambda side: u_copy(p, c, side).wait_send())
        corners(lambda a, b: c_copy(p, c, a, b).wait_send())
        both("z", lambda side: z_copy(p, c, side).wait_send())
        final((0, CX - 1))
        edge = [
            jnp.where(one_row, UA[c, x, pl.ds(0, 1), :], UA[c, x, pl.ds(NY - 1, 1), :]) for x in (0, CX - 1)]
        CS[1 - p, c, 0, pl.ds(0, 1), :] = edge[0]
        CS[1 - p, c, 1, pl.ds(0, 1), :] = edge[1]

        @pl.when(n + 1 < last)
        def _():
            corners(lambda a, b: c_copy(1 - p, c, a, b).start())

        final((1, CX - 2))

        @pl.when(n + 1 < last)
        def _():
            both("x", lambda side: u_copy(1 - p, c, side).start())

        middle(p, c, xs, rows)
        final(range(2, CX - 2))
        ZS[1 - p, c, pl.ds(0, CX), :] = face_rows(UA, c, 0, NY - 1)
        ZS[1 - p, c, pl.ds(CX, CX), :] = face_rows(UA, c, 8, NY - 9)

        @pl.when(n + 1 < last)
        def _():
            both("z", lambda side: z_copy(1 - p, c, side).start())

    def early(k):
        p = lax.rem(k * (SWEEPS // 2), 2)

        def start(c, carry):
            arrive(p, c)
            middle(p, c, range(CX), beside(p, c), RHS)
            return carry

        lax.fori_loop(0, 3, start, 0)

    def first_pair(k):
        n = k * (SWEEPS // 2)
        p = lax.rem(n, 2)

        def rest(c, carry):
            rows = beside(p, c)
            middle(p, c, (-1, CX), rows)
            finish(n, p, c, rows, ())
            return carry

        lax.fori_loop(0, 3, rest, 0)

    def pair(n, carry):
        p = lax.rem(n, 2)

        def component(c, carry):
            arrive(p, c)
            rows = beside(p, c)
            middle(p, c, (-1, 0, 1, 2, CX, CX - 1, CX - 2, CX - 3), rows)
            finish(n, p, c, rows, range(3, CX - 3))
            return carry

        lax.fori_loop(0, 3, component, 0)
        return carry

    def shell_sweep(step, carry):
        drive = []
        lane24 = lax.broadcasted_iota(jnp.int32, (24, LANES), 1)
        for f in range(6):
            s = SH[f]
            up = pltpu.roll(s, 1, 1)
            before = jnp.where(lane24 == 0, pltpu.roll(up, 1, 0), up)
            down = pltpu.roll(s, LANES - 1, 1)
            after = jnp.where(lane24 == LANES - 1, pltpu.roll(down, 23, 0), down)
            drive.append(FORCE[f] + 0.4 * (before + after))
        for a in range(6):
            total = INV[6 * a] * drive[0]
            for b in range(1, 6):
                total = total + INV[6 * a + b] * drive[b]
            SH[a] = total
        return carry

    def give(i, carry):
        for c in range(3):
            rows = jnp.concatenate(
                [UA[c, 2 * i + p, pl.ds(m, 8, stride=8), :] for p in range(2) for m in range(8)], axis=0).T
            for n in range(8):
                top, low = rows[8 * n : 8 * n + 8], rows[NY + 8 * n : NY + 8 * n + 8]
                uout_ref[c, 2 * i, pl.ds(8 * n, 8), :] = jnp.where(half, top, pltpu.roll(low, LANES // 2, 1))
                uout_ref[c, 2 * i + 1, pl.ds(8 * n, 8), :] = jnp.where(half, pltpu.roll(top, LANES // 2, 1), low)
        return carry

    def subiteration(k, carry):
        take_wall(k)
        take_wall_halo(k)
        first_pair(k)
        lax.fori_loop(k * (SWEEPS // 2) + 1, (k + 1) * (SWEEPS // 2), pair, 0)
        tiles = [jnp.zeros((8, LANES), F32) for j in range(8)]
        for q in range(ROWS):
            here = (lane == q) | (lane == q + NY)
            for j in range(8):
                tile = UA[q // CX, q % CX, pl.ds(8 * j, 8), :]
                tiles[j] = jnp.where(here, pltpu.roll(tile, q, 1) if q else tile, tiles[j])
        for j in range(8):
            PULL[pl.ds(j, 8, stride=8), :] = jnp.where(half, tiles[j], 0.0)
            PULL[pl.ds(NY + j, 8, stride=8), :] = jnp.where(half, pltpu.roll(tiles[j], LANES // 2, 1), 0.0)
        pulls = N2[...] * (PULL[...] - WT[...])
        AS[3 + k] = pick(S[...], pulls.T).reshape(ndev, 8, LANES)
        exchange_start(3 + k)

        @pl.when(k + 1 < SUBITERS)
        def _():
            early(k + 1)

        @pl.when(k + 1 == SUBITERS)
        def _():
            lax.fori_loop(0, CX // 2, give, 0)

        exchange_wait(3 + k)
        added = pick(GT[...], AR[3 + k].reshape(8 * ndev, LANES))
        for f in range(6):
            force = LOAD[f]
            if f < 3:
                force = force + added[NB * f : NB * (f + 1)]
            FORCE[f, pl.ds(0, NB), :] = force
            HS[k, 0, pl.ds(f, 1), :] = force[0:1]
            HS[k, 1, pl.ds(f, 1), :] = force[NB - 1 : NB]
            HS[k, 0, pl.ds(8 + f, 1), :] = SH[f, pl.ds(0, 1), :]
            HS[k, 1, pl.ds(8 + f, 1), :] = SH[f, pl.ds(NB - 1, 1), :]
        both("z", lambda side: end_copy(k, side).start())
        both("z", lambda side: end_copy(k, side).wait_send())
        both("z", lambda side: end_copy(k, 1 - side).wait_recv())
        for f in range(6):
            FORCE[f, pl.ds(NB, 8), :] = ends(HR[k, 1, pl.ds(f, 1), :], HR[k, 0, pl.ds(f, 1), :])
            SH[f, pl.ds(NB, 8), :] = ends(HR[k, 1, pl.ds(8 + f, 1), :], HR[k, 0, pl.ds(8 + f, 1), :])
        lax.fori_loop(0, SHELL_SWEEPS, shell_sweep, 0)

        @pl.when(k + 1 < SUBITERS)
        def _():
            send_wall(k + 1)
        return carry

    take_edges()
    for n in range(NB):
        LOAD[:, n, :] = load_ref[:, pl.ds(LANES * n, LANES)]
    early(0)
    lax.fori_loop(0, SUBITERS, subiteration, 0)

    for n in range(NB):
        sout_ref[:, pl.ds(LANES * n, LANES)] = SH[:, n, :]


def body(velocity, source, viscosity, owners, targets, shell_load, shell_state, shell_inverse):
    nsec = lax.axis_size("sec")
    ndev = lax.axis_size("dev")
    vmem = pl.BlockSpec(memory_space=pltpu.VMEM)
    hbm = pl.BlockSpec(memory_space=pltpu.HBM)
    bf16 = jnp.bfloat16
    dma = pltpu.SemaphoreType.DMA
    out = pl.pallas_call(
        lambda *refs: kernel(nsec, ndev, *refs),
        out_shape=(
            jax.ShapeDtypeStruct((3, CX, NY, LANES), F32),
            jax.ShapeDtypeStruct((6, NB * LANES), F32),
        ),
        in_specs=[hbm, hbm, hbm, vmem, vmem, hbm, hbm, hbm],
        out_specs=(vmem, vmem),
        scratch_shapes=[
            pltpu.VMEM((3, CX, NY, LANES), F32),
            pltpu.VMEM((3, CX, NY, LANES), F32),
            pltpu.VMEM((1, CX, NY, LANES), F32),
            pltpu.VMEM((6, NB * LANES), F32),
            pltpu.VMEM((6, NB * LANES), F32),
            pltpu.VMEM((6, 6, NB * LANES), F32),
            pltpu.VMEM((3, CX, NY, LANES), F32),
            pltpu.VMEM((3, CX + 2, NY, LANES), F32),
            pltpu.VMEM((1, CX, NY, LANES), F32),
            pltpu.VMEM((6, CX + 2, NY, LANES), F32),
            pltpu.VMEM((CX + 2, NY, LANES), F32),
            pltpu.VMEM((3, CX, NY, LANES), F32),
            pltpu.VMEM((3, CX + 2, NY, LANES), F32),
            pltpu.VMEM((3, CX + 2, NY, LANES), F32),
            pltpu.VMEM((2, 3, 2, 2, NY, LANES), F32),
            pltpu.VMEM((2, 3, 2 * CX, LANES), F32),
            pltpu.VMEM((2, 3, 2, 2 * CX, LANES), F32),
            pltpu.VMEM((2, 3, 2, 8, LANES), F32),
            pltpu.VMEM((2, 3, 2, 2, 8, LANES), F32),
            pltpu.VMEM((2, 2, NY, LANES), F32),
            pltpu.VMEM((CX, LANES), F32),
            pltpu.VMEM((2, CX, LANES), F32),
            pltpu.VMEM((2, 8, LANES), F32),
            pltpu.VMEM((2, 2, 8, LANES), F32),
            pltpu.VMEM((2, 3, NY, LANES), F32),
            pltpu.VMEM((10, CX, LANES), F32),
            pltpu.VMEM((2, 10, CX, LANES), F32),
            pltpu.VMEM((10, CX, LANES), F32),
            pltpu.VMEM((3, CX, LANES), F32),
            pltpu.VMEM((8 * ndev, LANES), bf16),
            pltpu.VMEM((LANES, 8 * ndev), bf16),
            pltpu.VMEM((8 * ndev, LANES), bf16),
            pltpu.VMEM((LANES, 8 * ndev), bf16),
            pltpu.VMEM((5, ndev, 8, LANES), F32),
            pltpu.VMEM((5, ndev, 8, LANES), F32),
            pltpu.VMEM((LANES, LANES), F32),
            pltpu.VMEM((2, ROWS, LANES), F32),
            pltpu.VMEM((2, NY, LANES), F32),
            pltpu.VMEM((2, 2, NY, LANES), F32),
            pltpu.VMEM((2, 2, ROWS, LANES), F32),
            pltpu.VMEM((LANES, LANES), F32),
            pltpu.VMEM((LANES, LANES), F32),
            pltpu.VMEM((6, 24, LANES), F32),
            pltpu.VMEM((6, NB, LANES), F32),
            pltpu.VMEM((6, 24, LANES), F32),
            pltpu.VMEM((36, 24, LANES), F32),
            pltpu.VMEM((2, 40, LANES), F32),
            pltpu.VMEM((2, 40, LANES), F32),
            pltpu.VMEM((2, 2, 16, LANES), F32),
            pltpu.VMEM((2, 2, 16, LANES), F32),
            dma((2, 3, 2)), dma((2, 3, 2)), dma((2, 3, 2)), dma((2, 3, 2)),
            dma((2, 3, 2, 2)), dma((2, 3, 2, 2)),
            dma((2,)), dma((2,)), dma((2,)), dma((2,)), dma((2, 2)), dma((2, 2)),
            dma((2,)), dma((2,)), dma((2,)), dma((2,)),
            dma((2, 2)), dma((2, 2)), dma((2, 2)), dma((2, 2)),
            dma((5,)), dma((5,)),
            dma((2,)), dma((2,)), dma((2, 2)), dma((2, 2)), dma((6,)),
        ],
        compiler_params=pltpu.CompilerParams(
            collective_id=0, has_side_effects=True, vmem_limit_bytes=40 * 1024 * 1024),
    )(
        velocity, source, viscosity[None], owners.reshape(1, CX), targets,
        shell_load, shell_state, shell_inverse,
    )
    return tuple(out)


def solution(mesh):
    in_specs = (
        P(None, "sec", None, "dev"),
        P(None, "sec", None, "dev"),
        P("sec", None, "dev"),
        P("dev", "sec", None),
        P("dev", "sec"),
        P(None, ("sec", "dev")),
        P(None, ("sec", "dev")),
        P(None, None, ("sec", "dev")),
    )
    out_specs = (P(None, "sec", None, "dev"), P(None, ("sec", "dev")))
    return jax.shard_map(body, mesh=mesh, in_specs=in_specs, out_specs=out_specs, check_vma=False)
```

```python
import jax
import jax.numpy as jnp
from jax import lax
from jax.experimental import pallas as pl
from jax.experimental.pallas import tpu as pltpu
from jax.sharding import PartitionSpec as P

SWEEPS = 8
SHELL_SWEEPS = 8
SUBITERS = 2
CX = 16
NY = 64
LANES = 128
NB = 16
ROWS = 3 * CX
MESH = pl.DeviceIdType.MESH
F32 = jnp.float32


def kernel(
    nsec, ndev,
    vel_hbm, src_hbm, nu_hbm, owner_ref, name_ref, load_hbm, state_hbm, inv_hbm,
    uout_hbm, sout_ref,
    vel_ref, src_ref, nu_ref, load_ref, state_ref, inv_ref,
    UA, UB, NU, CF, CW, SRC, RHS, RW, XR, ZS, ZR, CS, CR,
    NXR, NZS, NZR, NCS, NCR, SXR, EC, ECR, HC, RH,
    S, ST, G, GT, AS, AR, WT, WQ, WX, WXR, WZR, PULL, N2,
    SH, LOAD, FORCE, INV, IS, IR, HS, HR,
    xs_sem, xr_sem, zs_sem, zr_sem, cs_sem, cr_sem,
    nxs_sem, nxr_sem, nzs_sem, nzr_sem, ncs_sem, ncr_sem, ss_sem, sr_sem, es_sem, er_sem,
    wxs_sem, wxr_sem, wzs_sem, wzr_sem,
    as_sem, ar_sem, is_sem, ir_sem, hs_sem, hr_sem, in_sem,
):
    sec = lax.axis_index("sec")
    dev = lax.axis_index("dev")
    has = {("x", 0): sec > 0, ("x", 1): sec < nsec - 1, ("z", 0): dev > 0, ("z", 1): dev < ndev - 1}
    lane = lax.broadcasted_iota(jnp.int32, (8, LANES), 1)
    sub = lax.broadcasted_iota(jnp.int32, (8, LANES), 0)

    def target(axis, side):
        step = 1 if side else -1
        return {"sec": sec + step} if axis == "x" else {"dev": dev + step}

    def remote(src, dst, send_sem, recv_sem, device):
        return pltpu.make_async_remote_copy(
            src_ref=src, dst_ref=dst, send_sem=send_sem, recv_sem=recv_sem,
            device_id=device, device_id_type=MESH)

    def u_copy(p, c, side):
        return remote(UA.at[c, pl.ds((CX - 2) * side, 2)], XR.at[p, c, 1 - side],
                      xs_sem.at[p, c, side], xr_sem.at[p, c, 1 - side], target("x", side))

    def z_copy(p, c, side):
        return remote(ZS.at[p, c], ZR.at[p, c, 1 - side],
                      zs_sem.at[p, c, side], zr_sem.at[p, c, 1 - side], target("z", side))

    def corner(a, b):
        return {"sec": sec + 2 * a - 1, "dev": dev + 2 * b - 1}

    def c_copy(p, c, a, b):
        return remote(CS.at[p, c, a], CR.at[p, c, 1 - a, 1 - b],
                      cs_sem.at[p, c, a, b], cr_sem.at[p, c, 1 - a, 1 - b], corner(a, b))

    def nu_copy(side):
        return remote(NU.at[0, pl.ds((CX - 2) * side, 2)], NXR.at[1 - side],
                      nxs_sem.at[side], nxr_sem.at[1 - side], target("x", side))

    def nz_copy(side):
        return remote(NZS, NZR.at[1 - side], nzs_sem.at[side], nzr_sem.at[1 - side], target("z", side))

    def nc_copy(a, b):
        return remote(NCS.at[a], NCR.at[1 - a, 1 - b],
                      ncs_sem.at[a, b], ncr_sem.at[1 - a, 1 - b], corner(a, b))

    def src_copy(side):
        return remote(SRC.at[:, (CX - 1) * side], SXR.at[1 - side],
                      ss_sem.at[side], sr_sem.at[1 - side], target("x", side))

    def edge_copy(side):
        return remote(EC, ECR.at[1 - side], es_sem.at[side], er_sem.at[1 - side], target("z", side))

    def wall_x_copy(k, side):
        return remote(WX.at[k], WXR.at[k, 1 - side],
                      wxs_sem.at[k, side], wxr_sem.at[k, 1 - side], target("x", side))

    def wall_z_copy(k, side):
        return remote(WQ.at[k], WZR.at[k, 1 - side],
                      wzs_sem.at[k, side], wzr_sem.at[k, 1 - side], target("z", side))

    def inv_copy(side):
        return pltpu.make_async_remote_copy(
            src_ref=IS.at[side], dst_ref=IR.at[1 - side],
            send_sem=is_sem.at[side], recv_sem=ir_sem.at[1 - side],
            device_id=target("z", side), device_id_type=MESH)

    def end_copy(k, side):
        return pltpu.make_async_remote_copy(
            src_ref=HS.at[k, side], dst_ref=HR.at[k, 1 - side],
            send_sem=hs_sem.at[k, side], recv_sem=hr_sem.at[k, 1 - side],
            device_id=target("z", side), device_id_type=MESH)

    def both(axis, act):
        for side in (0, 1):
            @pl.when(has[(axis, side)])
            def _():
                act(side)

    def corners(act):
        for a in (0, 1):
            for b in (0, 1):
                @pl.when(has[("x", a)] & has[("z", b)])
                def _():
                    act(a, b)

    def exchange_start(phase):
        def send(i, carry):
            peer = lax.rem(dev + i, ndev)
            pltpu.make_async_remote_copy(
                src_ref=AS.at[phase, peer], dst_ref=AR.at[phase, dev],
                send_sem=as_sem.at[phase], recv_sem=ar_sem.at[phase],
                device_id={"dev": peer}, device_id_type=MESH).start()
            return carry

        lax.fori_loop(1, ndev, send, 0)
        AR[phase, dev] = AS[phase, dev]

    def exchange_wait(phase):
        copy = pltpu.make_async_remote_copy(
            src_ref=AS.at[phase, pl.ds(0, ndev - 1)], dst_ref=AR.at[phase, pl.ds(0, ndev - 1)],
            send_sem=as_sem.at[phase], recv_sem=ar_sem.at[phase],
            device_id={"dev": lax.rem(dev + 1, ndev)}, device_id_type=MESH)
        copy.wait_send()
        copy.wait_recv()

    def pick(one_hot, b):
        high = b.astype(jnp.bfloat16)
        rest = b - high.astype(F32)
        middle = rest.astype(jnp.bfloat16)
        low = (rest - middle.astype(F32)).astype(jnp.bfloat16)
        parts = jnp.concatenate([high, middle, low], axis=1)
        out = lax.dot_general(one_hot, parts, (((1,), (0,)), ((), ())), preferred_element_type=F32)
        return (out[:, :LANES] + out[:, LANES : 2 * LANES]) + out[:, 2 * LANES :]

    def tall(rows):
        return jnp.concatenate([rows, jnp.zeros((LANES - ROWS, LANES), F32)], axis=0)

    half = lane < LANES // 2
    half16 = lax.broadcasted_iota(jnp.int32, (CX, LANES), 1) < LANES // 2

    def turn(first, second):
        top = [jnp.where(half, first[n], pltpu.roll(second[n], LANES // 2, 1)) for n in range(8)]
        low = [jnp.where(half, pltpu.roll(first[n], LANES // 2, 1), second[n]) for n in range(8)]
        return jnp.concatenate(top + low, axis=0).T

    def spread(ref, c, x, rows):
        for m in range(8):
            ref[c, x, pl.ds(m, 8, stride=8), :] = rows[8 * m : 8 * m + 8]

    def face_rows(ref, c, low, high):
        return jnp.where(half16, ref[c, pl.ds(0, CX), low, :], ref[c, pl.ds(0, CX), high, :])

    def outer(before, after):
        part = lax.broadcasted_iota(jnp.int32, before.shape, 1) < LANES // 2
        return jnp.where(part, pltpu.roll(before, LANES // 2, 1), pltpu.roll(after, LANES // 2, 1))

    def z_first(row, tile):
        t = pltpu.roll(tile, 1, 0)
        return jnp.where(sub == 0, jnp.where(half, row, pltpu.roll(t, LANES // 2, 1)), t)

    def z_last(row, tile):
        t = pltpu.roll(tile, 7, 0)
        return jnp.where(sub == 7, jnp.where(half, pltpu.roll(t, LANES // 2, 1), row), t)

    loads = [
        pltpu.make_async_copy(src, dst, in_sem.at[n])
        for n, (src, dst) in enumerate((
            (state_hbm, state_ref), (nu_hbm, nu_ref), (vel_hbm, vel_ref),
            (src_hbm, src_ref), (inv_hbm, inv_ref), (load_hbm, load_ref)))]
    for copy in loads:
        copy.start()

    for ref in (XR, ZR, CR, NXR, NZR, NCR, SXR, ECR, WXR, WZR, CS, NCS):
        ref[...] = jnp.zeros(ref.shape, F32)
    IR[...] = jnp.zeros(IR.shape, F32)
    IS[...] = jnp.zeros(IS.shape, F32)
    HR[...] = jnp.zeros(HR.shape, F32)
    HS[...] = jnp.zeros(HS.shape, F32)

    barrier = pltpu.get_barrier_semaphore()

    def greet(i, carry):
        pl.semaphore_signal(barrier, inc=1, device_id={"dev": lax.rem(dev + i, ndev)}, device_id_type=MESH)
        return carry

    lax.fori_loop(1, ndev, greet, 0)
    both("x", lambda side: pl.semaphore_signal(barrier, inc=1, device_id=target("x", side), device_id_type=MESH))
    corners(lambda a, b: pl.semaphore_signal(barrier, inc=1, device_id=corner(a, b), device_id_type=MESH))

    place16 = lax.broadcasted_iota(jnp.int32, (CX, CX), 0)
    other16 = lax.broadcasted_iota(jnp.int32, (CX, CX), 1)

    def column(row):
        return jnp.sum(jnp.where(place16 == other16, jnp.broadcast_to(row, (CX, CX)), 0.0), axis=1, keepdims=True)

    owner_row = owner_ref[...].astype(F32)
    owner = column(owner_row)
    name = column(name_ref[...].astype(F32))
    same = (owner == owner_row) & (other16 < place16)
    rank = jnp.sum(jnp.where(same, 1.0, 0.0), axis=1, keepdims=True)
    slots = lax.broadcasted_iota(jnp.int32, (CX, 8 * ndev), 1).astype(F32)
    blocks = lax.broadcasted_iota(jnp.int32, (CX, LANES), 1).astype(F32)
    key = 8.0 * owner + rank
    one_hot = jnp.concatenate(
        [jnp.where(slots == key + 2.0 * c, 1.0, 0.0) for c in range(3)]
        + [jnp.zeros((LANES - ROWS, 8 * ndev), F32)], axis=0)
    names = tall(jnp.concatenate(
        [jnp.where(blocks == name + float(NB * c), 1.0, 0.0) for c in range(3)], axis=0))
    ST[...] = one_hot.astype(jnp.bfloat16)
    S[...] = one_hot.T.astype(jnp.bfloat16)
    AS[0] = lax.dot_general(
        S[...], names.astype(jnp.bfloat16), (((1,), (0,)), ((), ())), preferred_element_type=F32
    ).reshape(ndev, 8, LANES)

    sides_x = jnp.where(has[("x", 0)], 1, 0) + jnp.where(has[("x", 1)], 1, 0)
    sides_z = jnp.where(has[("z", 0)], 1, 0) + jnp.where(has[("z", 1)], 1, 0)
    pl.semaphore_wait(barrier, (ndev - 1) + sides_x + sides_x * sides_z)
    exchange_start(0)

    def take(refs):
        def step(i, carry):
            for ref, c, out, d in refs:
                first = [ref[c, 2 * i, pl.ds(8 * n, 8), :] for n in range(8)]
                second = [ref[c, 2 * i + 1, pl.ds(8 * n, 8), :] for n in range(8)]
                rows = turn(first, second)
                spread(out, d, 2 * i, rows[:NY])
                spread(out, d, 2 * i + 1, rows[NY:])
            return carry

        lax.fori_loop(0, CX // 2, step, 0)

    def send_corner(ref, rows):
        ref[0, pl.ds(0, 1), :] = rows[0:1]
        ref[1, pl.ds(0, 1), :] = rows[CX - 1 : CX]

    loads[1].wait()
    take([(nu_ref, 0, NU, 0)])
    NZS[...] = face_rows(NU, 0, 0, NY - 1)
    send_corner(NCS, NZS[...])
    corners(lambda a, b: nc_copy(a, b).start())
    both("z", lambda side: nz_copy(side).start())
    both("x", lambda side: nu_copy(side).start())
    wet = nu_ref[0, :, 0, :]
    N2[...] = 2.0 * tall(jnp.concatenate([wet, wet, wet], axis=0)).T

    loads[2].wait()
    take([(vel_ref, c, UA, c) for c in range(3)])
    for c in range(3):
        ZS[0, c, pl.ds(0, CX), :] = face_rows(UA, c, 0, NY - 1)
        ZS[0, c, pl.ds(CX, CX), :] = face_rows(UA, c, 8, NY - 9)
        send_corner(CS.at[0, c], ZS[0, c, pl.ds(0, CX), :])
        corners(lambda a, b: c_copy(0, c, a, b).start())
        both("z", lambda side: z_copy(0, c, side).start())
        both("x", lambda side: u_copy(0, c, side).start())

    loads[0].wait()
    SH[...] = jnp.zeros(SH.shape, F32)
    FORCE[...] = jnp.zeros(FORCE.shape, F32)
    for n in range(NB):
        SH[:, n, :] = state_ref[:, pl.ds(LANES * n, LANES)]

    def ends(right, left):
        return jnp.where(sub == 0, right, jnp.where(sub == 7, left, 0.0))

    exchange_wait(0)
    got = AR[0].reshape(8 * ndev, LANES)
    G[...] = got.astype(jnp.bfloat16)
    GT[...] = got.T.astype(jnp.bfloat16)

    def send_wall(k):
        rows = jnp.concatenate([SH[f, pl.ds(0, NB), :] for f in range(3)], axis=0)
        AS[1 + k] = pick(G[...], tall(rows)).reshape(ndev, 8, LANES)
        exchange_start(1 + k)

    def take_wall(k):
        exchange_wait(1 + k)
        wall = pick(ST[...], AR[1 + k].reshape(8 * ndev, LANES))
        WQ[k] = wall[:ROWS]
        both("z", lambda side: wall_z_copy(k, side).start())
        WT[...] = wall.T
        for j in range(8):
            WX[k, pl.ds(8 * j, 8), :] = jnp.where(
                half,
                WT[pl.ds(j, 8, stride=8), :],
                pltpu.roll(WT[pl.ds(NY + j, 8, stride=8), :], LANES // 2, 1))
        both("x", lambda side: wall_x_copy(k, side).start())
        tiles = [WX[k, pl.ds(8 * j, 8), :] for j in range(8)]
        for c in range(3):
            for x in range(CX):
                for j, value in enumerate(add_wall(c, x, c * CX + x, tiles)):
                    rows = pl.ds(8 * j, 8)
                    UB[c, x + 1, rows, :] = UB[c, x + 1, rows, :] + value

    def add_wall(c, x, q, tiles):
        values = []
        for j in range(8):
            rows = pl.ds(8 * j, 8)
            wall = pltpu.roll(tiles[j], LANES - q, 1) if q else tiles[j]
            values.append(CW[x + 1, rows, :] * wall)
            RW[c, x + 1, rows, :] = RHS[c, x + 1, rows, :] + values[-1]
        return values

    def take_wall_halo(k):
        both("z", lambda side: wall_z_copy(k, side).wait_send())
        both("z", lambda side: wall_z_copy(k, 1 - side).wait_recv())
        both("x", lambda side: wall_x_copy(k, side).wait_send())
        both("x", lambda side: wall_x_copy(k, 1 - side).wait_recv())
        for c in range(3):
            rows = pl.ds(CX * c, CX)
            wall = jnp.where(half16, pltpu.roll(WZR[k, 0, rows, :], 1, 1), pltpu.roll(WZR[k, 1, rows, :], LANES // 2, 1))
            RH[c] = HC[7 + c] + HC[6] * wall
        for side, x, own in ((0, -1, CX - 1), (1, CX, 0)):
            tiles = [WXR[k, side, pl.ds(8 * j, 8), :] for j in range(8)]
            for c in range(3):
                add_wall(c, x, c * CX + own, tiles)

    send_wall(0)

    loads[3].wait()
    take([(src_ref, c, SRC, c) for c in range(3)])
    both("x", lambda side: src_copy(side).start())
    loads[4].wait()
    for a in range(6):
        IS[0, pl.ds(6 * a, 6), :] = inv_ref[a, :, pl.ds(0, LANES)]
        IS[1, pl.ds(6 * a, 6), :] = inv_ref[a, :, pl.ds(LANES * (NB - 1), LANES)]
    both("z", lambda side: inv_copy(side).start())
    loads[5].wait()

    both("x", lambda side: nu_copy(side).wait_send())
    both("x", lambda side: nu_copy(1 - side).wait_recv())
    both("z", lambda side: nz_copy(side).wait_send())
    both("z", lambda side: nz_copy(1 - side).wait_recv())
    corners(lambda a, b: nc_copy(a, b).wait_send())
    corners(lambda a, b: nc_copy(1 - a, 1 - b).wait_recv())
    y_first = lane % NY == 0
    y_last = lane % NY == NY - 1
    nu_rows = outer(NZR[0], NZR[1])

    def halo_planes(ref, c, near):
        def get(x, j):
            rows = pl.ds(8 * j, 8)
            if x < 0:
                return near(0, x + 2, rows)
            if x >= CX:
                return near(1, x - CX, rows)
            return ref[c, x, rows, :]
        return get

    get_nu = halo_planes(NU, 0, lambda side, n, rows: NXR[side, n, rows, :])

    def coefficients(x, row, valid):
        tiles = [get_nu(x, j) for j in range(8)]
        for j in range(8):
            rows = pl.ds(8 * j, 8)
            t = tiles[j]
            zm = tiles[j - 1] if j else z_first(row, tiles[7])
            zp = tiles[j + 1] if j < 7 else z_last(row, tiles[0])
            ym = jnp.where(y_first, t, pltpu.roll(t, 1, 1))
            yp = jnp.where(y_last, t, pltpu.roll(t, LANES - 1, 1))
            faces = [0.5 * (t + o) for o in (get_nu(x - 1, j), get_nu(x + 1, j), zm, zp, ym, yp)]
            total = 1.0 + faces[0]
            for f in faces[1:]:
                total = total + f
            inverse = valid / total
            for n in range(4):
                CF[n, x + 1, rows, :] = faces[n] * inverse
            below = faces[4] * inverse
            CW[x + 1, rows, :] = jnp.where(y_first, below, 0.0)
            CF[4, x + 1, rows, :] = jnp.where(y_first, 0.0, below)
            CF[5, x + 1, rows, :] = jnp.where(y_last, 0.0, faces[5] * inverse)
            for c in range(3):
                if x < 0:
                    base = SXR[0, c, rows, :]
                elif x >= CX:
                    base = SXR[1, c, rows, :]
                else:
                    base = SRC[c, x, rows, :]
                RHS[c, x + 1, rows, :] = base * inverse

    for x in range(CX):
        coefficients(x, nu_rows[x : x + 1], 1.0)

    def edge_rows(ref, n, m):
        return jnp.where(half16, ref[n, pl.ds(1, CX), 0, :], ref[m, pl.ds(1, CX), NY - 1, :])

    for i, (n, m) in enumerate(((0, 0), (1, 1), (3, 2), (2, 3), (4, 4), (5, 5))):
        EC[i] = edge_rows(CF, n, m)
    EC[6] = jnp.where(half16, CW[pl.ds(1, CX), 0, :], CW[pl.ds(1, CX), NY - 1, :])
    for c in range(3):
        EC[7 + c] = edge_rows(RHS, c, c)
    both("z", lambda side: edge_copy(side).start())

    both("x", lambda side: src_copy(side).wait_send())
    both("x", lambda side: src_copy(1 - side).wait_recv())
    one_row = lax.broadcasted_iota(jnp.int32, (1, LANES), 1) < LANES // 2
    for side, x in ((0, -1), (1, CX)):
        row = outer(NCR[side, 0, pl.ds(0, 8), :], NCR[side, 1, pl.ds(0, 8), :])[0:1]
        coefficients(x, row, jnp.where(has[("x", side)], 1.0, 0.0))

    def take_edges():
        both("z", lambda side: edge_copy(side).wait_send())
        both("z", lambda side: edge_copy(1 - side).wait_recv())
        for i in range(10):
            HC[i] = outer(ECR[0, i], ECR[1, i])

    both("z", lambda side: inv_copy(side).wait_send())
    both("z", lambda side: inv_copy(1 - side).wait_recv())
    for a in range(6):
        for n in range(NB):
            INV[pl.ds(6 * a, 6), n, :] = inv_ref[a, :, pl.ds(LANES * n, LANES)]
    for n in range(36):
        INV[n, pl.ds(NB, 8), :] = ends(IR[1, pl.ds(n, 1), :], IR[0, pl.ds(n, 1), :])

    def plane(c, x, get, put, row, base=RW):
        tiles = [get(x, j) for j in range(8)]
        for j in range(8):
            rows = pl.ds(8 * j, 8)
            t = tiles[j]
            zm = tiles[j - 1] if j else z_first(row, tiles[7])
            zp = tiles[j + 1] if j < 7 else z_last(row, tiles[0])
            num = base[c, x + 1, rows, :] + CF[0, x + 1, rows, :] * get(x - 1, j)
            num = num + CF[1, x + 1, rows, :] * get(x + 1, j)
            num = num + CF[2, x + 1, rows, :] * zm + CF[3, x + 1, rows, :] * zp
            ys = CF[4, x + 1, rows, :] * pltpu.roll(t, 1, 1)
            ys = ys + CF[5, x + 1, rows, :] * pltpu.roll(t, LANES - 1, 1)
            put(x, rows, num + ys)

    sub16 = lax.broadcasted_iota(jnp.int32, (CX, LANES), 0)
    last = SUBITERS * SWEEPS // 2

    def arrive(p, c):
        both("z", lambda side: z_copy(p, c, 1 - side).wait_recv())
        both("x", lambda side: u_copy(p, c, 1 - side).wait_recv())
        corners(lambda a, b: c_copy(p, c, 1 - a, 1 - b).wait_recv())

    def beside(p, c):
        near = outer(ZR[p, c, 0, pl.ds(0, CX), :], ZR[p, c, 1, pl.ds(0, CX), :])
        far = outer(ZR[p, c, 0, pl.ds(CX, CX), :], ZR[p, c, 1, pl.ds(CX, CX), :])
        low = outer(CR[p, c, 0, 0], CR[p, c, 0, 1])[0:1]
        high = outer(CR[p, c, 1, 0], CR[p, c, 1, 1])[0:1]
        return near, far, low, high

    def even(p, c):
        return halo_planes(UA, c, lambda side, n, rows: XR[p, c, side, n, rows, :])

    def odd(c):
        return lambda x, j: UB[c, x + 1, pl.ds(8 * j, 8), :]

    def put_odd(c):
        def put(x, rows, value):
            UB[c, x + 1, rows, :] = value
        return put

    def put_even(c):
        def put(x, rows, value):
            UA[c, x, rows, :] = value
        return put

    def middle(p, c, xs, rows, base=RW):
        near, far, low, high = rows
        for x in xs:
            row = low if x < 0 else high if x >= CX else near[x : x + 1]
            plane(c, x, even(p, c), put_odd(c), row, base)

    def middle_rows(p, c, rows):
        near, far, low, high = rows
        before = jnp.where(sub16 == 0, low, pltpu.roll(near, 1, 0))
        after = jnp.where(sub16 == CX - 1, high, pltpu.roll(near, CX - 1, 0))
        total = RH[c] + HC[0] * before + HC[1] * after + HC[2] * far
        total = total + HC[3] * ZS[p, c, pl.ds(0, CX), :]
        return total + HC[4] * pltpu.roll(near, 1, 1) + HC[5] * pltpu.roll(near, LANES - 1, 1)

    def finish(n, p, c, rows, xs):
        near = middle_rows(p, c, rows)

        def final(group):
            for x in group:
                plane(c, x, odd(c), put_even(c), near[x : x + 1])

        both("x", lambda side: u_copy(p, c, side).wait_send())
        corners(lambda a, b: c_copy(p, c, a, b).wait_send())
        both("z", lambda side: z_copy(p, c, side).wait_send())
        final((0, CX - 1))
        edge = [
            jnp.where(one_row, UA[c, x, pl.ds(0, 1), :], UA[c, x, pl.ds(NY - 1, 1), :]) for x in (0, CX - 1)]
        CS[1 - p, c, 0, pl.ds(0, 1), :] = edge[0]
        CS[1 - p, c, 1, pl.ds(0, 1), :] = edge[1]

        @pl.when(n + 1 < last)
        def _():
            corners(lambda a, b: c_copy(1 - p, c, a, b).start())

        final((1, CX - 2))

        @pl.when(n + 1 < last)
        def _():
            both("x", lambda side: u_copy(1 - p, c, side).start())

        middle(p, c, xs, rows)
        final(range(2, CX - 2))
        ZS[1 - p, c, pl.ds(0, CX), :] = face_rows(UA, c, 0, NY - 1)
        ZS[1 - p, c, pl.ds(CX, CX), :] = face_rows(UA, c, 8, NY - 9)

        @pl.when(n + 1 < last)
        def _():
            both("z", lambda side: z_copy(1 - p, c, side).start())

    def early(k):
        p = lax.rem(k * (SWEEPS // 2), 2)

        def start(c, carry):
            arrive(p, c)
            middle(p, c, range(CX), beside(p, c), RHS)
            return carry

        lax.fori_loop(0, 3, start, 0)

    def first_pair(k):
        n = k * (SWEEPS // 2)
        p = lax.rem(n, 2)

        def rest(c, carry):
            rows = beside(p, c)
            middle(p, c, (-1, CX), rows)
            finish(n, p, c, rows, ())
            return carry

        lax.fori_loop(0, 3, rest, 0)

    def pair(n, carry):
        p = lax.rem(n, 2)

        def component(c, carry):
            arrive(p, c)
            rows = beside(p, c)
            middle(p, c, (-1, 0, 1, 2, CX, CX - 1, CX - 2, CX - 3), rows)
            finish(n, p, c, rows, range(3, CX - 3))
            return carry

        lax.fori_loop(0, 3, component, 0)
        return carry

    def shell_sweep(step, carry):
        drive = []
        lane24 = lax.broadcasted_iota(jnp.int32, (24, LANES), 1)
        for f in range(6):
            s = SH[f]
            up = pltpu.roll(s, 1, 1)
            before = jnp.where(lane24 == 0, pltpu.roll(up, 1, 0), up)
            down = pltpu.roll(s, LANES - 1, 1)
            after = jnp.where(lane24 == LANES - 1, pltpu.roll(down, 23, 0), down)
            drive.append(FORCE[f] + 0.4 * (before + after))
        for a in range(6):
            total = INV[6 * a] * drive[0]
            for b in range(1, 6):
                total = total + INV[6 * a + b] * drive[b]
            SH[a] = total
        return carry

    store = pltpu.make_async_copy(vel_ref, uout_hbm, in_sem.at[2])

    def give(i, carry):
        for c in range(3):
            rows = jnp.concatenate(
                [UA[c, 2 * i + p, pl.ds(m, 8, stride=8), :] for p in range(2) for m in range(8)], axis=0).T
            for n in range(8):
                top, low = rows[8 * n : 8 * n + 8], rows[NY + 8 * n : NY + 8 * n + 8]
                vel_ref[c, 2 * i, pl.ds(8 * n, 8), :] = jnp.where(half, top, pltpu.roll(low, LANES // 2, 1))
                vel_ref[c, 2 * i + 1, pl.ds(8 * n, 8), :] = jnp.where(half, pltpu.roll(top, LANES // 2, 1), low)
        return carry

    def subiteration(k, carry):
        take_wall(k)
        take_wall_halo(k)
        first_pair(k)
        lax.fori_loop(k * (SWEEPS // 2) + 1, (k + 1) * (SWEEPS // 2), pair, 0)
        tiles = [jnp.zeros((8, LANES), F32) for j in range(8)]
        for q in range(ROWS):
            here = (lane == q) | (lane == q + NY)
            for j in range(8):
                tile = UA[q // CX, q % CX, pl.ds(8 * j, 8), :]
                tiles[j] = jnp.where(here, pltpu.roll(tile, q, 1) if q else tile, tiles[j])
        for j in range(8):
            PULL[pl.ds(j, 8, stride=8), :] = jnp.where(half, tiles[j], 0.0)
            PULL[pl.ds(NY + j, 8, stride=8), :] = jnp.where(half, pltpu.roll(tiles[j], LANES // 2, 1), 0.0)
        pulls = N2[...] * (PULL[...] - WT[...])
        AS[3 + k] = pick(S[...], pulls.T).reshape(ndev, 8, LANES)
        exchange_start(3 + k)

        @pl.when(k + 1 < SUBITERS)
        def _():
            early(k + 1)

        @pl.when(k + 1 == SUBITERS)
        def _():
            lax.fori_loop(0, CX // 2, give, 0)
            store.start()

        exchange_wait(3 + k)
        added = pick(GT[...], AR[3 + k].reshape(8 * ndev, LANES))
        for f in range(6):
            force = LOAD[f]
            if f < 3:
                force = force + added[NB * f : NB * (f + 1)]
            FORCE[f, pl.ds(0, NB), :] = force
            HS[k, 0, pl.ds(f, 1), :] = force[0:1]
            HS[k, 1, pl.ds(f, 1), :] = force[NB - 1 : NB]
            HS[k, 0, pl.ds(8 + f, 1), :] = SH[f, pl.ds(0, 1), :]
            HS[k, 1, pl.ds(8 + f, 1), :] = SH[f, pl.ds(NB - 1, 1), :]
        both("z", lambda side: end_copy(k, side).start())
        both("z", lambda side: end_copy(k, side).wait_send())
        both("z", lambda side: end_copy(k, 1 - side).wait_recv())
        for f in range(6):
            FORCE[f, pl.ds(NB, 8), :] = ends(HR[k, 1, pl.ds(f, 1), :], HR[k, 0, pl.ds(f, 1), :])
            SH[f, pl.ds(NB, 8), :] = ends(HR[k, 1, pl.ds(8 + f, 1), :], HR[k, 0, pl.ds(8 + f, 1), :])
        lax.fori_loop(0, SHELL_SWEEPS, shell_sweep, 0)

        @pl.when(k + 1 < SUBITERS)
        def _():
            send_wall(k + 1)
        return carry

    take_edges()
    for n in range(NB):
        LOAD[:, n, :] = load_ref[:, pl.ds(LANES * n, LANES)]
    early(0)
    lax.fori_loop(0, SUBITERS, subiteration, 0)

    for n in range(NB):
        sout_ref[:, pl.ds(LANES * n, LANES)] = SH[:, n, :]
    store.wait()


def body(velocity, source, viscosity, owners, targets, shell_load, shell_state, shell_inverse):
    nsec = lax.axis_size("sec")
    ndev = lax.axis_size("dev")
    vmem = pl.BlockSpec(memory_space=pltpu.VMEM)
    hbm = pl.BlockSpec(memory_space=pltpu.HBM)
    bf16 = jnp.bfloat16
    dma = pltpu.SemaphoreType.DMA
    out = pl.pallas_call(
        lambda *refs: kernel(nsec, ndev, *refs),
        out_shape=(
            jax.ShapeDtypeStruct((3, CX, NY, LANES), F32),
            jax.ShapeDtypeStruct((6, NB * LANES), F32),
        ),
        in_specs=[hbm, hbm, hbm, vmem, vmem, hbm, hbm, hbm],
        out_specs=(hbm, vmem),
        scratch_shapes=[
            pltpu.VMEM((3, CX, NY, LANES), F32),
            pltpu.VMEM((3, CX, NY, LANES), F32),
            pltpu.VMEM((1, CX, NY, LANES), F32),
            pltpu.VMEM((6, NB * LANES), F32),
            pltpu.VMEM((6, NB * LANES), F32),
            pltpu.VMEM((6, 6, NB * LANES), F32),
            pltpu.VMEM((3, CX, NY, LANES), F32),
            pltpu.VMEM((3, CX + 2, NY, LANES), F32),
            pltpu.VMEM((1, CX, NY, LANES), F32),
            pltpu.VMEM((6, CX + 2, NY, LANES), F32),
            pltpu.VMEM((CX + 2, NY, LANES), F32),
            pltpu.VMEM((3, CX, NY, LANES), F32),
            pltpu.VMEM((3, CX + 2, NY, LANES), F32),
            pltpu.VMEM((3, CX + 2, NY, LANES), F32),
            pltpu.VMEM((2, 3, 2, 2, NY, LANES), F32),
            pltpu.VMEM((2, 3, 2 * CX, LANES), F32),
            pltpu.VMEM((2, 3, 2, 2 * CX, LANES), F32),
            pltpu.VMEM((2, 3, 2, 8, LANES), F32),
            pltpu.VMEM((2, 3, 2, 2, 8, LANES), F32),
            pltpu.VMEM((2, 2, NY, LANES), F32),
            pltpu.VMEM((CX, LANES), F32),
            pltpu.VMEM((2, CX, LANES), F32),
            pltpu.VMEM((2, 8, LANES), F32),
            pltpu.VMEM((2, 2, 8, LANES), F32),
            pltpu.VMEM((2, 3, NY, LANES), F32),
            pltpu.VMEM((10, CX, LANES), F32),
            pltpu.VMEM((2, 10, CX, LANES), F32),
            pltpu.VMEM((10, CX, LANES), F32),
            pltpu.VMEM((3, CX, LANES), F32),
            pltpu.VMEM((8 * ndev, LANES), bf16),
            pltpu.VMEM((LANES, 8 * ndev), bf16),
            pltpu.VMEM((8 * ndev, LANES), bf16),
            pltpu.VMEM((LANES, 8 * ndev), bf16),
            pltpu.VMEM((5, ndev, 8, LANES), F32),
            pltpu.VMEM((5, ndev, 8, LANES), F32),
            pltpu.VMEM((LANES, LANES), F32),
            pltpu.VMEM((2, ROWS, LANES), F32),
            pltpu.VMEM((2, NY, LANES), F32),
            pltpu.VMEM((2, 2, NY, LANES), F32),
            pltpu.VMEM((2, 2, ROWS, LANES), F32),
            pltpu.VMEM((LANES, LANES), F32),
            pltpu.VMEM((LANES, LANES), F32),
            pltpu.VMEM((6, 24, LANES), F32),
            pltpu.VMEM((6, NB, LANES), F32),
            pltpu.VMEM((6, 24, LANES), F32),
            pltpu.VMEM((36, 24, LANES), F32),
            pltpu.VMEM((2, 40, LANES), F32),
            pltpu.VMEM((2, 40, LANES), F32),
            pltpu.VMEM((2, 2, 16, LANES), F32),
            pltpu.VMEM((2, 2, 16, LANES), F32),
            dma((2, 3, 2)), dma((2, 3, 2)), dma((2, 3, 2)), dma((2, 3, 2)),
            dma((2, 3, 2, 2)), dma((2, 3, 2, 2)),
            dma((2,)), dma((2,)), dma((2,)), dma((2,)), dma((2, 2)), dma((2, 2)),
            dma((2,)), dma((2,)), dma((2,)), dma((2,)),
            dma((2, 2)), dma((2, 2)), dma((2, 2)), dma((2, 2)),
            dma((5,)), dma((5,)),
            dma((2,)), dma((2,)), dma((2, 2)), dma((2, 2)), dma((6,)),
        ],
        compiler_params=pltpu.CompilerParams(
            collective_id=0, has_side_effects=True, vmem_limit_bytes=60 * 1024 * 1024),
    )(
        velocity, source, viscosity[None], owners.reshape(1, CX), targets,
        shell_load, shell_state, shell_inverse,
    )
    return tuple(out)


def solution(mesh):
    in_specs = (
        P(None, "sec", None, "dev"),
        P(None, "sec", None, "dev"),
        P("sec", None, "dev"),
        P("dev", "sec", None),
        P("dev", "sec"),
        P(None, ("sec", "dev")),
        P(None, ("sec", "dev")),
        P(None, None, ("sec", "dev")),
    )
    out_specs = (P(None, "sec", None, "dev"), P(None, ("sec", "dev")))
    return jax.shard_map(body, mesh=mesh, in_specs=in_specs, out_specs=out_specs, check_vma=False)
```

```python
import jax
import jax.numpy as jnp
from jax import lax
from jax.experimental import pallas as pl
from jax.experimental.pallas import tpu as pltpu
from jax.sharding import PartitionSpec as P

SWEEPS = 8
SHELL_SWEEPS = 8
SUBITERS = 2
CX = 16
NY = 64
LANES = 128
NB = 16
ROWS = 3 * CX
MESH = pl.DeviceIdType.MESH
F32 = jnp.float32


def kernel(
    nsec, ndev,
    vel_hbm, src_hbm, nu_hbm, owner_ref, name_ref, load_hbm, state_hbm, inv_hbm,
    uout_hbm, sout_ref,
    vel_ref, src_ref, nu_ref, load_ref, state_ref, inv_ref,
    UA, UB, NU, CF, CW, SRC, RHS, RW, XR, ZS, ZR, CS, CR,
    NXR, NZS, NZR, NCS, NCR, SXR, EC, ECR, HC, RH,
    S, ST, G, GT, AS, AR, WT, WQ, WX, WXR, WZR, PULL, N2,
    SH, LOAD, FORCE, INV, IS, IR, HS, HR,
    xs_sem, xr_sem, zs_sem, zr_sem, cs_sem, cr_sem,
    nxs_sem, nxr_sem, nzs_sem, nzr_sem, ncs_sem, ncr_sem, ss_sem, sr_sem, es_sem, er_sem,
    wxs_sem, wxr_sem, wzs_sem, wzr_sem,
    as_sem, ar_sem, is_sem, ir_sem, hs_sem, hr_sem, in_sem,
):
    sec = lax.axis_index("sec")
    dev = lax.axis_index("dev")
    has = {("x", 0): sec > 0, ("x", 1): sec < nsec - 1, ("z", 0): dev > 0, ("z", 1): dev < ndev - 1}
    lane = lax.broadcasted_iota(jnp.int32, (8, LANES), 1)
    sub = lax.broadcasted_iota(jnp.int32, (8, LANES), 0)

    def target(axis, side):
        step = 1 if side else -1
        return {"sec": lax.rem(sec + step + nsec, nsec)} if axis == "x" else {"dev": lax.rem(dev + step + ndev, ndev)}

    def remote(src, dst, send_sem, recv_sem, device):
        return pltpu.make_async_remote_copy(
            src_ref=src, dst_ref=dst, send_sem=send_sem, recv_sem=recv_sem,
            device_id=device, device_id_type=MESH)

    def u_copy(p, c, side):
        return remote(UA.at[c, pl.ds((CX - 2) * side, 2)], XR.at[p, c, 1 - side],
                      xs_sem.at[p, c, side], xr_sem.at[p, c, 1 - side], target("x", side))

    def z_copy(p, c, side):
        return remote(ZS.at[p, c], ZR.at[p, c, 1 - side],
                      zs_sem.at[p, c, side], zr_sem.at[p, c, 1 - side], target("z", side))

    def corner(a, b):
        return target("x", a) | target("z", b)

    def c_copy(p, c, a, b):
        return remote(CS.at[p, c, a], CR.at[p, c, 1 - a, 1 - b],
                      cs_sem.at[p, c, a, b], cr_sem.at[p, c, 1 - a, 1 - b], corner(a, b))

    def nu_copy(side):
        return remote(NU.at[0, pl.ds((CX - 2) * side, 2)], NXR.at[1 - side],
                      nxs_sem.at[side], nxr_sem.at[1 - side], target("x", side))

    def nz_copy(side):
        return remote(NZS, NZR.at[1 - side], nzs_sem.at[side], nzr_sem.at[1 - side], target("z", side))

    def nc_copy(a, b):
        return remote(NCS.at[a], NCR.at[1 - a, 1 - b],
                      ncs_sem.at[a, b], ncr_sem.at[1 - a, 1 - b], corner(a, b))

    def src_copy(side):
        return remote(SRC.at[:, (CX - 1) * side], SXR.at[1 - side],
                      ss_sem.at[side], sr_sem.at[1 - side], target("x", side))

    def edge_copy(side):
        return remote(EC, ECR.at[1 - side], es_sem.at[side], er_sem.at[1 - side], target("z", side))

    def wall_x_copy(k, side):
        return remote(WX.at[k], WXR.at[k, 1 - side],
                      wxs_sem.at[k, side], wxr_sem.at[k, 1 - side], target("x", side))

    def wall_z_copy(k, side):
        return remote(WQ.at[k], WZR.at[k, 1 - side],
                      wzs_sem.at[k, side], wzr_sem.at[k, 1 - side], target("z", side))

    def inv_copy(side):
        return pltpu.make_async_remote_copy(
            src_ref=IS.at[side], dst_ref=IR.at[1 - side],
            send_sem=is_sem.at[side], recv_sem=ir_sem.at[1 - side],
            device_id=target("z", side), device_id_type=MESH)

    def end_copy(k, side):
        return pltpu.make_async_remote_copy(
            src_ref=HS.at[k, side], dst_ref=HR.at[k, 1 - side],
            send_sem=hs_sem.at[k, side], recv_sem=hr_sem.at[k, 1 - side],
            device_id=target("z", side), device_id_type=MESH)

    def both(axis, act):
        for side in (0, 1):
            @pl.when(has[(axis, side)])
            def _():
                act(side)

    def sides(act):
        for side in (0, 1):
            act(side)

    def all_corners(act):
        for a in (0, 1):
            for b in (0, 1):
                act(a, b)

    def corners(act):
        for a in (0, 1):
            for b in (0, 1):
                @pl.when(has[("x", a)] & has[("z", b)])
                def _():
                    act(a, b)

    def exchange_start(phase):
        def send(i, carry):
            peer = lax.rem(dev + i, ndev)
            pltpu.make_async_remote_copy(
                src_ref=AS.at[phase, peer], dst_ref=AR.at[phase, dev],
                send_sem=as_sem.at[phase], recv_sem=ar_sem.at[phase],
                device_id={"dev": peer}, device_id_type=MESH).start()
            return carry

        lax.fori_loop(1, ndev, send, 0)
        AR[phase, dev] = AS[phase, dev]

    def exchange_wait(phase):
        copy = pltpu.make_async_remote_copy(
            src_ref=AS.at[phase, pl.ds(0, ndev - 1)], dst_ref=AR.at[phase, pl.ds(0, ndev - 1)],
            send_sem=as_sem.at[phase], recv_sem=ar_sem.at[phase],
            device_id={"dev": lax.rem(dev + 1, ndev)}, device_id_type=MESH)
        copy.wait_send()
        copy.wait_recv()

    def pick(one_hot, b):
        high = b.astype(jnp.bfloat16)
        rest = b - high.astype(F32)
        middle = rest.astype(jnp.bfloat16)
        low = (rest - middle.astype(F32)).astype(jnp.bfloat16)
        parts = jnp.concatenate([high, middle, low], axis=1)
        out = lax.dot_general(one_hot, parts, (((1,), (0,)), ((), ())), preferred_element_type=F32)
        return (out[:, :LANES] + out[:, LANES : 2 * LANES]) + out[:, 2 * LANES :]

    def tall(rows):
        return jnp.concatenate([rows, jnp.zeros((LANES - ROWS, LANES), F32)], axis=0)

    half = lane < LANES // 2
    half16 = lax.broadcasted_iota(jnp.int32, (CX, LANES), 1) < LANES // 2

    def turn(first, second):
        top = [jnp.where(half, first[n], pltpu.roll(second[n], LANES // 2, 1)) for n in range(8)]
        low = [jnp.where(half, pltpu.roll(first[n], LANES // 2, 1), second[n]) for n in range(8)]
        return jnp.concatenate(top + low, axis=0).T

    def spread(ref, c, x, rows):
        for m in range(8):
            ref[c, x, pl.ds(m, 8, stride=8), :] = rows[8 * m : 8 * m + 8]

    def face_rows(ref, c, low, high):
        return jnp.where(half16, ref[c, pl.ds(0, CX), low, :], ref[c, pl.ds(0, CX), high, :])

    def outer(before, after):
        part = lax.broadcasted_iota(jnp.int32, before.shape, 1) < LANES // 2
        return jnp.where(part, pltpu.roll(before, LANES // 2, 1), pltpu.roll(after, LANES // 2, 1))

    def z_first(row, tile):
        t = pltpu.roll(tile, 1, 0)
        return jnp.where(sub == 0, jnp.where(half, row, pltpu.roll(t, LANES // 2, 1)), t)

    def z_last(row, tile):
        t = pltpu.roll(tile, 7, 0)
        return jnp.where(sub == 7, jnp.where(half, pltpu.roll(t, LANES // 2, 1), row), t)

    loads = [
        pltpu.make_async_copy(src, dst, in_sem.at[n])
        for n, (src, dst) in enumerate((
            (state_hbm, state_ref), (nu_hbm, nu_ref), (vel_hbm, vel_ref),
            (src_hbm, src_ref), (inv_hbm, inv_ref), (load_hbm, load_ref)))]
    for copy in loads:
        copy.start()

    for ref in (XR, ZR, CR, NXR, NZR, NCR, SXR, ECR, WXR, WZR, CS, NCS):
        ref[...] = jnp.zeros(ref.shape, F32)
    IR[...] = jnp.zeros(IR.shape, F32)
    IS[...] = jnp.zeros(IS.shape, F32)
    HR[...] = jnp.zeros(HR.shape, F32)
    HS[...] = jnp.zeros(HS.shape, F32)

    barrier = pltpu.get_barrier_semaphore()

    def greet(i, carry):
        pl.semaphore_signal(barrier, inc=1, device_id={"dev": lax.rem(dev + i, ndev)}, device_id_type=MESH)
        return carry

    lax.fori_loop(1, ndev, greet, 0)
    sides(lambda side: pl.semaphore_signal(barrier, inc=1, device_id=target("x", side), device_id_type=MESH))
    all_corners(lambda a, b: pl.semaphore_signal(barrier, inc=1, device_id=corner(a, b), device_id_type=MESH))

    place16 = lax.broadcasted_iota(jnp.int32, (CX, CX), 0)
    other16 = lax.broadcasted_iota(jnp.int32, (CX, CX), 1)

    def column(row):
        return jnp.sum(jnp.where(place16 == other16, jnp.broadcast_to(row, (CX, CX)), 0.0), axis=1, keepdims=True)

    owner_row = owner_ref[...].astype(F32)
    owner = column(owner_row)
    name = column(name_ref[...].astype(F32))
    same = (owner == owner_row) & (other16 < place16)
    rank = jnp.sum(jnp.where(same, 1.0, 0.0), axis=1, keepdims=True)
    slots = lax.broadcasted_iota(jnp.int32, (CX, 8 * ndev), 1).astype(F32)
    blocks = lax.broadcasted_iota(jnp.int32, (CX, LANES), 1).astype(F32)
    key = 8.0 * owner + rank
    one_hot = jnp.concatenate(
        [jnp.where(slots == key + 2.0 * c, 1.0, 0.0) for c in range(3)]
        + [jnp.zeros((LANES - ROWS, 8 * ndev), F32)], axis=0)
    names = tall(jnp.concatenate(
        [jnp.where(blocks == name + float(NB * c), 1.0, 0.0) for c in range(3)], axis=0))
    ST[...] = one_hot.astype(jnp.bfloat16)
    S[...] = one_hot.T.astype(jnp.bfloat16)
    AS[0] = lax.dot_general(
        S[...], names.astype(jnp.bfloat16), (((1,), (0,)), ((), ())), preferred_element_type=F32
    ).reshape(ndev, 8, LANES)


    def take(refs):
        def step(i, carry):
            for ref, c, out, d in refs:
                first = [ref[c, 2 * i, pl.ds(8 * n, 8), :] for n in range(8)]
                second = [ref[c, 2 * i + 1, pl.ds(8 * n, 8), :] for n in range(8)]
                rows = turn(first, second)
                spread(out, d, 2 * i, rows[:NY])
                spread(out, d, 2 * i + 1, rows[NY:])
            return carry

        lax.fori_loop(0, CX // 2, step, 0)

    def send_corner(ref, rows):
        ref[0, pl.ds(0, 1), :] = rows[0:1]
        ref[1, pl.ds(0, 1), :] = rows[CX - 1 : CX]

    loads[1].wait()
    take([(nu_ref, 0, NU, 0)])
    NZS[...] = face_rows(NU, 0, 0, NY - 1)
    send_corner(NCS, NZS[...])

    pl.semaphore_wait(barrier, (ndev - 1) + 6)
    exchange_start(0)
    corners(lambda a, b: nc_copy(a, b).start())
    both("z", lambda side: nz_copy(side).start())
    both("x", lambda side: nu_copy(side).start())
    wet = nu_ref[0, :, 0, :]
    N2[...] = 2.0 * tall(jnp.concatenate([wet, wet, wet], axis=0)).T

    loads[2].wait()
    take([(vel_ref, c, UA, c) for c in range(3)])
    for c in range(3):
        ZS[0, c, pl.ds(0, CX), :] = face_rows(UA, c, 0, NY - 1)
        ZS[0, c, pl.ds(CX, CX), :] = face_rows(UA, c, 8, NY - 9)
        send_corner(CS.at[0, c], ZS[0, c, pl.ds(0, CX), :])
        all_corners(lambda a, b: c_copy(0, c, a, b).start())
        sides(lambda side: z_copy(0, c, side).start())
        sides(lambda side: u_copy(0, c, side).start())

    loads[0].wait()
    SH[...] = jnp.zeros(SH.shape, F32)
    FORCE[...] = jnp.zeros(FORCE.shape, F32)
    for n in range(NB):
        SH[:, n, :] = state_ref[:, pl.ds(LANES * n, LANES)]

    def ends(right, left):
        return jnp.where(sub == 0, right, jnp.where(sub == 7, left, 0.0))

    exchange_wait(0)
    got = AR[0].reshape(8 * ndev, LANES)
    G[...] = got.astype(jnp.bfloat16)
    GT[...] = got.T.astype(jnp.bfloat16)

    def send_wall(k):
        rows = jnp.concatenate([SH[f, pl.ds(0, NB), :] for f in range(3)], axis=0)
        AS[1 + k] = pick(G[...], tall(rows)).reshape(ndev, 8, LANES)
        exchange_start(1 + k)

    def take_wall(k, begun):
        exchange_wait(1 + k)
        wall = pick(ST[...], AR[1 + k].reshape(8 * ndev, LANES))
        WQ[k] = wall[:ROWS]
        both("z", lambda side: wall_z_copy(k, side).start())
        WT[...] = wall.T
        for j in range(8):
            WX[k, pl.ds(8 * j, 8), :] = jnp.where(
                half,
                WT[pl.ds(j, 8, stride=8), :],
                pltpu.roll(WT[pl.ds(NY + j, 8, stride=8), :], LANES // 2, 1))
        both("x", lambda side: wall_x_copy(k, side).start())
        tiles = [WX[k, pl.ds(8 * j, 8), :] for j in range(8)]
        for c in range(3):
            for x in range(CX):
                for j, value in enumerate(add_wall(c, x, c * CX + x, tiles)):
                    rows = pl.ds(8 * j, 8)
                    if begun:
                        UB[c, x + 1, rows, :] = UB[c, x + 1, rows, :] + value

    def add_wall(c, x, q, tiles):
        values = []
        for j in range(8):
            rows = pl.ds(8 * j, 8)
            wall = pltpu.roll(tiles[j], LANES - q, 1) if q else tiles[j]
            values.append(CW[x + 1, rows, :] * wall)
            RW[c, x + 1, rows, :] = RHS[c, x + 1, rows, :] + values[-1]
        return values

    def take_wall_halo(k):
        both("z", lambda side: wall_z_copy(k, side).wait_send())
        both("z", lambda side: wall_z_copy(k, 1 - side).wait_recv())
        both("x", lambda side: wall_x_copy(k, side).wait_send())
        both("x", lambda side: wall_x_copy(k, 1 - side).wait_recv())
        for c in range(3):
            rows = pl.ds(CX * c, CX)
            wall = jnp.where(half16, pltpu.roll(WZR[k, 0, rows, :], 1, 1), pltpu.roll(WZR[k, 1, rows, :], LANES // 2, 1))
            RH[c] = HC[7 + c] + HC[6] * wall
        for side, x, own in ((0, -1, CX - 1), (1, CX, 0)):
            tiles = [WXR[k, side, pl.ds(8 * j, 8), :] for j in range(8)]
            for c in range(3):
                add_wall(c, x, c * CX + own, tiles)

    send_wall(0)

    loads[3].wait()
    take([(src_ref, c, SRC, c) for c in range(3)])
    both("x", lambda side: src_copy(side).start())
    loads[4].wait()
    for a in range(6):
        IS[0, pl.ds(6 * a, 6), :] = inv_ref[a, :, pl.ds(0, LANES)]
        IS[1, pl.ds(6 * a, 6), :] = inv_ref[a, :, pl.ds(LANES * (NB - 1), LANES)]
    both("z", lambda side: inv_copy(side).start())
    loads[5].wait()

    both("x", lambda side: nu_copy(side).wait_send())
    both("x", lambda side: nu_copy(1 - side).wait_recv())
    both("z", lambda side: nz_copy(side).wait_send())
    both("z", lambda side: nz_copy(1 - side).wait_recv())
    corners(lambda a, b: nc_copy(a, b).wait_send())
    corners(lambda a, b: nc_copy(1 - a, 1 - b).wait_recv())
    y_first = lane % NY == 0
    y_last = lane % NY == NY - 1
    nu_rows = outer(NZR[0], NZR[1])
    z_low = jnp.where((sub == 0) & half, jnp.where(has[("z", 0)], 1.0, 0.0), 1.0)
    z_high = jnp.where((sub == 7) & ~half, jnp.where(has[("z", 1)], 1.0, 0.0), 1.0)
    x_low = jnp.where(has[("x", 0)], 1.0, 0.0)
    x_high = jnp.where(has[("x", 1)], 1.0, 0.0)

    def halo_planes(ref, c, near):
        def get(x, j):
            rows = pl.ds(8 * j, 8)
            if x < 0:
                return near(0, x + 2, rows)
            if x >= CX:
                return near(1, x - CX, rows)
            return ref[c, x, rows, :]
        return get

    get_nu = halo_planes(NU, 0, lambda side, n, rows: NXR[side, n, rows, :])

    def coefficients(x, row, valid):
        tiles = [get_nu(x, j) for j in range(8)]
        for j in range(8):
            rows = pl.ds(8 * j, 8)
            t = tiles[j]
            zm = tiles[j - 1] if j else z_first(row, tiles[7])
            zp = tiles[j + 1] if j < 7 else z_last(row, tiles[0])
            ym = jnp.where(y_first, t, pltpu.roll(t, 1, 1))
            yp = jnp.where(y_last, t, pltpu.roll(t, LANES - 1, 1))
            faces = [0.5 * (t + o) for o in (get_nu(x - 1, j), get_nu(x + 1, j), zm, zp, ym, yp)]
            total = 1.0 + faces[0]
            for f in faces[1:]:
                total = total + f
            inverse = valid / total
            ends_at = [x_low if x == 0 else None, x_high if x == CX - 1 else None,
                       z_low if j == 0 else None, z_high if j == 7 else None]
            for n in range(4):
                face = faces[n] * inverse
                CF[n, x + 1, rows, :] = face if ends_at[n] is None else face * ends_at[n]
            below = faces[4] * inverse
            CW[x + 1, rows, :] = jnp.where(y_first, below, 0.0)
            CF[4, x + 1, rows, :] = jnp.where(y_first, 0.0, below)
            CF[5, x + 1, rows, :] = jnp.where(y_last, 0.0, faces[5] * inverse)
            for c in range(3):
                if x < 0:
                    base = SXR[0, c, rows, :]
                elif x >= CX:
                    base = SXR[1, c, rows, :]
                else:
                    base = SRC[c, x, rows, :]
                RHS[c, x + 1, rows, :] = base * inverse

    for x in range(CX):
        coefficients(x, nu_rows[x : x + 1], 1.0)

    def edge_rows(ref, n, m):
        return jnp.where(half16, ref[n, pl.ds(1, CX), 0, :], ref[m, pl.ds(1, CX), NY - 1, :])

    for i, (n, m) in enumerate(((0, 0), (1, 1), (3, 2), (2, 3), (4, 4), (5, 5))):
        EC[i] = edge_rows(CF, n, m)
    EC[6] = jnp.where(half16, CW[pl.ds(1, CX), 0, :], CW[pl.ds(1, CX), NY - 1, :])
    for c in range(3):
        EC[7 + c] = edge_rows(RHS, c, c)
    both("z", lambda side: edge_copy(side).start())

    both("x", lambda side: src_copy(side).wait_send())
    both("x", lambda side: src_copy(1 - side).wait_recv())
    one_row = lax.broadcasted_iota(jnp.int32, (1, LANES), 1) < LANES // 2
    for side, x in ((0, -1), (1, CX)):
        row = outer(NCR[side, 0, pl.ds(0, 8), :], NCR[side, 1, pl.ds(0, 8), :])[0:1]
        coefficients(x, row, jnp.where(has[("x", side)], 1.0, 0.0))

    def take_edges():
        both("z", lambda side: edge_copy(side).wait_send())
        both("z", lambda side: edge_copy(1 - side).wait_recv())
        for i in range(10):
            HC[i] = outer(ECR[0, i], ECR[1, i])

    def plane(c, x, get, put, row, base=RW):
        tiles = [get(x, j) for j in range(8)]
        for j in range(8):
            rows = pl.ds(8 * j, 8)
            t = tiles[j]
            zm = tiles[j - 1] if j else z_first(row, tiles[7])
            zp = tiles[j + 1] if j < 7 else z_last(row, tiles[0])
            num = base[c, x + 1, rows, :] + CF[0, x + 1, rows, :] * get(x - 1, j)
            num = num + CF[1, x + 1, rows, :] * get(x + 1, j)
            num = num + CF[2, x + 1, rows, :] * zm + CF[3, x + 1, rows, :] * zp
            ys = CF[4, x + 1, rows, :] * pltpu.roll(t, 1, 1)
            ys = ys + CF[5, x + 1, rows, :] * pltpu.roll(t, LANES - 1, 1)
            put(x, rows, num + ys)

    sub16 = lax.broadcasted_iota(jnp.int32, (CX, LANES), 0)
    last = SUBITERS * SWEEPS // 2

    def arrive(p, c):
        sides(lambda side: z_copy(p, c, 1 - side).wait_recv())
        sides(lambda side: u_copy(p, c, 1 - side).wait_recv())

    def beside(p, c):
        near = outer(ZR[p, c, 0, pl.ds(0, CX), :], ZR[p, c, 1, pl.ds(0, CX), :])
        far = outer(ZR[p, c, 0, pl.ds(CX, CX), :], ZR[p, c, 1, pl.ds(CX, CX), :])
        return near, far

    def beside_corners(p, c):
        all_corners(lambda a, b: c_copy(p, c, 1 - a, 1 - b).wait_recv())
        low = outer(CR[p, c, 0, 0], CR[p, c, 0, 1])[0:1]
        high = outer(CR[p, c, 1, 0], CR[p, c, 1, 1])[0:1]
        return low, high

    def even(p, c):
        return halo_planes(UA, c, lambda side, n, rows: XR[p, c, side, n, rows, :])

    def odd(c):
        return lambda x, j: UB[c, x + 1, pl.ds(8 * j, 8), :]

    def put_odd(c):
        def put(x, rows, value):
            UB[c, x + 1, rows, :] = value
        return put

    def put_even(c):
        def put(x, rows, value):
            UA[c, x, rows, :] = value
        return put

    def middle(p, c, xs, rows, base=RW):
        for x in xs:
            row = rows[0] if x < 0 else rows[1] if x >= CX else rows[0][x : x + 1]
            plane(c, x, even(p, c), put_odd(c), row, base)

    def middle_rows(p, c, rows, ends_of):
        near, far = rows
        low, high = ends_of
        before = jnp.where(sub16 == 0, low, pltpu.roll(near, 1, 0))
        after = jnp.where(sub16 == CX - 1, high, pltpu.roll(near, CX - 1, 0))
        total = RH[c] + HC[0] * before + HC[1] * after + HC[2] * far
        total = total + HC[3] * ZS[p, c, pl.ds(0, CX), :]
        return total + HC[4] * pltpu.roll(near, 1, 1) + HC[5] * pltpu.roll(near, LANES - 1, 1)

    def finish(n, p, c, rows, ends_of, xs):
        near = middle_rows(p, c, rows, ends_of)

        def final(group):
            for x in group:
                plane(c, x, odd(c), put_even(c), near[x : x + 1])

        sides(lambda side: u_copy(p, c, side).wait_send())
        all_corners(lambda a, b: c_copy(p, c, a, b).wait_send())
        sides(lambda side: z_copy(p, c, side).wait_send())
        final((0, CX - 1))
        edge = [
            jnp.where(one_row, UA[c, x, pl.ds(0, 1), :], UA[c, x, pl.ds(NY - 1, 1), :]) for x in (0, CX - 1)]
        CS[1 - p, c, 0, pl.ds(0, 1), :] = edge[0]
        CS[1 - p, c, 1, pl.ds(0, 1), :] = edge[1]

        @pl.when(n + 1 < last)
        def _():
            all_corners(lambda a, b: c_copy(1 - p, c, a, b).start())

        final((1, CX - 2))

        @pl.when(n + 1 < last)
        def _():
            sides(lambda side: u_copy(1 - p, c, side).start())

        middle(p, c, xs, rows)
        final(range(2, CX - 2))
        ZS[1 - p, c, pl.ds(0, CX), :] = face_rows(UA, c, 0, NY - 1)
        ZS[1 - p, c, pl.ds(CX, CX), :] = face_rows(UA, c, 8, NY - 9)

        @pl.when(n + 1 < last)
        def _():
            sides(lambda side: z_copy(1 - p, c, side).start())

    def early(k, base):
        p = lax.rem(k * (SWEEPS // 2), 2)

        def start(c, carry):
            arrive(p, c)
            middle(p, c, range(CX), beside(p, c), base)
            return carry

        lax.fori_loop(0, 3, start, 0)

    def first_pair(k):
        n = k * (SWEEPS // 2)
        p = lax.rem(n, 2)

        def rest(c, carry):
            ends_of = beside_corners(p, c)
            middle(p, c, (-1, CX), ends_of)
            finish(n, p, c, beside(p, c), ends_of, ())
            return carry

        lax.fori_loop(0, 3, rest, 0)

    def pair(n, carry):
        p = lax.rem(n, 2)

        def component(c, carry):
            arrive(p, c)
            rows = beside(p, c)
            middle(p, c, (0, 1, 2, CX - 1, CX - 2, CX - 3), rows)
            ends_of = beside_corners(p, c)
            middle(p, c, (-1, CX), ends_of)
            finish(n, p, c, rows, ends_of, range(3, CX - 3))
            return carry

        lax.fori_loop(0, 3, component, 0)
        return carry

    def shell_sweep(step, carry):
        drive = []
        lane24 = lax.broadcasted_iota(jnp.int32, (24, LANES), 1)
        for f in range(6):
            s = SH[f]
            up = pltpu.roll(s, 1, 1)
            before = jnp.where(lane24 == 0, pltpu.roll(up, 1, 0), up)
            down = pltpu.roll(s, LANES - 1, 1)
            after = jnp.where(lane24 == LANES - 1, pltpu.roll(down, 23, 0), down)
            drive.append(FORCE[f] + 0.4 * (before + after))
        for a in range(6):
            total = INV[6 * a] * drive[0]
            for b in range(1, 6):
                total = total + INV[6 * a + b] * drive[b]
            SH[a] = total
        return carry

    store = pltpu.make_async_copy(vel_ref, uout_hbm, in_sem.at[2])

    def give(i, carry):
        for c in range(3):
            rows = jnp.concatenate(
                [UA[c, 2 * i + p, pl.ds(m, 8, stride=8), :] for p in range(2) for m in range(8)], axis=0).T
            for n in range(8):
                top, low = rows[8 * n : 8 * n + 8], rows[NY + 8 * n : NY + 8 * n + 8]
                vel_ref[c, 2 * i, pl.ds(8 * n, 8), :] = jnp.where(half, top, pltpu.roll(low, LANES // 2, 1))
                vel_ref[c, 2 * i + 1, pl.ds(8 * n, 8), :] = jnp.where(half, pltpu.roll(top, LANES // 2, 1), low)
        return carry

    def build_shell():
        both("z", lambda side: inv_copy(side).wait_send())
        both("z", lambda side: inv_copy(1 - side).wait_recv())
        for a in range(6):
            for n in range(NB):
                INV[pl.ds(6 * a, 6), n, :] = inv_ref[a, :, pl.ds(LANES * n, LANES)]
        for n in range(36):
            INV[n, pl.ds(NB, 8), :] = ends(IR[1, pl.ds(n, 1), :], IR[0, pl.ds(n, 1), :])
        for n in range(NB):
            LOAD[:, n, :] = load_ref[:, pl.ds(LANES * n, LANES)]

    def subiteration(k, carry):
        @pl.when(k > 0)
        def _():
            take_wall(k, True)

        take_wall_halo(k)
        first_pair(k)
        lax.fori_loop(k * (SWEEPS // 2) + 1, (k + 1) * (SWEEPS // 2), pair, 0)
        tiles = [jnp.zeros((8, LANES), F32) for j in range(8)]
        for q in range(ROWS):
            here = (lane == q) | (lane == q + NY)
            for j in range(8):
                tile = UA[q // CX, q % CX, pl.ds(8 * j, 8), :]
                tiles[j] = jnp.where(here, pltpu.roll(tile, q, 1) if q else tile, tiles[j])
        for j in range(8):
            PULL[pl.ds(j, 8, stride=8), :] = jnp.where(half, tiles[j], 0.0)
            PULL[pl.ds(NY + j, 8, stride=8), :] = jnp.where(half, pltpu.roll(tiles[j], LANES // 2, 1), 0.0)
        pulls = N2[...] * (PULL[...] - WT[...])
        AS[3 + k] = pick(S[...], pulls.T).reshape(ndev, 8, LANES)
        exchange_start(3 + k)

        @pl.when(k + 1 < SUBITERS)
        def _():
            early(k + 1, RHS)
            build_shell()

        @pl.when(k + 1 == SUBITERS)
        def _():
            lax.fori_loop(0, CX // 2, give, 0)
            store.start()

        exchange_wait(3 + k)
        added = pick(GT[...], AR[3 + k].reshape(8 * ndev, LANES))
        for f in range(6):
            force = LOAD[f]
            if f < 3:
                force = force + added[NB * f : NB * (f + 1)]
            FORCE[f, pl.ds(0, NB), :] = force
            HS[k, 0, pl.ds(f, 1), :] = force[0:1]
            HS[k, 1, pl.ds(f, 1), :] = force[NB - 1 : NB]
            HS[k, 0, pl.ds(8 + f, 1), :] = SH[f, pl.ds(0, 1), :]
            HS[k, 1, pl.ds(8 + f, 1), :] = SH[f, pl.ds(NB - 1, 1), :]
        both("z", lambda side: end_copy(k, side).start())
        both("z", lambda side: end_copy(k, side).wait_send())
        both("z", lambda side: end_copy(k, 1 - side).wait_recv())
        for f in range(6):
            FORCE[f, pl.ds(NB, 8), :] = ends(HR[k, 1, pl.ds(f, 1), :], HR[k, 0, pl.ds(f, 1), :])
            SH[f, pl.ds(NB, 8), :] = ends(HR[k, 1, pl.ds(8 + f, 1), :], HR[k, 0, pl.ds(8 + f, 1), :])
        lax.fori_loop(0, SHELL_SWEEPS, shell_sweep, 0)

        @pl.when(k + 1 < SUBITERS)
        def _():
            send_wall(k + 1)
        return carry

    take_wall(0, False)
    early(0, RW)
    take_edges()
    lax.fori_loop(0, SUBITERS, subiteration, 0)

    for n in range(NB):
        sout_ref[:, pl.ds(LANES * n, LANES)] = SH[:, n, :]
    store.wait()


def body(velocity, source, viscosity, owners, targets, shell_load, shell_state, shell_inverse):
    nsec = lax.axis_size("sec")
    ndev = lax.axis_size("dev")
    vmem = pl.BlockSpec(memory_space=pltpu.VMEM)
    hbm = pl.BlockSpec(memory_space=pltpu.HBM)
    bf16 = jnp.bfloat16
    dma = pltpu.SemaphoreType.DMA
    out = pl.pallas_call(
        lambda *refs: kernel(nsec, ndev, *refs),
        out_shape=(
            jax.ShapeDtypeStruct((3, CX, NY, LANES), F32),
            jax.ShapeDtypeStruct((6, NB * LANES), F32),
        ),
        in_specs=[hbm, hbm, hbm, vmem, vmem, hbm, hbm, hbm],
        out_specs=(hbm, vmem),
        scratch_shapes=[
            pltpu.VMEM((3, CX, NY, LANES), F32),
            pltpu.VMEM((3, CX, NY, LANES), F32),
            pltpu.VMEM((1, CX, NY, LANES), F32),
            pltpu.VMEM((6, NB * LANES), F32),
            pltpu.VMEM((6, NB * LANES), F32),
            pltpu.VMEM((6, 6, NB * LANES), F32),
            pltpu.VMEM((3, CX, NY, LANES), F32),
            pltpu.VMEM((3, CX + 2, NY, LANES), F32),
            pltpu.VMEM((1, CX, NY, LANES), F32),
            pltpu.VMEM((6, CX + 2, NY, LANES), F32),
            pltpu.VMEM((CX + 2, NY, LANES), F32),
            pltpu.VMEM((3, CX, NY, LANES), F32),
            pltpu.VMEM((3, CX + 2, NY, LANES), F32),
            pltpu.VMEM((3, CX + 2, NY, LANES), F32),
            pltpu.VMEM((2, 3, 2, 2, NY, LANES), F32),
            pltpu.VMEM((2, 3, 2 * CX, LANES), F32),
            pltpu.VMEM((2, 3, 2, 2 * CX, LANES), F32),
            pltpu.VMEM((2, 3, 2, 8, LANES), F32),
            pltpu.VMEM((2, 3, 2, 2, 8, LANES), F32),
            pltpu.VMEM((2, 2, NY, LANES), F32),
            pltpu.VMEM((CX, LANES), F32),
            pltpu.VMEM((2, CX, LANES), F32),
            pltpu.VMEM((2, 8, LANES), F32),
            pltpu.VMEM((2, 2, 8, LANES), F32),
            pltpu.VMEM((2, 3, NY, LANES), F32),
            pltpu.VMEM((10, CX, LANES), F32),
            pltpu.VMEM((2, 10, CX, LANES), F32),
            pltpu.VMEM((10, CX, LANES), F32),
            pltpu.VMEM((3, CX, LANES), F32),
            pltpu.VMEM((8 * ndev, LANES), bf16),
            pltpu.VMEM((LANES, 8 * ndev), bf16),
            pltpu.VMEM((8 * ndev, LANES), bf16),
            pltpu.VMEM((LANES, 8 * ndev), bf16),
            pltpu.VMEM((5, ndev, 8, LANES), F32),
            pltpu.VMEM((5, ndev, 8, LANES), F32),
            pltpu.VMEM((LANES, LANES), F32),
            pltpu.VMEM((2, ROWS, LANES), F32),
            pltpu.VMEM((2, NY, LANES), F32),
            pltpu.VMEM((2, 2, NY, LANES), F32),
            pltpu.VMEM((2, 2, ROWS, LANES), F32),
            pltpu.VMEM((LANES, LANES), F32),
            pltpu.VMEM((LANES, LANES), F32),
            pltpu.VMEM((6, 24, LANES), F32),
            pltpu.VMEM((6, NB, LANES), F32),
            pltpu.VMEM((6, 24, LANES), F32),
            pltpu.VMEM((36, 24, LANES), F32),
            pltpu.VMEM((2, 40, LANES), F32),
            pltpu.VMEM((2, 40, LANES), F32),
            pltpu.VMEM((2, 2, 16, LANES), F32),
            pltpu.VMEM((2, 2, 16, LANES), F32),
            dma((2, 3, 2)), dma((2, 3, 2)), dma((2, 3, 2)), dma((2, 3, 2)),
            dma((2, 3, 2, 2)), dma((2, 3, 2, 2)),
            dma((2,)), dma((2,)), dma((2,)), dma((2,)), dma((2, 2)), dma((2, 2)),
            dma((2,)), dma((2,)), dma((2,)), dma((2,)),
            dma((2, 2)), dma((2, 2)), dma((2, 2)), dma((2, 2)),
            dma((5,)), dma((5,)),
            dma((2,)), dma((2,)), dma((2, 2)), dma((2, 2)), dma((6,)),
        ],
        compiler_params=pltpu.CompilerParams(
            collective_id=0, has_side_effects=True, vmem_limit_bytes=60 * 1024 * 1024),
    )(
        velocity, source, viscosity[None], owners.reshape(1, CX), targets,
        shell_load, shell_state, shell_inverse,
    )
    return tuple(out)


def solution(mesh):
    in_specs = (
        P(None, "sec", None, "dev"),
        P(None, "sec", None, "dev"),
        P("sec", None, "dev"),
        P("dev", "sec", None),
        P("dev", "sec"),
        P(None, ("sec", "dev")),
        P(None, ("sec", "dev")),
        P(None, None, ("sec", "dev")),
    )
    out_specs = (P(None, "sec", None, "dev"), P(None, ("sec", "dev")))
    return jax.shard_map(body, mesh=mesh, in_specs=in_specs, out_specs=out_specs, check_vma=False)
```

```python
import jax
import jax.numpy as jnp
from jax import lax
from jax.experimental import pallas as pl
from jax.experimental.pallas import tpu as pltpu
from jax.sharding import PartitionSpec as P

SWEEPS = 8
SHELL_SWEEPS = 8
SUBITERS = 2
CX = 16
NY = 64
LANES = 128
NB = 16
ROWS = 3 * CX
MESH = pl.DeviceIdType.MESH
F32 = jnp.float32


def kernel(
    nsec, ndev,
    vel_hbm, src_hbm, nu_hbm, owner_ref, name_ref, load_hbm, state_hbm, inv_hbm,
    uout_hbm, sout_ref,
    vel_ref, src_ref, nu_ref, load_ref, state_ref, inv_ref,
    UA, UB, NU, CF, CW, SRC, RHS, RW, XR, ZS, ZR, CS, CR,
    NXR, NZS, NZR, NCS, NCR, SXR, EC, ECR, HC, RH,
    S, ST, G, GT, AS, AR, WT, WQ, WX, WXR, WZR, PULL, N2,
    SH, LOAD, FORCE, INV, IS, IR, HS, HR,
    xs_sem, xr_sem, zs_sem, zr_sem, cs_sem, cr_sem,
    nxs_sem, nxr_sem, nzs_sem, nzr_sem, ncs_sem, ncr_sem, ss_sem, sr_sem, es_sem, er_sem,
    wxs_sem, wxr_sem, wzs_sem, wzr_sem,
    as_sem, ar_sem, is_sem, ir_sem, hs_sem, hr_sem, in_sem,
):
    sec = lax.axis_index("sec")
    dev = lax.axis_index("dev")
    has = {("x", 0): sec > 0, ("x", 1): sec < nsec - 1, ("z", 0): dev > 0, ("z", 1): dev < ndev - 1}
    lane = lax.broadcasted_iota(jnp.int32, (8, LANES), 1)
    sub = lax.broadcasted_iota(jnp.int32, (8, LANES), 0)

    def target(axis, side):
        step = 1 if side else -1
        return {"sec": lax.rem(sec + step + nsec, nsec)} if axis == "x" else {"dev": lax.rem(dev + step + ndev, ndev)}

    def remote(src, dst, send_sem, recv_sem, device):
        return pltpu.make_async_remote_copy(
            src_ref=src, dst_ref=dst, send_sem=send_sem, recv_sem=recv_sem,
            device_id=device, device_id_type=MESH)

    def u_copy(p, c, side):
        return remote(UA.at[c, pl.ds((CX - 2) * side, 2)], XR.at[p, c, 1 - side],
                      xs_sem.at[p, c, side], xr_sem.at[p, c, 1 - side], target("x", side))

    def z_copy(p, c, side):
        return remote(ZS.at[p, c], ZR.at[p, c, 1 - side],
                      zs_sem.at[p, c, side], zr_sem.at[p, c, 1 - side], target("z", side))

    def corner(a, b):
        return target("x", a) | target("z", b)

    def c_copy(p, c, a, b):
        return remote(CS.at[p, c, a], CR.at[p, c, 1 - a, 1 - b],
                      cs_sem.at[p, c, a, b], cr_sem.at[p, c, 1 - a, 1 - b], corner(a, b))

    def nu_copy(side):
        return remote(NU.at[0, pl.ds((CX - 2) * side, 2)], NXR.at[1 - side],
                      nxs_sem.at[side], nxr_sem.at[1 - side], target("x", side))

    def nz_copy(side):
        return remote(NZS, NZR.at[1 - side], nzs_sem.at[side], nzr_sem.at[1 - side], target("z", side))

    def nc_copy(a, b):
        return remote(NCS.at[a], NCR.at[1 - a, 1 - b],
                      ncs_sem.at[a, b], ncr_sem.at[1 - a, 1 - b], corner(a, b))

    def src_copy(side):
        return remote(SRC.at[:, (CX - 1) * side], SXR.at[1 - side],
                      ss_sem.at[side], sr_sem.at[1 - side], target("x", side))

    def edge_copy(side):
        return remote(EC, ECR.at[1 - side], es_sem.at[side], er_sem.at[1 - side], target("z", side))

    def wall_x_copy(k, side):
        return remote(WX.at[k], WXR.at[k, 1 - side],
                      wxs_sem.at[k, side], wxr_sem.at[k, 1 - side], target("x", side))

    def wall_z_copy(k, side):
        return remote(WQ.at[k], WZR.at[k, 1 - side],
                      wzs_sem.at[k, side], wzr_sem.at[k, 1 - side], target("z", side))

    def inv_copy(side):
        return pltpu.make_async_remote_copy(
            src_ref=IS.at[side], dst_ref=IR.at[1 - side],
            send_sem=is_sem.at[side], recv_sem=ir_sem.at[1 - side],
            device_id=target("z", side), device_id_type=MESH)

    def end_copy(k, side):
        return pltpu.make_async_remote_copy(
            src_ref=HS.at[k, side], dst_ref=HR.at[k, 1 - side],
            send_sem=hs_sem.at[k, side], recv_sem=hr_sem.at[k, 1 - side],
            device_id=target("z", side), device_id_type=MESH)

    def both(axis, act):
        for side in (0, 1):
            @pl.when(has[(axis, side)])
            def _():
                act(side)

    def sides(act):
        for side in (0, 1):
            act(side)

    def all_corners(act):
        for a in (0, 1):
            for b in (0, 1):
                act(a, b)

    def corners(act):
        for a in (0, 1):
            for b in (0, 1):
                @pl.when(has[("x", a)] & has[("z", b)])
                def _():
                    act(a, b)

    def exchange_start(phase):
        def hops(i):
            y, z = i // 8, i // 2 % 4
            return min(y, 4 - y) + min(z, 4 - z)

        for i in sorted(range(1, ndev), key=lambda i: -hops(i)):
            peer = lax.rem(dev + i, ndev)
            remote(AS.at[phase, peer], AR.at[phase, dev], as_sem.at[phase], ar_sem.at[phase], {"dev": peer}).start()
        AR[phase, dev] = AS[phase, dev]

    def exchange_wait(phase):
        copy = pltpu.make_async_remote_copy(
            src_ref=AS.at[phase, pl.ds(0, ndev - 1)], dst_ref=AR.at[phase, pl.ds(0, ndev - 1)],
            send_sem=as_sem.at[phase], recv_sem=ar_sem.at[phase],
            device_id={"dev": lax.rem(dev + 1, ndev)}, device_id_type=MESH)
        copy.wait_send()
        copy.wait_recv()

    def pick(one_hot, b):
        high = b.astype(jnp.bfloat16)
        rest = b - high.astype(F32)
        middle = rest.astype(jnp.bfloat16)
        low = (rest - middle.astype(F32)).astype(jnp.bfloat16)
        parts = jnp.concatenate([high, middle, low], axis=1)
        out = lax.dot_general(one_hot, parts, (((1,), (0,)), ((), ())), preferred_element_type=F32)
        return (out[:, :LANES] + out[:, LANES : 2 * LANES]) + out[:, 2 * LANES :]

    def tall(rows):
        return jnp.concatenate([rows, jnp.zeros((LANES - ROWS, LANES), F32)], axis=0)

    half = lane < LANES // 2
    half16 = lax.broadcasted_iota(jnp.int32, (CX, LANES), 1) < LANES // 2

    def turn(first, second):
        top = [jnp.where(half, first[n], pltpu.roll(second[n], LANES // 2, 1)) for n in range(8)]
        low = [jnp.where(half, pltpu.roll(first[n], LANES // 2, 1), second[n]) for n in range(8)]
        return jnp.concatenate(top + low, axis=0).T

    def spread(ref, c, x, rows):
        for m in range(8):
            ref[c, x, pl.ds(m, 8, stride=8), :] = rows[8 * m : 8 * m + 8]

    def face_rows(ref, c, low, high):
        return jnp.where(half16, ref[c, pl.ds(0, CX), low, :], ref[c, pl.ds(0, CX), high, :])

    def outer(before, after):
        part = lax.broadcasted_iota(jnp.int32, before.shape, 1) < LANES // 2
        return jnp.where(part, pltpu.roll(before, LANES // 2, 1), pltpu.roll(after, LANES // 2, 1))

    def z_first(row, tile):
        t = pltpu.roll(tile, 1, 0)
        return jnp.where(sub == 0, jnp.where(half, row, pltpu.roll(t, LANES // 2, 1)), t)

    def z_last(row, tile):
        t = pltpu.roll(tile, 7, 0)
        return jnp.where(sub == 7, jnp.where(half, pltpu.roll(t, LANES // 2, 1), row), t)

    loads = [
        pltpu.make_async_copy(src, dst, in_sem.at[n])
        for n, (src, dst) in enumerate((
            (state_hbm, state_ref), (nu_hbm, nu_ref), (vel_hbm, vel_ref),
            (src_hbm, src_ref), (inv_hbm, inv_ref), (load_hbm, load_ref)))]
    for copy in loads:
        copy.start()

    for ref in (NXR, NZR, NCR, SXR, ECR, WXR, WZR, CS, NCS):
        ref[...] = jnp.zeros(ref.shape, F32)
    IR[...] = jnp.zeros(IR.shape, F32)
    IS[...] = jnp.zeros(IS.shape, F32)
    HR[...] = jnp.zeros(HR.shape, F32)
    HS[...] = jnp.zeros(HS.shape, F32)

    barrier = pltpu.get_barrier_semaphore()

    def greet(i, carry):
        pl.semaphore_signal(barrier, inc=1, device_id={"dev": lax.rem(dev + i, ndev)}, device_id_type=MESH)
        return carry

    lax.fori_loop(1, ndev, greet, 0)
    sides(lambda side: pl.semaphore_signal(barrier, inc=1, device_id=target("x", side), device_id_type=MESH))
    all_corners(lambda a, b: pl.semaphore_signal(barrier, inc=1, device_id=corner(a, b), device_id_type=MESH))

    place16 = lax.broadcasted_iota(jnp.int32, (CX, CX), 0)
    other16 = lax.broadcasted_iota(jnp.int32, (CX, CX), 1)

    def column(row):
        return jnp.sum(jnp.where(place16 == other16, jnp.broadcast_to(row, (CX, CX)), 0.0), axis=1, keepdims=True)

    owner_row = owner_ref[...].astype(F32)
    owner = column(owner_row)
    name = column(name_ref[...].astype(F32))
    same = (owner == owner_row) & (other16 < place16)
    rank = jnp.sum(jnp.where(same, 1.0, 0.0), axis=1, keepdims=True)
    slots = lax.broadcasted_iota(jnp.int32, (CX, 8 * ndev), 1).astype(F32)
    blocks = lax.broadcasted_iota(jnp.int32, (CX, LANES), 1).astype(F32)
    key = 8.0 * owner + rank
    one_hot = jnp.concatenate(
        [jnp.where(slots == key + 2.0 * c, 1.0, 0.0) for c in range(3)]
        + [jnp.zeros((LANES - ROWS, 8 * ndev), F32)], axis=0)
    names = tall(jnp.concatenate(
        [jnp.where(blocks == name + float(NB * c), 1.0, 0.0) for c in range(3)], axis=0))
    ST[...] = one_hot.astype(jnp.bfloat16)
    S[...] = one_hot.T.astype(jnp.bfloat16)
    AS[0] = lax.dot_general(
        S[...], names.astype(jnp.bfloat16), (((1,), (0,)), ((), ())), preferred_element_type=F32
    ).reshape(ndev, 8, LANES)


    def take(refs):
        def step(i, carry):
            for ref, c, out, d in refs:
                first = [ref[c, 2 * i, pl.ds(8 * n, 8), :] for n in range(8)]
                second = [ref[c, 2 * i + 1, pl.ds(8 * n, 8), :] for n in range(8)]
                rows = turn(first, second)
                spread(out, d, 2 * i, rows[:NY])
                spread(out, d, 2 * i + 1, rows[NY:])
            return carry

        lax.fori_loop(0, CX // 2, step, 0)

    def send_corner(ref, rows):
        ref[0, pl.ds(0, 1), :] = rows[0:1]
        ref[1, pl.ds(0, 1), :] = rows[CX - 1 : CX]

    loads[1].wait()
    take([(nu_ref, 0, NU, 0)])
    NZS[...] = face_rows(NU, 0, 0, NY - 1)
    send_corner(NCS, NZS[...])

    pl.semaphore_wait(barrier, (ndev - 1) + 6)
    exchange_start(0)
    corners(lambda a, b: nc_copy(a, b).start())
    both("z", lambda side: nz_copy(side).start())
    both("x", lambda side: nu_copy(side).start())
    wet = nu_ref[0, :, 0, :]
    N2[...] = 2.0 * tall(jnp.concatenate([wet, wet, wet], axis=0)).T

    loads[2].wait()
    take([(vel_ref, c, UA, c) for c in range(3)])
    for c in range(3):
        ZS[0, c, pl.ds(0, CX), :] = face_rows(UA, c, 0, NY - 1)
        ZS[0, c, pl.ds(CX, CX), :] = face_rows(UA, c, 8, NY - 9)
        send_corner(CS.at[0, c], ZS[0, c, pl.ds(0, CX), :])
        all_corners(lambda a, b: c_copy(0, c, a, b).start())
        sides(lambda side: z_copy(0, c, side).start())
        sides(lambda side: u_copy(0, c, side).start())

    loads[0].wait()
    SH[...] = jnp.zeros(SH.shape, F32)
    FORCE[...] = jnp.zeros(FORCE.shape, F32)
    for n in range(NB):
        SH[:, n, :] = state_ref[:, pl.ds(LANES * n, LANES)]

    def ends(right, left):
        return jnp.where(sub == 0, right, jnp.where(sub == 7, left, 0.0))

    exchange_wait(0)
    got = AR[0].reshape(8 * ndev, LANES)
    G[...] = got.astype(jnp.bfloat16)

    def send_wall(k):
        rows = jnp.concatenate([SH[f, pl.ds(0, NB), :] for f in range(3)], axis=0)
        AS[1 + k] = pick(G[...], tall(rows)).reshape(ndev, 8, LANES)
        exchange_start(1 + k)

    def take_wall(k, begun):
        exchange_wait(1 + k)
        wall = pick(ST[...], AR[1 + k].reshape(8 * ndev, LANES))
        WQ[k] = wall[:ROWS]
        both("z", lambda side: wall_z_copy(k, side).start())
        WT[...] = wall.T
        for j in range(8):
            WX[k, pl.ds(8 * j, 8), :] = jnp.where(
                half,
                WT[pl.ds(j, 8, stride=8), :],
                pltpu.roll(WT[pl.ds(NY + j, 8, stride=8), :], LANES // 2, 1))
        both("x", lambda side: wall_x_copy(k, side).start())
        tiles = [WX[k, pl.ds(8 * j, 8), :] for j in range(8)]
        for c in range(3):
            for x in range(CX):
                for j, value in enumerate(add_wall(c, x, c * CX + x, tiles)):
                    rows = pl.ds(8 * j, 8)
                    if begun:
                        UB[c, x + 1, rows, :] = UB[c, x + 1, rows, :] + value

    def add_wall(c, x, q, tiles):
        values = []
        for j in range(8):
            rows = pl.ds(8 * j, 8)
            wall = pltpu.roll(tiles[j], LANES - q, 1) if q else tiles[j]
            values.append(CW[x + 1, rows, :] * wall)
            RW[c, x + 1, rows, :] = RHS[c, x + 1, rows, :] + values[-1]
        return values

    def take_wall_halo(k):
        both("z", lambda side: wall_z_copy(k, side).wait_send())
        both("z", lambda side: wall_z_copy(k, 1 - side).wait_recv())
        both("x", lambda side: wall_x_copy(k, side).wait_send())
        both("x", lambda side: wall_x_copy(k, 1 - side).wait_recv())
        for c in range(3):
            rows = pl.ds(CX * c, CX)
            wall = jnp.where(half16, pltpu.roll(WZR[k, 0, rows, :], 1, 1), pltpu.roll(WZR[k, 1, rows, :], LANES // 2, 1))
            RH[c] = HC[7 + c] + HC[6] * wall
        for side, x, own in ((0, -1, CX - 1), (1, CX, 0)):
            tiles = [WXR[k, side, pl.ds(8 * j, 8), :] for j in range(8)]
            for c in range(3):
                add_wall(c, x, c * CX + own, tiles)

    send_wall(0)
    GT[...] = got.T.astype(jnp.bfloat16)

    loads[3].wait()
    take([(src_ref, c, SRC, c) for c in range(3)])
    both("x", lambda side: src_copy(side).start())
    loads[4].wait()
    for a in range(6):
        IS[0, pl.ds(6 * a, 6), :] = inv_ref[a, :, pl.ds(0, LANES)]
        IS[1, pl.ds(6 * a, 6), :] = inv_ref[a, :, pl.ds(LANES * (NB - 1), LANES)]
    both("z", lambda side: inv_copy(side).start())
    loads[5].wait()

    both("x", lambda side: nu_copy(side).wait_send())
    both("x", lambda side: nu_copy(1 - side).wait_recv())
    both("z", lambda side: nz_copy(side).wait_send())
    both("z", lambda side: nz_copy(1 - side).wait_recv())
    corners(lambda a, b: nc_copy(a, b).wait_send())
    corners(lambda a, b: nc_copy(1 - a, 1 - b).wait_recv())
    y_first = lane % NY == 0
    y_last = lane % NY == NY - 1
    nu_rows = outer(NZR[0], NZR[1])
    z_low = jnp.where((sub == 0) & half, jnp.where(has[("z", 0)], 1.0, 0.0), 1.0)
    z_high = jnp.where((sub == 7) & ~half, jnp.where(has[("z", 1)], 1.0, 0.0), 1.0)
    x_low = jnp.where(has[("x", 0)], 1.0, 0.0)
    x_high = jnp.where(has[("x", 1)], 1.0, 0.0)

    def halo_planes(ref, c, near):
        def get(x, j):
            rows = pl.ds(8 * j, 8)
            if x < 0:
                return near(0, x + 2, rows)
            if x >= CX:
                return near(1, x - CX, rows)
            return ref[c, x, rows, :]
        return get

    get_nu = halo_planes(NU, 0, lambda side, n, rows: NXR[side, n, rows, :])

    def coefficients(x, row, valid):
        tiles = [get_nu(x, j) for j in range(8)]
        for j in range(8):
            rows = pl.ds(8 * j, 8)
            t = tiles[j]
            zm = tiles[j - 1] if j else z_first(row, tiles[7])
            zp = tiles[j + 1] if j < 7 else z_last(row, tiles[0])
            ym = jnp.where(y_first, t, pltpu.roll(t, 1, 1))
            yp = jnp.where(y_last, t, pltpu.roll(t, LANES - 1, 1))
            faces = [0.5 * (t + o) for o in (get_nu(x - 1, j), get_nu(x + 1, j), zm, zp, ym, yp)]
            total = 1.0 + faces[0]
            for f in faces[1:]:
                total = total + f
            inverse = valid / total
            ends_at = [x_low if x == 0 else None, x_high if x == CX - 1 else None,
                       z_low if j == 0 else None, z_high if j == 7 else None]
            for n in range(4):
                face = faces[n] * inverse
                CF[n, x + 1, rows, :] = face if ends_at[n] is None else face * ends_at[n]
            below = faces[4] * inverse
            CW[x + 1, rows, :] = jnp.where(y_first, below, 0.0)
            CF[4, x + 1, rows, :] = jnp.where(y_first, 0.0, below)
            CF[5, x + 1, rows, :] = jnp.where(y_last, 0.0, faces[5] * inverse)
            for c in range(3):
                if x < 0:
                    base = SXR[0, c, rows, :]
                elif x >= CX:
                    base = SXR[1, c, rows, :]
                else:
                    base = SRC[c, x, rows, :]
                RHS[c, x + 1, rows, :] = base * inverse

    for x in range(CX):
        coefficients(x, nu_rows[x : x + 1], 1.0)

    def edge_rows(ref, n, m):
        return jnp.where(half16, ref[n, pl.ds(1, CX), 0, :], ref[m, pl.ds(1, CX), NY - 1, :])

    for i, (n, m) in enumerate(((0, 0), (1, 1), (3, 2), (2, 3), (4, 4), (5, 5))):
        EC[i] = edge_rows(CF, n, m)
    EC[6] = jnp.where(half16, CW[pl.ds(1, CX), 0, :], CW[pl.ds(1, CX), NY - 1, :])
    for c in range(3):
        EC[7 + c] = edge_rows(RHS, c, c)
    both("z", lambda side: edge_copy(side).start())

    both("x", lambda side: src_copy(side).wait_send())
    both("x", lambda side: src_copy(1 - side).wait_recv())
    one_row = lax.broadcasted_iota(jnp.int32, (1, LANES), 1) < LANES // 2
    for side, x in ((0, -1), (1, CX)):
        row = outer(NCR[side, 0, pl.ds(0, 8), :], NCR[side, 1, pl.ds(0, 8), :])[0:1]
        coefficients(x, row, jnp.where(has[("x", side)], 1.0, 0.0))

    def take_edges():
        both("z", lambda side: edge_copy(side).wait_send())
        both("z", lambda side: edge_copy(1 - side).wait_recv())
        for i in range(10):
            HC[i] = outer(ECR[0, i], ECR[1, i])

    def plane(c, x, get, put, row, base=RW, js=range(8)):
        tiles = [get(x, j) for j in range(8)]
        for j in js:
            rows = pl.ds(8 * j, 8)
            t = tiles[j]
            zm = tiles[j - 1] if j else z_first(row, tiles[7])
            zp = tiles[j + 1] if j < 7 else z_last(row, tiles[0])
            num = base[c, x + 1, rows, :] + CF[0, x + 1, rows, :] * get(x - 1, j)
            num = num + CF[1, x + 1, rows, :] * get(x + 1, j)
            num = num + CF[2, x + 1, rows, :] * zm + CF[3, x + 1, rows, :] * zp
            ys = CF[4, x + 1, rows, :] * pltpu.roll(t, 1, 1)
            ys = ys + CF[5, x + 1, rows, :] * pltpu.roll(t, LANES - 1, 1)
            put(x, rows, num + ys)

    sub16 = lax.broadcasted_iota(jnp.int32, (CX, LANES), 0)
    last = SUBITERS * SWEEPS // 2

    def arrive(p, c):
        sides(lambda side: z_copy(p, c, 1 - side).wait_recv())
        sides(lambda side: u_copy(p, c, 1 - side).wait_recv())

    def beside(p, c):
        near = outer(ZR[p, c, 0, pl.ds(0, CX), :], ZR[p, c, 1, pl.ds(0, CX), :])
        far = outer(ZR[p, c, 0, pl.ds(CX, CX), :], ZR[p, c, 1, pl.ds(CX, CX), :])
        return near, far

    def beside_corners(p, c):
        all_corners(lambda a, b: c_copy(p, c, 1 - a, 1 - b).wait_recv())
        low = outer(CR[p, c, 0, 0], CR[p, c, 0, 1])[0:1]
        high = outer(CR[p, c, 1, 0], CR[p, c, 1, 1])[0:1]
        return low, high

    def even(p, c):
        return halo_planes(UA, c, lambda side, n, rows: XR[p, c, side, n, rows, :])

    def odd(c):
        return lambda x, j: UB[c, x + 1, pl.ds(8 * j, 8), :]

    def put_odd(c):
        def put(x, rows, value):
            UB[c, x + 1, rows, :] = value
        return put

    def put_even(c):
        def put(x, rows, value):
            UA[c, x, rows, :] = value
        return put

    def middle(p, c, xs, rows, base=RW, js=range(8)):
        for x in xs:
            row = None if rows is None else rows[0] if x < 0 else rows[1] if x >= CX else rows[0][x : x + 1]
            plane(c, x, even(p, c), put_odd(c), row, base, js)

    def middle_rows(p, c, rows, ends_of):
        near, far = rows
        low, high = ends_of
        before = jnp.where(sub16 == 0, low, pltpu.roll(near, 1, 0))
        after = jnp.where(sub16 == CX - 1, high, pltpu.roll(near, CX - 1, 0))
        total = RH[c] + HC[0] * before + HC[1] * after + HC[2] * far
        total = total + HC[3] * ZS[p, c, pl.ds(0, CX), :]
        return total + HC[4] * pltpu.roll(near, 1, 1) + HC[5] * pltpu.roll(near, LANES - 1, 1)

    def finish(n, p, c, rows, ends_of, xs):
        near = middle_rows(p, c, rows, ends_of)

        def final(group):
            for x in group:
                plane(c, x, odd(c), put_even(c), near[x : x + 1])

        sides(lambda side: u_copy(p, c, side).wait_send())
        all_corners(lambda a, b: c_copy(p, c, a, b).wait_send())
        sides(lambda side: z_copy(p, c, side).wait_send())
        final((0, CX - 1))
        edge = [
            jnp.where(one_row, UA[c, x, pl.ds(0, 1), :], UA[c, x, pl.ds(NY - 1, 1), :]) for x in (0, CX - 1)]
        CS[1 - p, c, 0, pl.ds(0, 1), :] = edge[0]
        CS[1 - p, c, 1, pl.ds(0, 1), :] = edge[1]

        @pl.when(n + 1 < last)
        def _():
            all_corners(lambda a, b: c_copy(1 - p, c, a, b).start())

        final((1, CX - 2))

        @pl.when(n + 1 < last)
        def _():
            sides(lambda side: u_copy(1 - p, c, side).start())

        middle(p, c, xs, rows)
        final(range(2, CX - 2))
        ZS[1 - p, c, pl.ds(0, CX), :] = face_rows(UA, c, 0, NY - 1)
        ZS[1 - p, c, pl.ds(CX, CX), :] = face_rows(UA, c, 8, NY - 9)

        @pl.when(n + 1 < last)
        def _():
            sides(lambda side: z_copy(1 - p, c, side).start())

    def early(k, base):
        p = lax.rem(k * (SWEEPS // 2), 2)

        def start(c, carry):
            arrive(p, c)
            middle(p, c, range(CX), beside(p, c), base)
            return carry

        lax.fori_loop(0, 3, start, 0)

    def first_pair(k):
        n = k * (SWEEPS // 2)
        p = lax.rem(n, 2)

        def rest(c, carry):
            ends_of = beside_corners(p, c)
            middle(p, c, (-1, CX), ends_of)
            finish(n, p, c, beside(p, c), ends_of, ())
            return carry

        lax.fori_loop(0, 3, rest, 0)

    def pair(n, carry):
        p = lax.rem(n, 2)

        def component(c, carry):
            middle(p, c, range(1, CX - 1), None, js=range(1, 7))
            sides(lambda side: z_copy(p, c, 1 - side).wait_recv())
            rows = beside(p, c)
            middle(p, c, range(1, CX - 1), rows, js=(0, 7))
            sides(lambda side: u_copy(p, c, 1 - side).wait_recv())
            middle(p, c, (0, CX - 1), rows)
            ends_of = beside_corners(p, c)
            middle(p, c, (-1, CX), ends_of)
            finish(n, p, c, rows, ends_of, ())
            return carry

        lax.fori_loop(0, 3, component, 0)
        return carry

    def shell_sweep(step, carry):
        drive = []
        lane24 = lax.broadcasted_iota(jnp.int32, (24, LANES), 1)
        for f in range(6):
            s = SH[f]
            up = pltpu.roll(s, 1, 1)
            before = jnp.where(lane24 == 0, pltpu.roll(up, 1, 0), up)
            down = pltpu.roll(s, LANES - 1, 1)
            after = jnp.where(lane24 == LANES - 1, pltpu.roll(down, 23, 0), down)
            drive.append(FORCE[f] + 0.4 * (before + after))
        for a in range(6):
            total = INV[6 * a] * drive[0]
            for b in range(1, 6):
                total = total + INV[6 * a + b] * drive[b]
            SH[a] = total
        return carry

    store = pltpu.make_async_copy(vel_ref, uout_hbm, in_sem.at[2])

    def give(i, carry):
        for c in range(3):
            rows = jnp.concatenate(
                [UA[c, 2 * i + p, pl.ds(m, 8, stride=8), :] for p in range(2) for m in range(8)], axis=0).T
            for n in range(8):
                top, low = rows[8 * n : 8 * n + 8], rows[NY + 8 * n : NY + 8 * n + 8]
                vel_ref[c, 2 * i, pl.ds(8 * n, 8), :] = jnp.where(half, top, pltpu.roll(low, LANES // 2, 1))
                vel_ref[c, 2 * i + 1, pl.ds(8 * n, 8), :] = jnp.where(half, pltpu.roll(top, LANES // 2, 1), low)
        return carry

    def build_shell():
        both("z", lambda side: inv_copy(side).wait_send())
        both("z", lambda side: inv_copy(1 - side).wait_recv())
        for a in range(6):
            for n in range(NB):
                INV[pl.ds(6 * a, 6), n, :] = inv_ref[a, :, pl.ds(LANES * n, LANES)]
        for n in range(36):
            INV[n, pl.ds(NB, 8), :] = ends(IR[1, pl.ds(n, 1), :], IR[0, pl.ds(n, 1), :])
        for n in range(NB):
            LOAD[:, n, :] = load_ref[:, pl.ds(LANES * n, LANES)]

    def subiteration(k, carry):
        @pl.when(k > 0)
        def _():
            take_wall(k, True)

        take_wall_halo(k)
        first_pair(k)
        lax.fori_loop(k * (SWEEPS // 2) + 1, (k + 1) * (SWEEPS // 2), pair, 0)
        tiles = [jnp.zeros((8, LANES), F32) for j in range(8)]
        for q in range(ROWS):
            here = (lane == q) | (lane == q + NY)
            for j in range(8):
                tile = UA[q // CX, q % CX, pl.ds(8 * j, 8), :]
                tiles[j] = jnp.where(here, pltpu.roll(tile, q, 1) if q else tile, tiles[j])
        for j in range(8):
            PULL[pl.ds(j, 8, stride=8), :] = jnp.where(half, tiles[j], 0.0)
            PULL[pl.ds(NY + j, 8, stride=8), :] = jnp.where(half, pltpu.roll(tiles[j], LANES // 2, 1), 0.0)
        pulls = N2[...] * (PULL[...] - WT[...])
        AS[3 + k] = pick(S[...], pulls.T).reshape(ndev, 8, LANES)
        exchange_start(3 + k)

        @pl.when(k + 1 < SUBITERS)
        def _():
            early(k + 1, RHS)
            build_shell()

        @pl.when(k + 1 == SUBITERS)
        def _():
            lax.fori_loop(0, CX // 2, give, 0)
            store.start()

        exchange_wait(3 + k)
        added = pick(GT[...], AR[3 + k].reshape(8 * ndev, LANES))
        for f in range(6):
            force = LOAD[f]
            if f < 3:
                force = force + added[NB * f : NB * (f + 1)]
            FORCE[f, pl.ds(0, NB), :] = force
            HS[k, 0, pl.ds(f, 1), :] = force[0:1]
            HS[k, 1, pl.ds(f, 1), :] = force[NB - 1 : NB]
            HS[k, 0, pl.ds(8 + f, 1), :] = SH[f, pl.ds(0, 1), :]
            HS[k, 1, pl.ds(8 + f, 1), :] = SH[f, pl.ds(NB - 1, 1), :]
        both("z", lambda side: end_copy(k, side).start())
        both("z", lambda side: end_copy(k, side).wait_send())
        both("z", lambda side: end_copy(k, 1 - side).wait_recv())
        for f in range(6):
            FORCE[f, pl.ds(NB, 8), :] = ends(HR[k, 1, pl.ds(f, 1), :], HR[k, 0, pl.ds(f, 1), :])
            SH[f, pl.ds(NB, 8), :] = ends(HR[k, 1, pl.ds(8 + f, 1), :], HR[k, 0, pl.ds(8 + f, 1), :])
        lax.fori_loop(0, SHELL_SWEEPS, shell_sweep, 0)

        @pl.when(k + 1 < SUBITERS)
        def _():
            send_wall(k + 1)
        return carry

    take_wall(0, False)
    early(0, RW)
    take_edges()
    lax.fori_loop(0, SUBITERS, subiteration, 0)

    for n in range(NB):
        sout_ref[:, pl.ds(LANES * n, LANES)] = SH[:, n, :]
    store.wait()


def body(velocity, source, viscosity, owners, targets, shell_load, shell_state, shell_inverse):
    nsec = lax.axis_size("sec")
    ndev = lax.axis_size("dev")
    vmem = pl.BlockSpec(memory_space=pltpu.VMEM)
    hbm = pl.BlockSpec(memory_space=pltpu.HBM)
    bf16 = jnp.bfloat16
    dma = pltpu.SemaphoreType.DMA
    out = pl.pallas_call(
        lambda *refs: kernel(nsec, ndev, *refs),
        out_shape=(
            jax.ShapeDtypeStruct((3, CX, NY, LANES), F32),
            jax.ShapeDtypeStruct((6, NB * LANES), F32),
        ),
        in_specs=[hbm, hbm, hbm, vmem, vmem, hbm, hbm, hbm],
        out_specs=(hbm, vmem),
        scratch_shapes=[
            pltpu.VMEM((3, CX, NY, LANES), F32),
            pltpu.VMEM((3, CX, NY, LANES), F32),
            pltpu.VMEM((1, CX, NY, LANES), F32),
            pltpu.VMEM((6, NB * LANES), F32),
            pltpu.VMEM((6, NB * LANES), F32),
            pltpu.VMEM((6, 6, NB * LANES), F32),
            pltpu.VMEM((3, CX, NY, LANES), F32),
            pltpu.VMEM((3, CX + 2, NY, LANES), F32),
            pltpu.VMEM((1, CX, NY, LANES), F32),
            pltpu.VMEM((6, CX + 2, NY, LANES), F32),
            pltpu.VMEM((CX + 2, NY, LANES), F32),
            pltpu.VMEM((3, CX, NY, LANES), F32),
            pltpu.VMEM((3, CX + 2, NY, LANES), F32),
            pltpu.VMEM((3, CX + 2, NY, LANES), F32),
            pltpu.VMEM((2, 3, 2, 2, NY, LANES), F32),
            pltpu.VMEM((2, 3, 2 * CX, LANES), F32),
            pltpu.VMEM((2, 3, 2, 2 * CX, LANES), F32),
            pltpu.VMEM((2, 3, 2, 8, LANES), F32),
            pltpu.VMEM((2, 3, 2, 2, 8, LANES), F32),
            pltpu.VMEM((2, 2, NY, LANES), F32),
            pltpu.VMEM((CX, LANES), F32),
            pltpu.VMEM((2, CX, LANES), F32),
            pltpu.VMEM((2, 8, LANES), F32),
            pltpu.VMEM((2, 2, 8, LANES), F32),
            pltpu.VMEM((2, 3, NY, LANES), F32),
            pltpu.VMEM((10, CX, LANES), F32),
            pltpu.VMEM((2, 10, CX, LANES), F32),
            pltpu.VMEM((10, CX, LANES), F32),
            pltpu.VMEM((3, CX, LANES), F32),
            pltpu.VMEM((8 * ndev, LANES), bf16),
            pltpu.VMEM((LANES, 8 * ndev), bf16),
            pltpu.VMEM((8 * ndev, LANES), bf16),
            pltpu.VMEM((LANES, 8 * ndev), bf16),
            pltpu.VMEM((5, ndev, 8, LANES), F32),
            pltpu.VMEM((5, ndev, 8, LANES), F32),
            pltpu.VMEM((LANES, LANES), F32),
            pltpu.VMEM((2, ROWS, LANES), F32),
            pltpu.VMEM((2, NY, LANES), F32),
            pltpu.VMEM((2, 2, NY, LANES), F32),
            pltpu.VMEM((2, 2, ROWS, LANES), F32),
            pltpu.VMEM((LANES, LANES), F32),
            pltpu.VMEM((LANES, LANES), F32),
            pltpu.VMEM((6, 24, LANES), F32),
            pltpu.VMEM((6, NB, LANES), F32),
            pltpu.VMEM((6, 24, LANES), F32),
            pltpu.VMEM((36, 24, LANES), F32),
            pltpu.VMEM((2, 40, LANES), F32),
            pltpu.VMEM((2, 40, LANES), F32),
            pltpu.VMEM((2, 2, 16, LANES), F32),
            pltpu.VMEM((2, 2, 16, LANES), F32),
            dma((2, 3, 2)), dma((2, 3, 2)), dma((2, 3, 2)), dma((2, 3, 2)),
            dma((2, 3, 2, 2)), dma((2, 3, 2, 2)),
            dma((2,)), dma((2,)), dma((2,)), dma((2,)), dma((2, 2)), dma((2, 2)),
            dma((2,)), dma((2,)), dma((2,)), dma((2,)),
            dma((2, 2)), dma((2, 2)), dma((2, 2)), dma((2, 2)),
            dma((5,)), dma((5,)),
            dma((2,)), dma((2,)), dma((2, 2)), dma((2, 2)), dma((6,)),
        ],
        compiler_params=pltpu.CompilerParams(
            collective_id=0, has_side_effects=True, vmem_limit_bytes=60 * 1024 * 1024),
    )(
        velocity, source, viscosity[None], owners.reshape(1, CX), targets,
        shell_load, shell_state, shell_inverse,
    )
    return tuple(out)


def solution(mesh):
    in_specs = (
        P(None, "sec", None, "dev"),
        P(None, "sec", None, "dev"),
        P("sec", None, "dev"),
        P("dev", "sec", None),
        P("dev", "sec"),
        P(None, ("sec", "dev")),
        P(None, ("sec", "dev")),
        P(None, None, ("sec", "dev")),
    )
    out_specs = (P(None, "sec", None, "dev"), P(None, ("sec", "dev")))
    return jax.shard_map(body, mesh=mesh, in_specs=in_specs, out_specs=out_specs, check_vma=False)
```

```python
import jax
import jax.numpy as jnp
from jax import lax
from jax.experimental import pallas as pl
from jax.experimental.pallas import tpu as pltpu
from jax.sharding import PartitionSpec as P

SWEEPS = 8
SHELL_SWEEPS = 8
SUBITERS = 2
CX = 16
NY = 64
LANES = 128
NB = 16
ROWS = 3 * CX
MESH = pl.DeviceIdType.MESH
F32 = jnp.float32


def kernel(
    nsec, ndev,
    vel_hbm, src_hbm, nu_hbm, owner_ref, name_ref, load_hbm, state_hbm, inv_hbm,
    uout_hbm, sout_ref,
    vel_ref, src_ref, nu_ref, load_ref, state_ref, inv_ref,
    UA, UB, NU, CF, CW, SRC, RHS, RW, XR, ZS, ZR, CS, CR,
    NXR, NZS, NZR, NCS, NCR, SXR, EC, ECR, HC, RH,
    S, ST, G, GT, AS, AR, WT, WQ, WX, WXR, WZR, PULL, N2,
    SH, LOAD, FORCE, INV, IS, IR, HS, HR,
    xs_sem, xr_sem, zs_sem, zr_sem, cs_sem, cr_sem,
    nxs_sem, nxr_sem, nzs_sem, nzr_sem, ncs_sem, ncr_sem, ss_sem, sr_sem, es_sem, er_sem,
    wxs_sem, wxr_sem, wzs_sem, wzr_sem,
    as_sem, ar_sem, is_sem, ir_sem, hs_sem, hr_sem, in_sem,
):
    sec = lax.axis_index("sec")
    dev = lax.axis_index("dev")
    has = {("x", 0): sec > 0, ("x", 1): sec < nsec - 1, ("z", 0): dev > 0, ("z", 1): dev < ndev - 1}
    lane = lax.broadcasted_iota(jnp.int32, (8, LANES), 1)
    sub = lax.broadcasted_iota(jnp.int32, (8, LANES), 0)

    def target(axis, side):
        step = 1 if side else -1
        return {"sec": lax.rem(sec + step + nsec, nsec)} if axis == "x" else {"dev": lax.rem(dev + step + ndev, ndev)}

    def remote(src, dst, send_sem, recv_sem, device):
        return pltpu.make_async_remote_copy(
            src_ref=src, dst_ref=dst, send_sem=send_sem, recv_sem=recv_sem,
            device_id=device, device_id_type=MESH)

    def u_copy(p, c, side):
        return remote(UA.at[c, pl.ds((CX - 2) * side, 2)], XR.at[p, c, 1 - side],
                      xs_sem.at[p, c, side], xr_sem.at[p, c, 1 - side], target("x", side))

    def z_copy(p, c, side):
        return remote(ZS.at[p, c], ZR.at[p, c, 1 - side],
                      zs_sem.at[p, c, side], zr_sem.at[p, c, 1 - side], target("z", side))

    def corner(a, b):
        return target("x", a) | target("z", b)

    def c_copy(p, c, a, b):
        return remote(CS.at[p, c, a], CR.at[p, c, 1 - a, 1 - b],
                      cs_sem.at[p, c, a, b], cr_sem.at[p, c, 1 - a, 1 - b], corner(a, b))

    def nu_copy(side):
        return remote(NU.at[0, pl.ds((CX - 2) * side, 2)], NXR.at[1 - side],
                      nxs_sem.at[side], nxr_sem.at[1 - side], target("x", side))

    def nz_copy(side):
        return remote(NZS, NZR.at[1 - side], nzs_sem.at[side], nzr_sem.at[1 - side], target("z", side))

    def nc_copy(a, b):
        return remote(NCS.at[a], NCR.at[1 - a, 1 - b],
                      ncs_sem.at[a, b], ncr_sem.at[1 - a, 1 - b], corner(a, b))

    def src_copy(side):
        return remote(SRC.at[:, (CX - 1) * side], SXR.at[1 - side],
                      ss_sem.at[side], sr_sem.at[1 - side], target("x", side))

    def edge_copy(side):
        return remote(EC, ECR.at[1 - side], es_sem.at[side], er_sem.at[1 - side], target("z", side))

    def wall_x_copy(k, side):
        return remote(WX.at[k], WXR.at[k, 1 - side],
                      wxs_sem.at[k, side], wxr_sem.at[k, 1 - side], target("x", side))

    def wall_z_copy(k, side):
        return remote(WQ.at[k], WZR.at[k, 1 - side],
                      wzs_sem.at[k, side], wzr_sem.at[k, 1 - side], target("z", side))

    def inv_copy(side):
        return pltpu.make_async_remote_copy(
            src_ref=IS.at[side], dst_ref=IR.at[1 - side],
            send_sem=is_sem.at[side], recv_sem=ir_sem.at[1 - side],
            device_id=target("z", side), device_id_type=MESH)

    def end_copy(k, side):
        return pltpu.make_async_remote_copy(
            src_ref=HS.at[k, side], dst_ref=HR.at[k, 1 - side],
            send_sem=hs_sem.at[k, side], recv_sem=hr_sem.at[k, 1 - side],
            device_id=target("z", side), device_id_type=MESH)

    def both(axis, act):
        for side in (0, 1):
            @pl.when(has[(axis, side)])
            def _():
                act(side)

    def sides(act):
        for side in (0, 1):
            act(side)

    def all_corners(act):
        for a in (0, 1):
            for b in (0, 1):
                act(a, b)

    def corners(act):
        for a in (0, 1):
            for b in (0, 1):
                @pl.when(has[("x", a)] & has[("z", b)])
                def _():
                    act(a, b)

    def exchange_start(phase):
        def hops(i):
            y, z = i // 8, i // 2 % 4
            return min(y, 4 - y) + min(z, 4 - z)

        for i in sorted(range(1, ndev), key=lambda i: -hops(i)):
            peer = lax.rem(dev + i, ndev)
            remote(AS.at[phase, peer], AR.at[phase, dev], as_sem.at[phase], ar_sem.at[phase], {"dev": peer}).start()
        AR[phase, dev] = AS[phase, dev]

    def exchange_wait(phase):
        copy = pltpu.make_async_remote_copy(
            src_ref=AS.at[phase, pl.ds(0, ndev - 1)], dst_ref=AR.at[phase, pl.ds(0, ndev - 1)],
            send_sem=as_sem.at[phase], recv_sem=ar_sem.at[phase],
            device_id={"dev": lax.rem(dev + 1, ndev)}, device_id_type=MESH)
        copy.wait_send()
        copy.wait_recv()

    def pick(one_hot, b):
        high = b.astype(jnp.bfloat16)
        rest = b - high.astype(F32)
        middle = rest.astype(jnp.bfloat16)
        low = (rest - middle.astype(F32)).astype(jnp.bfloat16)
        parts = jnp.concatenate([high, middle, low], axis=1)
        out = lax.dot_general(one_hot, parts, (((1,), (0,)), ((), ())), preferred_element_type=F32)
        return (out[:, :LANES] + out[:, LANES : 2 * LANES]) + out[:, 2 * LANES :]

    def tall(rows):
        return jnp.concatenate([rows, jnp.zeros((LANES - ROWS, LANES), F32)], axis=0)

    half = lane < LANES // 2
    half16 = lax.broadcasted_iota(jnp.int32, (CX, LANES), 1) < LANES // 2

    def turn(first, second):
        top = [jnp.where(half, first[n], pltpu.roll(second[n], LANES // 2, 1)) for n in range(8)]
        low = [jnp.where(half, pltpu.roll(first[n], LANES // 2, 1), second[n]) for n in range(8)]
        return jnp.concatenate(top + low, axis=0).T

    def spread(ref, c, x, rows):
        for m in range(8):
            ref[c, x, pl.ds(m, 8, stride=8), :] = rows[8 * m : 8 * m + 8]

    def face_rows(ref, c, low, high):
        return jnp.where(half16, ref[c, pl.ds(0, CX), low, :], ref[c, pl.ds(0, CX), high, :])

    def outer(before, after):
        part = lax.broadcasted_iota(jnp.int32, before.shape, 1) < LANES // 2
        return jnp.where(part, pltpu.roll(before, LANES // 2, 1), pltpu.roll(after, LANES // 2, 1))

    def z_first(row, tile):
        t = pltpu.roll(tile, 1, 0)
        return jnp.where(sub == 0, jnp.where(half, row, pltpu.roll(t, LANES // 2, 1)), t)

    def z_last(row, tile):
        t = pltpu.roll(tile, 7, 0)
        return jnp.where(sub == 7, jnp.where(half, pltpu.roll(t, LANES // 2, 1), row), t)

    loads = [
        pltpu.make_async_copy(src, dst, in_sem.at[n])
        for n, (src, dst) in enumerate((
            (state_hbm, state_ref), (nu_hbm, nu_ref), (vel_hbm, vel_ref),
            (src_hbm, src_ref), (inv_hbm, inv_ref), (load_hbm, load_ref)))]
    for copy in loads:
        copy.start()

    for ref in (NXR, NZR, NCR, SXR, ECR, WXR, WZR, CS, NCS):
        ref[...] = jnp.zeros(ref.shape, F32)
    IR[...] = jnp.zeros(IR.shape, F32)
    IS[...] = jnp.zeros(IS.shape, F32)
    HR[...] = jnp.zeros(HR.shape, F32)
    HS[...] = jnp.zeros(HS.shape, F32)

    barrier = pltpu.get_barrier_semaphore()

    def greet(i, carry):
        pl.semaphore_signal(barrier, inc=1, device_id={"dev": lax.rem(dev + i, ndev)}, device_id_type=MESH)
        return carry

    lax.fori_loop(1, ndev, greet, 0)
    sides(lambda side: pl.semaphore_signal(barrier, inc=1, device_id=target("x", side), device_id_type=MESH))
    all_corners(lambda a, b: pl.semaphore_signal(barrier, inc=1, device_id=corner(a, b), device_id_type=MESH))

    place16 = lax.broadcasted_iota(jnp.int32, (CX, CX), 0)
    other16 = lax.broadcasted_iota(jnp.int32, (CX, CX), 1)

    def column(row):
        return jnp.sum(jnp.where(place16 == other16, jnp.broadcast_to(row, (CX, CX)), 0.0), axis=1, keepdims=True)

    owner_row = owner_ref[...].astype(F32)
    owner = column(owner_row)
    name = column(name_ref[...].astype(F32))
    same = (owner == owner_row) & (other16 < place16)
    rank = jnp.sum(jnp.where(same, 1.0, 0.0), axis=1, keepdims=True)
    slots = lax.broadcasted_iota(jnp.int32, (CX, 8 * ndev), 1).astype(F32)
    blocks = lax.broadcasted_iota(jnp.int32, (CX, LANES), 1).astype(F32)
    key = 8.0 * owner + rank
    one_hot = jnp.concatenate(
        [jnp.where(slots == key + 2.0 * c, 1.0, 0.0) for c in range(3)]
        + [jnp.zeros((LANES - ROWS, 8 * ndev), F32)], axis=0)
    names = tall(jnp.concatenate(
        [jnp.where(blocks == name + float(NB * c), 1.0, 0.0) for c in range(3)], axis=0))
    ST[...] = one_hot.astype(jnp.bfloat16)
    S[...] = one_hot.T.astype(jnp.bfloat16)
    AS[0] = lax.dot_general(
        S[...], names.astype(jnp.bfloat16), (((1,), (0,)), ((), ())), preferred_element_type=F32
    ).reshape(ndev, 8, LANES)


    def take(refs):
        def step(i, carry):
            for ref, c, out, d in refs:
                first = [ref[c, 2 * i, pl.ds(8 * n, 8), :] for n in range(8)]
                second = [ref[c, 2 * i + 1, pl.ds(8 * n, 8), :] for n in range(8)]
                rows = turn(first, second)
                spread(out, d, 2 * i, rows[:NY])
                spread(out, d, 2 * i + 1, rows[NY:])
            return carry

        lax.fori_loop(0, CX // 2, step, 0)

    def send_corner(ref, rows):
        ref[0, pl.ds(0, 1), :] = rows[0:1]
        ref[1, pl.ds(0, 1), :] = rows[CX - 1 : CX]

    loads[1].wait()
    take([(nu_ref, 0, NU, 0)])
    NZS[...] = face_rows(NU, 0, 0, NY - 1)
    send_corner(NCS, NZS[...])

    pl.semaphore_wait(barrier, (ndev - 1) + 6)
    exchange_start(0)
    corners(lambda a, b: nc_copy(a, b).start())
    both("z", lambda side: nz_copy(side).start())
    both("x", lambda side: nu_copy(side).start())
    wet = nu_ref[0, :, 0, :]
    N2[...] = 2.0 * tall(jnp.concatenate([wet, wet, wet], axis=0)).T

    loads[2].wait()
    take([(vel_ref, c, UA, c) for c in range(3)])
    for c in range(3):
        ZS[0, c, pl.ds(0, CX), :] = face_rows(UA, c, 0, NY - 1)
        ZS[0, c, pl.ds(CX, CX), :] = face_rows(UA, c, 8, NY - 9)
        send_corner(CS.at[0, c], ZS[0, c, pl.ds(0, CX), :])
        all_corners(lambda a, b: c_copy(0, c, a, b).start())
        sides(lambda side: z_copy(0, c, side).start())
        sides(lambda side: u_copy(0, c, side).start())

    loads[0].wait()
    SH[...] = jnp.zeros(SH.shape, F32)
    FORCE[...] = jnp.zeros(FORCE.shape, F32)
    for n in range(NB):
        SH[:, n, :] = state_ref[:, pl.ds(LANES * n, LANES)]

    def ends(right, left):
        return jnp.where(sub == 0, right, jnp.where(sub == 7, left, 0.0))

    exchange_wait(0)
    got = AR[0].reshape(8 * ndev, LANES)
    G[...] = got.astype(jnp.bfloat16)

    def send_wall(k):
        rows = jnp.concatenate([SH[f, pl.ds(0, NB), :] for f in range(3)], axis=0)
        AS[1 + k] = pick(G[...], tall(rows)).reshape(ndev, 8, LANES)
        exchange_start(1 + k)

    def take_wall(k, begun):
        exchange_wait(1 + k)
        wall = pick(ST[...], AR[1 + k].reshape(8 * ndev, LANES))
        WQ[k] = wall[:ROWS]
        both("z", lambda side: wall_z_copy(k, side).start())
        WT[...] = wall.T
        for j in range(8):
            WX[k, pl.ds(8 * j, 8), :] = jnp.where(
                half,
                WT[pl.ds(j, 8, stride=8), :],
                pltpu.roll(WT[pl.ds(NY + j, 8, stride=8), :], LANES // 2, 1))
        both("x", lambda side: wall_x_copy(k, side).start())
        tiles = [WX[k, pl.ds(8 * j, 8), :] for j in range(8)]
        for c in range(3):
            for x in range(CX):
                for j, value in enumerate(add_wall(c, x, c * CX + x, tiles)):
                    rows = pl.ds(8 * j, 8)
                    if begun:
                        UB[c, x + 1, rows, :] = UB[c, x + 1, rows, :] + value

    def add_wall(c, x, q, tiles):
        values = []
        for j in range(8):
            rows = pl.ds(8 * j, 8)
            wall = pltpu.roll(tiles[j], LANES - q, 1) if q else tiles[j]
            values.append(CW[x + 1, rows, :] * wall)
            RW[c, x + 1, rows, :] = RHS[c, x + 1, rows, :] + values[-1]
        return values

    def take_wall_halo(k):
        both("z", lambda side: wall_z_copy(k, side).wait_send())
        both("z", lambda side: wall_z_copy(k, 1 - side).wait_recv())
        both("x", lambda side: wall_x_copy(k, side).wait_send())
        both("x", lambda side: wall_x_copy(k, 1 - side).wait_recv())
        for c in range(3):
            rows = pl.ds(CX * c, CX)
            wall = jnp.where(half16, pltpu.roll(WZR[k, 0, rows, :], 1, 1), pltpu.roll(WZR[k, 1, rows, :], LANES // 2, 1))
            RH[c] = HC[7 + c] + HC[6] * wall
        for side, x, own in ((0, -1, CX - 1), (1, CX, 0)):
            tiles = [WXR[k, side, pl.ds(8 * j, 8), :] for j in range(8)]
            for c in range(3):
                add_wall(c, x, c * CX + own, tiles)

    send_wall(0)
    GT[...] = got.T.astype(jnp.bfloat16)

    loads[3].wait()
    take([(src_ref, c, SRC, c) for c in range(3)])
    both("x", lambda side: src_copy(side).start())
    loads[4].wait()
    for a in range(6):
        IS[0, pl.ds(6 * a, 6), :] = inv_ref[a, :, pl.ds(0, LANES)]
        IS[1, pl.ds(6 * a, 6), :] = inv_ref[a, :, pl.ds(LANES * (NB - 1), LANES)]
    both("z", lambda side: inv_copy(side).start())
    loads[5].wait()

    both("x", lambda side: nu_copy(side).wait_send())
    both("x", lambda side: nu_copy(1 - side).wait_recv())
    both("z", lambda side: nz_copy(side).wait_send())
    both("z", lambda side: nz_copy(1 - side).wait_recv())
    corners(lambda a, b: nc_copy(a, b).wait_send())
    corners(lambda a, b: nc_copy(1 - a, 1 - b).wait_recv())
    y_first = lane % NY == 0
    y_last = lane % NY == NY - 1
    nu_rows = outer(NZR[0], NZR[1])
    z_low = jnp.where((sub == 0) & half, jnp.where(has[("z", 0)], 1.0, 0.0), 1.0)
    z_high = jnp.where((sub == 7) & ~half, jnp.where(has[("z", 1)], 1.0, 0.0), 1.0)
    x_low = jnp.where(has[("x", 0)], 1.0, 0.0)
    x_high = jnp.where(has[("x", 1)], 1.0, 0.0)

    def halo_planes(ref, c, near):
        def get(x, j):
            rows = pl.ds(8 * j, 8)
            if x < 0:
                return near(0, x + 2, rows)
            if x >= CX:
                return near(1, x - CX, rows)
            return ref[c, x, rows, :]
        return get

    get_nu = halo_planes(NU, 0, lambda side, n, rows: NXR[side, n, rows, :])

    def coefficients(x, row, valid):
        tiles = [get_nu(x, j) for j in range(8)]
        for j in range(8):
            rows = pl.ds(8 * j, 8)
            t = tiles[j]
            zm = tiles[j - 1] if j else z_first(row, tiles[7])
            zp = tiles[j + 1] if j < 7 else z_last(row, tiles[0])
            ym = jnp.where(y_first, t, pltpu.roll(t, 1, 1))
            yp = jnp.where(y_last, t, pltpu.roll(t, LANES - 1, 1))
            faces = [0.5 * (t + o) for o in (get_nu(x - 1, j), get_nu(x + 1, j), zm, zp, ym, yp)]
            total = 1.0 + faces[0]
            for f in faces[1:]:
                total = total + f
            inverse = valid / total
            ends_at = [x_low if x == 0 else None, x_high if x == CX - 1 else None,
                       z_low if j == 0 else None, z_high if j == 7 else None]
            for n in range(4):
                face = faces[n] * inverse
                CF[n, x + 1, rows, :] = face if ends_at[n] is None else face * ends_at[n]
            below = faces[4] * inverse
            CW[x + 1, rows, :] = jnp.where(y_first, below, 0.0)
            CF[4, x + 1, rows, :] = jnp.where(y_first, 0.0, below)
            CF[5, x + 1, rows, :] = jnp.where(y_last, 0.0, faces[5] * inverse)
            for c in range(3):
                if x < 0:
                    base = SXR[0, c, rows, :]
                elif x >= CX:
                    base = SXR[1, c, rows, :]
                else:
                    base = SRC[c, x, rows, :]
                RHS[c, x + 1, rows, :] = base * inverse

    for x in range(CX):
        coefficients(x, nu_rows[x : x + 1], 1.0)

    def edge_rows(ref, n, m):
        return jnp.where(half16, ref[n, pl.ds(1, CX), 0, :], ref[m, pl.ds(1, CX), NY - 1, :])

    for i, (n, m) in enumerate(((0, 0), (1, 1), (3, 2), (2, 3), (4, 4), (5, 5))):
        EC[i] = edge_rows(CF, n, m)
    EC[6] = jnp.where(half16, CW[pl.ds(1, CX), 0, :], CW[pl.ds(1, CX), NY - 1, :])
    for c in range(3):
        EC[7 + c] = edge_rows(RHS, c, c)
    both("z", lambda side: edge_copy(side).start())

    both("x", lambda side: src_copy(side).wait_send())
    both("x", lambda side: src_copy(1 - side).wait_recv())
    one_row = lax.broadcasted_iota(jnp.int32, (1, LANES), 1) < LANES // 2
    for side, x in ((0, -1), (1, CX)):
        row = outer(NCR[side, 0, pl.ds(0, 8), :], NCR[side, 1, pl.ds(0, 8), :])[0:1]
        coefficients(x, row, jnp.where(has[("x", side)], 1.0, 0.0))

    def take_edges():
        both("z", lambda side: edge_copy(side).wait_send())
        both("z", lambda side: edge_copy(1 - side).wait_recv())
        for i in range(10):
            HC[i] = outer(ECR[0, i], ECR[1, i])

    def plane(c, x, get, put, row, base=RW, js=range(8)):
        tiles = [get(x, j) for j in range(8)]
        for j in js:
            rows = pl.ds(8 * j, 8)
            t = tiles[j]
            zm = tiles[j - 1] if j else z_first(row, tiles[7])
            zp = tiles[j + 1] if j < 7 else z_last(row, tiles[0])
            num = base[c, x + 1, rows, :] + CF[0, x + 1, rows, :] * get(x - 1, j)
            num = num + CF[1, x + 1, rows, :] * get(x + 1, j)
            num = num + CF[2, x + 1, rows, :] * zm + CF[3, x + 1, rows, :] * zp
            ys = CF[4, x + 1, rows, :] * pltpu.roll(t, 1, 1)
            ys = ys + CF[5, x + 1, rows, :] * pltpu.roll(t, LANES - 1, 1)
            put(x, rows, num + ys)

    sub16 = lax.broadcasted_iota(jnp.int32, (CX, LANES), 0)
    last = SUBITERS * SWEEPS // 2

    def arrive(p, c):
        sides(lambda side: z_copy(p, c, 1 - side).wait_recv())
        sides(lambda side: u_copy(p, c, 1 - side).wait_recv())

    def beside(p, c):
        near = outer(ZR[p, c, 0, pl.ds(0, CX), :], ZR[p, c, 1, pl.ds(0, CX), :])
        far = outer(ZR[p, c, 0, pl.ds(CX, CX), :], ZR[p, c, 1, pl.ds(CX, CX), :])
        return near, far

    def beside_corners(p, c):
        all_corners(lambda a, b: c_copy(p, c, 1 - a, 1 - b).wait_recv())
        low = outer(CR[p, c, 0, 0], CR[p, c, 0, 1])[0:1]
        high = outer(CR[p, c, 1, 0], CR[p, c, 1, 1])[0:1]
        return low, high

    def even(p, c):
        return halo_planes(UA, c, lambda side, n, rows: XR[p, c, side, n, rows, :])

    def odd(c):
        return lambda x, j: UB[c, x + 1, pl.ds(8 * j, 8), :]

    def put_odd(c):
        def put(x, rows, value):
            UB[c, x + 1, rows, :] = value
        return put

    def put_even(c):
        def put(x, rows, value):
            UA[c, x, rows, :] = value
        return put

    def middle(p, c, xs, rows, base=RW, js=range(8)):
        for x in xs:
            row = None if rows is None else rows[0] if x < 0 else rows[1] if x >= CX else rows[0][x : x + 1]
            plane(c, x, even(p, c), put_odd(c), row, base, js)

    def middle_rows(p, c, rows, ends_of):
        near, far = rows
        low, high = ends_of
        before = jnp.where(sub16 == 0, low, pltpu.roll(near, 1, 0))
        after = jnp.where(sub16 == CX - 1, high, pltpu.roll(near, CX - 1, 0))
        total = RH[c] + HC[0] * before + HC[1] * after + HC[2] * far
        total = total + HC[3] * ZS[p, c, pl.ds(0, CX), :]
        return total + HC[4] * pltpu.roll(near, 1, 1) + HC[5] * pltpu.roll(near, LANES - 1, 1)

    def finish(n, p, c, rows, ends_of, xs):
        near = middle_rows(p, c, rows, ends_of)

        def final(group, js=range(8)):
            for x in group:
                plane(c, x, odd(c), put_even(c), near[x : x + 1], js=js)

        sides(lambda side: u_copy(p, c, side).wait_send())
        all_corners(lambda a, b: c_copy(p, c, a, b).wait_send())
        sides(lambda side: z_copy(p, c, side).wait_send())
        final((0, CX - 1))
        edge = [
            jnp.where(one_row, UA[c, x, pl.ds(0, 1), :], UA[c, x, pl.ds(NY - 1, 1), :]) for x in (0, CX - 1)]
        CS[1 - p, c, 0, pl.ds(0, 1), :] = edge[0]
        CS[1 - p, c, 1, pl.ds(0, 1), :] = edge[1]

        @pl.when(n + 1 < last)
        def _():
            all_corners(lambda a, b: c_copy(1 - p, c, a, b).start())

        final((1, CX - 2))

        @pl.when(n + 1 < last)
        def _():
            sides(lambda side: u_copy(1 - p, c, side).start())

        middle(p, c, xs, rows)
        final(range(2, CX - 2), (0, 1, 6, 7))
        ZS[1 - p, c, pl.ds(0, CX), :] = face_rows(UA, c, 0, NY - 1)
        ZS[1 - p, c, pl.ds(CX, CX), :] = face_rows(UA, c, 8, NY - 9)

        @pl.when(n + 1 < last)
        def _():
            sides(lambda side: z_copy(1 - p, c, side).start())

        final(range(2, CX - 2), (2, 3, 4, 5))

    def early(k, base):
        p = lax.rem(k * (SWEEPS // 2), 2)

        def start(c, carry):
            arrive(p, c)
            middle(p, c, range(CX), beside(p, c), base)
            return carry

        lax.fori_loop(0, 3, start, 0)

    def first_pair(k):
        n = k * (SWEEPS // 2)
        p = lax.rem(n, 2)

        def rest(c, carry):
            ends_of = beside_corners(p, c)
            middle(p, c, (-1, CX), ends_of)
            finish(n, p, c, beside(p, c), ends_of, ())
            return carry

        lax.fori_loop(0, 3, rest, 0)

    def pair(n, carry):
        p = lax.rem(n, 2)

        def component(c, carry):
            middle(p, c, range(1, CX - 1), None, js=range(1, 7))
            sides(lambda side: z_copy(p, c, 1 - side).wait_recv())
            rows = beside(p, c)
            middle(p, c, range(1, CX - 1), rows, js=(0, 7))
            sides(lambda side: u_copy(p, c, 1 - side).wait_recv())
            middle(p, c, (0, CX - 1), rows)
            ends_of = beside_corners(p, c)
            middle(p, c, (-1, CX), ends_of)
            finish(n, p, c, rows, ends_of, ())
            return carry

        lax.fori_loop(0, 3, component, 0)
        return carry

    def shell_sweep(step, carry):
        drive = []
        lane24 = lax.broadcasted_iota(jnp.int32, (24, LANES), 1)
        for f in range(6):
            s = SH[f]
            up = pltpu.roll(s, 1, 1)
            before = jnp.where(lane24 == 0, pltpu.roll(up, 1, 0), up)
            down = pltpu.roll(s, LANES - 1, 1)
            after = jnp.where(lane24 == LANES - 1, pltpu.roll(down, 23, 0), down)
            drive.append(FORCE[f] + 0.4 * (before + after))
        for a in range(6):
            total = INV[6 * a] * drive[0]
            for b in range(1, 6):
                total = total + INV[6 * a + b] * drive[b]
            SH[a] = total
        return carry

    store = pltpu.make_async_copy(vel_ref, uout_hbm, in_sem.at[2])

    def give(i, carry):
        for c in range(3):
            rows = jnp.concatenate(
                [UA[c, 2 * i + p, pl.ds(m, 8, stride=8), :] for p in range(2) for m in range(8)], axis=0).T
            for n in range(8):
                top, low = rows[8 * n : 8 * n + 8], rows[NY + 8 * n : NY + 8 * n + 8]
                vel_ref[c, 2 * i, pl.ds(8 * n, 8), :] = jnp.where(half, top, pltpu.roll(low, LANES // 2, 1))
                vel_ref[c, 2 * i + 1, pl.ds(8 * n, 8), :] = jnp.where(half, pltpu.roll(top, LANES // 2, 1), low)
        return carry

    def build_shell():
        both("z", lambda side: inv_copy(side).wait_send())
        both("z", lambda side: inv_copy(1 - side).wait_recv())
        for a in range(6):
            for n in range(NB):
                INV[pl.ds(6 * a, 6), n, :] = inv_ref[a, :, pl.ds(LANES * n, LANES)]
        for n in range(36):
            INV[n, pl.ds(NB, 8), :] = ends(IR[1, pl.ds(n, 1), :], IR[0, pl.ds(n, 1), :])
        for n in range(NB):
            LOAD[:, n, :] = load_ref[:, pl.ds(LANES * n, LANES)]

    def subiteration(k, carry):
        @pl.when(k > 0)
        def _():
            take_wall(k, True)

        take_wall_halo(k)
        first_pair(k)
        lax.fori_loop(k * (SWEEPS // 2) + 1, (k + 1) * (SWEEPS // 2), pair, 0)
        tiles = [jnp.zeros((8, LANES), F32) for j in range(8)]
        for q in range(ROWS):
            here = (lane == q) | (lane == q + NY)
            for j in range(8):
                tile = UA[q // CX, q % CX, pl.ds(8 * j, 8), :]
                tiles[j] = jnp.where(here, pltpu.roll(tile, q, 1) if q else tile, tiles[j])
        for j in range(8):
            PULL[pl.ds(j, 8, stride=8), :] = jnp.where(half, tiles[j], 0.0)
            PULL[pl.ds(NY + j, 8, stride=8), :] = jnp.where(half, pltpu.roll(tiles[j], LANES // 2, 1), 0.0)
        pulls = N2[...] * (PULL[...] - WT[...])
        AS[3 + k] = pick(S[...], pulls.T).reshape(ndev, 8, LANES)
        exchange_start(3 + k)

        @pl.when(k + 1 < SUBITERS)
        def _():
            early(k + 1, RHS)
            build_shell()

        @pl.when(k + 1 == SUBITERS)
        def _():
            lax.fori_loop(0, CX // 2, give, 0)
            store.start()

        exchange_wait(3 + k)
        added = pick(GT[...], AR[3 + k].reshape(8 * ndev, LANES))
        for f in range(6):
            force = LOAD[f]
            if f < 3:
                force = force + added[NB * f : NB * (f + 1)]
            FORCE[f, pl.ds(0, NB), :] = force
            HS[k, 0, pl.ds(f, 1), :] = force[0:1]
            HS[k, 1, pl.ds(f, 1), :] = force[NB - 1 : NB]
            HS[k, 0, pl.ds(8 + f, 1), :] = SH[f, pl.ds(0, 1), :]
            HS[k, 1, pl.ds(8 + f, 1), :] = SH[f, pl.ds(NB - 1, 1), :]
        both("z", lambda side: end_copy(k, side).start())
        both("z", lambda side: end_copy(k, side).wait_send())
        both("z", lambda side: end_copy(k, 1 - side).wait_recv())
        for f in range(6):
            FORCE[f, pl.ds(NB, 8), :] = ends(HR[k, 1, pl.ds(f, 1), :], HR[k, 0, pl.ds(f, 1), :])
            SH[f, pl.ds(NB, 8), :] = ends(HR[k, 1, pl.ds(8 + f, 1), :], HR[k, 0, pl.ds(8 + f, 1), :])
        lax.fori_loop(0, SHELL_SWEEPS, shell_sweep, 0)

        @pl.when(k + 1 < SUBITERS)
        def _():
            send_wall(k + 1)
        return carry

    take_wall(0, False)
    early(0, RW)
    take_edges()
    lax.fori_loop(0, SUBITERS, subiteration, 0)

    for n in range(NB):
        sout_ref[:, pl.ds(LANES * n, LANES)] = SH[:, n, :]
    store.wait()


def body(velocity, source, viscosity, owners, targets, shell_load, shell_state, shell_inverse):
    nsec = lax.axis_size("sec")
    ndev = lax.axis_size("dev")
    vmem = pl.BlockSpec(memory_space=pltpu.VMEM)
    hbm = pl.BlockSpec(memory_space=pltpu.HBM)
    bf16 = jnp.bfloat16
    dma = pltpu.SemaphoreType.DMA
    out = pl.pallas_call(
        lambda *refs: kernel(nsec, ndev, *refs),
        out_shape=(
            jax.ShapeDtypeStruct((3, CX, NY, LANES), F32),
            jax.ShapeDtypeStruct((6, NB * LANES), F32),
        ),
        in_specs=[hbm, hbm, hbm, vmem, vmem, hbm, hbm, hbm],
        out_specs=(hbm, vmem),
        scratch_shapes=[
            pltpu.VMEM((3, CX, NY, LANES), F32),
            pltpu.VMEM((3, CX, NY, LANES), F32),
            pltpu.VMEM((1, CX, NY, LANES), F32),
            pltpu.VMEM((6, NB * LANES), F32),
            pltpu.VMEM((6, NB * LANES), F32),
            pltpu.VMEM((6, 6, NB * LANES), F32),
            pltpu.VMEM((3, CX, NY, LANES), F32),
            pltpu.VMEM((3, CX + 2, NY, LANES), F32),
            pltpu.VMEM((1, CX, NY, LANES), F32),
            pltpu.VMEM((6, CX + 2, NY, LANES), F32),
            pltpu.VMEM((CX + 2, NY, LANES), F32),
            pltpu.VMEM((3, CX, NY, LANES), F32),
            pltpu.VMEM((3, CX + 2, NY, LANES), F32),
            pltpu.VMEM((3, CX + 2, NY, LANES), F32),
            pltpu.VMEM((2, 3, 2, 2, NY, LANES), F32),
            pltpu.VMEM((2, 3, 2 * CX, LANES), F32),
            pltpu.VMEM((2, 3, 2, 2 * CX, LANES), F32),
            pltpu.VMEM((2, 3, 2, 8, LANES), F32),
            pltpu.VMEM((2, 3, 2, 2, 8, LANES), F32),
            pltpu.VMEM((2, 2, NY, LANES), F32),
            pltpu.VMEM((CX, LANES), F32),
            pltpu.VMEM((2, CX, LANES), F32),
            pltpu.VMEM((2, 8, LANES), F32),
            pltpu.VMEM((2, 2, 8, LANES), F32),
            pltpu.VMEM((2, 3, NY, LANES), F32),
            pltpu.VMEM((10, CX, LANES), F32),
            pltpu.VMEM((2, 10, CX, LANES), F32),
            pltpu.VMEM((10, CX, LANES), F32),
            pltpu.VMEM((3, CX, LANES), F32),
            pltpu.VMEM((8 * ndev, LANES), bf16),
            pltpu.VMEM((LANES, 8 * ndev), bf16),
            pltpu.VMEM((8 * ndev, LANES), bf16),
            pltpu.VMEM((LANES, 8 * ndev), bf16),
            pltpu.VMEM((5, ndev, 8, LANES), F32),
            pltpu.VMEM((5, ndev, 8, LANES), F32),
            pltpu.VMEM((LANES, LANES), F32),
            pltpu.VMEM((2, ROWS, LANES), F32),
            pltpu.VMEM((2, NY, LANES), F32),
            pltpu.VMEM((2, 2, NY, LANES), F32),
            pltpu.VMEM((2, 2, ROWS, LANES), F32),
            pltpu.VMEM((LANES, LANES), F32),
            pltpu.VMEM((LANES, LANES), F32),
            pltpu.VMEM((6, 24, LANES), F32),
            pltpu.VMEM((6, NB, LANES), F32),
            pltpu.VMEM((6, 24, LANES), F32),
            pltpu.VMEM((36, 24, LANES), F32),
            pltpu.VMEM((2, 40, LANES), F32),
            pltpu.VMEM((2, 40, LANES), F32),
            pltpu.VMEM((2, 2, 16, LANES), F32),
            pltpu.VMEM((2, 2, 16, LANES), F32),
            dma((2, 3, 2)), dma((2, 3, 2)), dma((2, 3, 2)), dma((2, 3, 2)),
            dma((2, 3, 2, 2)), dma((2, 3, 2, 2)),
            dma((2,)), dma((2,)), dma((2,)), dma((2,)), dma((2, 2)), dma((2, 2)),
            dma((2,)), dma((2,)), dma((2,)), dma((2,)),
            dma((2, 2)), dma((2, 2)), dma((2, 2)), dma((2, 2)),
            dma((5,)), dma((5,)),
            dma((2,)), dma((2,)), dma((2, 2)), dma((2, 2)), dma((6,)),
        ],
        compiler_params=pltpu.CompilerParams(
            collective_id=0, has_side_effects=True, vmem_limit_bytes=60 * 1024 * 1024),
    )(
        velocity, source, viscosity[None], owners.reshape(1, CX), targets,
        shell_load, shell_state, shell_inverse,
    )
    return tuple(out)


def solution(mesh):
    in_specs = (
        P(None, "sec", None, "dev"),
        P(None, "sec", None, "dev"),
        P("sec", None, "dev"),
        P("dev", "sec", None),
        P("dev", "sec"),
        P(None, ("sec", "dev")),
        P(None, ("sec", "dev")),
        P(None, None, ("sec", "dev")),
    )
    out_specs = (P(None, "sec", None, "dev"), P(None, ("sec", "dev")))
    return jax.shard_map(body, mesh=mesh, in_specs=in_specs, out_specs=out_specs, check_vma=False)
```
